32 devices in a mesh: groups: 2 (over y), vox: 4 (over z), chan: 2 (over x), frm: 2 (over core).
Axes of the slice: x: 2, y: 2, z: 4, core: 2. Of those that a mesh axis runs over, the one named last changes fastest.
Arguments:
- echo_data: bfloat16 [8, 2, 1024, 2, 512], P(('groups', 'vox'), 'chan', None, None, 'frm'), parts along dimension 0, may hold values from -36 to 36
- tile_weights: bfloat16 [4, 2, 64, 128, 128], P('vox', 'chan'), may hold values from -0.0625 to 0.0625
- tile_target: int32 [4, 2, 64], P('vox', 'chan'), may hold values from 0 to 1
- tile_offset: int32 [4, 2, 64], P('vox', 'chan'), may hold values from 0 to 896
- tile_count: int32 [4, 2], P('vox', 'chan'), may hold values from 8 to 64, as said below
- grid_map: int32 [4, 256], P('vox'), may hold values from 0 to 255, each once within a row
- psf_kernel: float32 [5, 5], replicated, may hold values from -1.25 to 1.25
Outputs:
- psf_image: float32 [64, 32, 512], P(('groups', 'vox'), 'chan', 'frm'), parts along dimension 0
The draws below stay inside these ranges and needn't reach their ends.
There are 2 independent parts, one for each index of `groups`. The reference program is written for one: setup_inputs(seed, part) draws one part's arguments, and reference() takes and returns one part's arrays. A program takes and returns all parts, laid end to end along the dimension named above; an argument that names none is the same for every part. Nothing has to cross between parts.
Inputs may be any that keep to these rules, and one draw needn't show every extreme that they name: `tile_count`: in each voxel block exactly one channel group uses all 64 slots; the others use far fewer. `grid_map`: each block's row is a permutation of 0 to 255.
All inputs are finite; a program needn't handle non-finite values.
Results may differ from the reference program's by a relative error of at most 0.014.
Values may be sent and summed in bfloat16 or wider, within the bound.
A program may use at most 64 MiB of HBM per device.

```python
import math
import jax
import jax.numpy as jnp
from jax import lax

FRAMES = 512
TILE = 128
VOX_DEV = 256
ROWS = 1024
TCAP = 64
BLOCKS = 4
CGROUPS = 2
NA = 32
NB = 32


def draw_echo_data(key, part):
    key_rows, key_frames, key_values = jax.random.split(jax.random.fold_in(key, 5), 3)
    shape_all = (BLOCKS, CGROUPS, ROWS, 2, FRAMES)
    row_scale = jnp.exp(jax.random.uniform(key_rows, (BLOCKS, CGROUPS, ROWS, 1, 1), jnp.float32, math.log(0.3), math.log(3.0)))
    frame_scale = jnp.exp(jax.random.uniform(key_frames, (FRAMES,), jnp.float32, 0.0, math.log(3.0)))
    values = jax.random.truncated_normal(key_values, -4.0, 4.0, shape_all, jnp.float32)
    return (values * row_scale * frame_scale).astype(jnp.bfloat16)


def draw_tile_count(key, part):
    key_busy, key_base = jax.random.split(jax.random.fold_in(key, 11))
    busiest = jax.random.randint(key_busy, (BLOCKS, 1), 0, CGROUPS)
    base_counts = jax.random.randint(key_base, (BLOCKS, CGROUPS), TCAP // 8, TCAP // 3 + 1)
    group_ids = jnp.arange(CGROUPS, dtype=jnp.int32)[None, :]
    return jnp.where(group_ids == busiest, TCAP, base_counts).astype(jnp.int32)


def plant(entries, key, least, high):
    extent = entries.shape
    spot = [jax.random.randint(jax.random.fold_in(key, axis), (), 0, extent[axis]) for axis in range(len(extent))]
    entries = entries.at[tuple(spot)].set(least)
    longest = extent.index(max(extent))
    spot[longest] = (spot[longest] + 1) % extent[longest]
    return entries.at[tuple(spot)].set(high)


def block_scale(stream_key, extent, cuts, least, largest):
    level, own = 1.0, jax.random.fold_in(stream_key, 6)
    for dim, parts in cuts:
        steps = jnp.exp(jax.random.uniform(jax.random.fold_in(own, dim), (parts,), jnp.float32, least / len(cuts), largest / len(cuts)))
        level = level * jnp.repeat(steps, extent[dim] // parts).reshape([-1 if axis == dim else 1 for axis in range(len(extent))])
    return level


def scatter_about(rng, dims, deviation, most, cuts=(), kind=jnp.bfloat16):
    result = deviation * jax.random.normal(rng, dims, jnp.float32)
    if cuts:
        result = result * block_scale(rng, dims, cuts, -0.22, 0.18)
    return jnp.clip(result, -most, most).astype(kind)


def setup_inputs(seed: int = 0, part: int = 0) -> dict:
    key_of = jax.random.split(jax.random.key(seed), 8)
    part_keys = jax.random.split(jax.random.fold_in(key_of[7], part), 8)
    return {
        "echo_data": draw_echo_data(jax.random.fold_in(jax.random.fold_in(key_of[7], part), 71), part),
        "tile_weights": scatter_about(key_of[1], (BLOCKS, CGROUPS, TCAP, TILE, TILE), (TILE * TCAP) ** -0.5, 0.0625, ((0, 4), (1, 2))),
        "tile_target": plant(jax.random.randint(key_of[2], (BLOCKS, CGROUPS, TCAP), 0, VOX_DEV // TILE), jax.random.fold_in(key_of[2], 1), 0, (VOX_DEV // TILE) - 1).astype(jnp.int32),
        "tile_offset": plant(jax.random.randint(key_of[3], (BLOCKS, CGROUPS, TCAP), 0, ROWS - TILE + 1), jax.random.fold_in(key_of[3], 1), 0, ROWS - TILE).astype(jnp.int32),
        "tile_count": draw_tile_count(jax.random.fold_in(key_of[7], 71), part),
        "grid_map": jax.vmap(lambda own: jax.random.permutation(own, VOX_DEV))(jax.random.split(key_of[5], BLOCKS)).reshape((BLOCKS, VOX_DEV)).astype(jnp.int32),
        "psf_kernel": scatter_about(key_of[6], (5, 5), 25 ** -0.5, 1.25, (), jnp.float32),
    }


POLY_COEFFS = (1.0, -0.6, 0.15, -0.03)

def complex_times(left_real, left_imag, right_real, right_imag):
    level = lax.Precision.HIGH
    real_part = jnp.dot(left_real, right_real, precision=level, preferred_element_type=jnp.float32) - jnp.dot(left_imag, right_imag, precision=level, preferred_element_type=jnp.float32)
    imag_part = jnp.dot(left_real, right_imag, precision=level, preferred_element_type=jnp.float32) + jnp.dot(left_imag, right_real, precision=level, preferred_element_type=jnp.float32)
    return (real_part, imag_part)

def beam_block(block_items):
    echo_block, weight_block, target_block, offset_block, count_block = block_items
    group_total = echo_block.shape[0]
    flat_echo = echo_block.reshape(group_total, ROWS, 2 * FRAMES)
    slot_total = group_total * TCAP
    slot_ids = jnp.arange(slot_total, dtype=jnp.int32)
    group_ids = slot_ids // TCAP
    keep_slots = slot_ids % TCAP < count_block[group_ids]
    zero_index = jnp.zeros((), jnp.int32)

    def add_tile(totals, item):
        weight_tile, group_id, target_id, offset_id, keep_tile = item
        samples = lax.dynamic_slice(flat_echo, (group_id, offset_id, zero_index), (1, TILE, 2 * FRAMES))[0]
        product = jnp.dot(weight_tile, samples, preferred_element_type=jnp.float32)
        product = jnp.where(keep_tile, product, jnp.zeros_like(product))
        return (totals.at[target_id].add(product), None)
    start_totals = jnp.zeros((VOX_DEV // TILE, TILE, 2 * FRAMES), jnp.float32)
    items = (weight_block.reshape(slot_total, TILE, TILE), group_ids, target_block.reshape(slot_total), offset_block.reshape(slot_total), keep_slots)
    totals, unused = lax.scan(add_tile, start_totals, items)
    return totals.reshape(VOX_DEV, 2, FRAMES)

def reference(echo_data, tile_weights, tile_target, tile_offset, tile_count, grid_map, psf_kernel):
    beams = lax.map(beam_block, (echo_data, tile_weights, tile_target, tile_offset, tile_count))
    arranged = jax.vmap(lambda beam_rows, order_ids: beam_rows[order_ids])(beams, grid_map)
    beamformed = arranged.reshape(NA, NB, 2, FRAMES).astype(jnp.bfloat16)
    stacked = beamformed.reshape(NA * NB, 2 * FRAMES)
    gram_block = lax.dot_general(stacked, stacked, (((0,), (0,)), ((), ())), preferred_element_type=jnp.float32)
    gram_real = gram_block[:FRAMES, :FRAMES] + gram_block[FRAMES:, FRAMES:]
    gram_imag = gram_block[:FRAMES, FRAMES:] - gram_block[FRAMES:, :FRAMES]
    factor = FRAMES / jnp.trace(gram_real)
    norm_real = factor * gram_real
    norm_imag = factor * gram_imag
    echo_real = beamformed[:, :, 0, :].reshape(NA * NB, FRAMES).astype(jnp.float32)
    echo_imag = beamformed[:, :, 1, :].reshape(NA * NB, FRAMES).astype(jnp.float32)
    term_real = POLY_COEFFS[3] * echo_real
    term_imag = POLY_COEFFS[3] * echo_imag
    for degree in (2, 1, 0):
        term_real, term_imag = complex_times(term_real, term_imag, norm_real, norm_imag)
        term_real = term_real + POLY_COEFFS[degree] * echo_real
        term_imag = term_imag + POLY_COEFFS[degree] * echo_imag
    envelope = jnp.sqrt(term_real * term_real + term_imag * term_imag + 1e-06)
    envelope = envelope.reshape(NA, NB, FRAMES)
    padded = jnp.pad(envelope, ((2, 2), (2, 2), (0, 0)))
    psf_image = jnp.zeros_like(envelope)
    for shift_a in range(5):
        for shift_b in range(5):
            psf_image = psf_image + psf_kernel[shift_a, shift_b] * padded[shift_a:shift_a + NA, shift_b:shift_b + NB]
    return psf_image
```

```python
import functools

import jax
import jax.numpy as jnp
from jax import lax
from jax.experimental import pallas as pl
from jax.experimental.pallas import tpu as pltpu
from jax.sharding import PartitionSpec as P

MESH = pl.DeviceIdType.MESH
PIECES = 4
GROUP = 8

TBATCH = 8
LAT_DEV = 8


POLY_COEFFS = (1.0, -0.6, 0.15, -0.03)


def with_halo(shard, sides, width):
    for axis, dim in sides:
        devices, length = (lax.axis_size(axis), shard.shape[dim])
        up = [(i, (i + 1) % devices) for i in range(devices - 1)]
        down = [(j, i) for i, j in up]
        last = lax.slice_in_dim(shard, length - width, length, axis=dim)
        leading = lax.slice_in_dim(shard, 0, width, axis=dim)
        before = lax.ppermute(last, axis, up)
        after = lax.ppermute(leading, axis, down)
        shard = jnp.concatenate([before, shard, after], axis=dim)
    return shard


def complex_times(left_real, left_imag, right_real, right_imag):
    level = lax.Precision.HIGH
    real_part = jnp.dot(
        left_real, right_real, precision=level, preferred_element_type=jnp.float32
    ) - jnp.dot(left_imag, right_imag, precision=level, preferred_element_type=jnp.float32)
    imag_part = jnp.dot(
        left_real, right_imag, precision=level, preferred_element_type=jnp.float32
    ) + jnp.dot(left_imag, right_real, precision=level, preferred_element_type=jnp.float32)
    return (real_part, imag_part)


def tile_pass(flat_echo, weights, tile_goal, tile_start, live_total, tiles_out):
    tile_size = weights.shape[-1]
    col_count = flat_echo.shape[-1]
    slot_count = weights.shape[0]
    lane_ids = jnp.arange(TBATCH, dtype=jnp.int32)
    target_ids = jnp.arange(tiles_out, dtype=jnp.int32)
    zero_index = jnp.zeros((), jnp.int32)

    def cut_rows(offset_id):
        return lax.dynamic_slice(flat_echo, (offset_id, zero_index), (tile_size, col_count))

    def one_turn(turn_index, totals):
        where_at = turn_index * TBATCH + lane_ids
        live_lane = where_at < live_total
        chosen = jnp.minimum(where_at, slot_count - 1)
        picked = weights[chosen]
        samples = jax.vmap(cut_rows)(tile_start[chosen])
        product = jnp.einsum("krs,ksc->krc", picked, samples, preferred_element_type=jnp.float32)
        placing = ((tile_goal[chosen][:, None] == target_ids[None, :]) & live_lane[:, None]).astype(
            jnp.float32
        )
        return totals + jnp.einsum(
            "kt,krc->trc", placing, product, precision=lax.Precision.HIGHEST
        )

    start_totals = jnp.zeros((tiles_out, tile_size, col_count), jnp.float32)
    turn_count = (live_total + TBATCH - 1) // TBATCH
    return lax.fori_loop(0, turn_count, one_turn, start_totals)


def shards(echo_data, tile_weights, tile_target, tile_offset, tile_count, grid_map, psf_kernel):
    row_count = echo_data.shape[2]
    half_frames = echo_data.shape[4]
    tile_size = tile_weights.shape[-1]
    slot_count = tile_weights.shape[2]
    voxels = grid_map.shape[1]
    tiles_out = voxels // tile_size
    flat_echo = echo_data.reshape(row_count, 2 * half_frames)
    weights = tile_weights.reshape(slot_count, tile_size, tile_size)
    tile_sums = tile_pass(
        flat_echo,
        weights,
        tile_target.reshape(-1),
        tile_offset.reshape(-1),
        tile_count[0, 0],
        tiles_out,
    )
    arranged = jnp.take(tile_sums.reshape(voxels, 2, half_frames), grid_map[0], axis=0)
    arranged = arranged.reshape(LAT_DEV, voxels // LAT_DEV, 2, half_frames)
    beamformed = lax.psum_scatter(arranged, "chan", scatter_dimension=1, tiled=True).astype(
        jnp.bfloat16
    )
    lat_count = beamformed.shape[0]
    depth_count = beamformed.shape[1]
    cell_count = lat_count * depth_count
    own_frames = beamformed.reshape(cell_count, 2, half_frames)
    all_frames = lax.all_gather(own_frames, "frm", axis=2, tiled=True)
    frames = all_frames.shape[2]
    own_flat = own_frames.reshape(cell_count, 2 * half_frames)
    all_flat = all_frames.reshape(cell_count, 2 * frames)
    gram_block = lax.dot_general(
        own_flat, all_flat, (((0,), (0,)), ((), ())), preferred_element_type=jnp.float32
    )
    gram_real = gram_block[:half_frames, :frames] + gram_block[half_frames:, frames:]
    gram_imag = gram_block[:half_frames, frames:] - gram_block[half_frames:, :frames]
    frame_start = lax.axis_index("frm") * half_frames
    echo_real = all_frames[:, 0, :].astype(jnp.float32)
    echo_imag = all_frames[:, 1, :].astype(jnp.float32)
    energy = jnp.sum(echo_real * echo_real + echo_imag * echo_imag)
    gram_real, gram_imag, trace_value = lax.psum((gram_real, gram_imag, energy), ("vox", "chan"))
    factor = frames / trace_value
    norm_real = factor * gram_real
    norm_imag = factor * gram_imag
    full_real, full_imag = (
        lax.all_gather(norm_real, "frm", axis=0, tiled=True),
        lax.all_gather(norm_imag, "frm", axis=0, tiled=True),
    )
    identity = jnp.eye(frames, dtype=jnp.float32)
    poly_real = POLY_COEFFS[3] * full_real + POLY_COEFFS[2] * identity
    poly_imag = POLY_COEFFS[3] * full_imag
    poly_real, poly_imag = complex_times(poly_real, poly_imag, full_real, full_imag)
    poly_real = poly_real + POLY_COEFFS[1] * identity
    cols_real = lax.dynamic_slice_in_dim(full_real, frame_start, half_frames, 1)
    cols_imag = lax.dynamic_slice_in_dim(full_imag, frame_start, half_frames, 1)
    filter_real, filter_imag = complex_times(poly_real, poly_imag, cols_real, cols_imag)
    filter_real = filter_real + POLY_COEFFS[0] * lax.dynamic_slice_in_dim(
        identity, frame_start, half_frames, 1
    )
    out_real, out_imag = complex_times(echo_real, echo_imag, filter_real, filter_imag)
    envelope = jnp.sqrt(out_real * out_real + out_imag * out_imag + 1e-06)
    envelope = envelope.reshape(lat_count, depth_count, half_frames)
    padded = with_halo(envelope, (("vox", 0), ("chan", 1)), 2)
    psf_image = jnp.zeros_like(envelope)
    for shift_a in range(5):
        for shift_b in range(5):
            psf_image = (
                psf_image
                + psf_kernel[shift_a, shift_b]
                * padded[shift_a : shift_a + lat_count, shift_b : shift_b + depth_count]
            )
    return psf_image


def split(value):
    high = value.astype(jnp.bfloat16)
    return high, (value - high.astype(jnp.float32)).astype(jnp.bfloat16)


def beam_kernel(goal_ref, start_ref, live_ref, weights_ref, echo_ref, map_ref, out_ref, small_ref, operator, high_ref, low_ref):
    blocks, voxels, tile = operator.shape
    operator[...] = jnp.zeros_like(operator)
    lane = lax.broadcasted_iota(jnp.int32, (tile, tile), 1)

    slots = weights_ref.shape[0]
    live = live_ref[0]

    def place(turn, carry):
        ready = []
        for index in range(GROUP):
            slot = turn * GROUP + index
            kept = jnp.minimum(slot, slots - 1)
            first = start_ref[kept]
            block = first // tile
            shift = first - block * tile
            rows = pl.ds(pl.multiple_of(goal_ref[kept] * tile, tile), tile)
            turned = pltpu.roll(weights_ref[kept].astype(jnp.float32), shift, 1)
            limit = jnp.where(slot < live, shift, tile)
            least = jnp.where(slot < live, 0, tile)
            ready.append((block, rows, jnp.where(lane >= limit, turned, 0.0), turned, shift, least))
        for block, rows, high, turned, shift, least in ready:
            operator[block, rows, :] += high
            operator[block + 1, rows, :] += jnp.where((lane < shift) & (lane >= least), turned, 0.0)
        return carry

    lax.fori_loop(0, (live + GROUP - 1) // GROUP, place, 0)
    picks = lax.broadcasted_iota(jnp.int32, (voxels, voxels), 0) == map_ref[...]
    picks = picks.astype(jnp.float32).T.astype(jnp.bfloat16)
    for block in range(blocks - 1):
        high, low = split(operator[block])
        columns = slice(block * tile, (block + 1) * tile)
        for part, target in ((high, high_ref), (low, low_ref)):
            moved = jnp.dot(picks, part, preferred_element_type=jnp.float32)
            target[:, columns] = moved.astype(jnp.bfloat16)
    sums = jnp.dot(high_ref[...], echo_ref[...], preferred_element_type=jnp.float32)
    sums += jnp.dot(low_ref[...], echo_ref[...], preferred_element_type=jnp.float32)
    halves, cells, _ = out_ref.shape
    width = cells // LAT_DEV
    for lat in range(LAT_DEV):
        for half in range(halves):
            source = (lat * halves + half) * width
            chosen = sums[source : source + width]
            out_ref[half, lat * width : (lat + 1) * width, :] = chosen
            small_ref[half, lat * width : (lat + 1) * width, :] = chosen.astype(small_ref.dtype)


def gather_kernel(
    count, part_ref, small_ref, out_ref, arrived, swap_send, swap_recv, own_recv, mate_recv, up_send, down_send, mate_send
):
    vox, chan, frm = lax.axis_index("vox"), lax.axis_index("chan"), lax.axis_index("frm")
    beside, mate = {"chan": 1 - chan}, {"frm": 1 - frm}
    above, below = {"vox": vox + 1}, {"vox": vox - 1}
    can_up, can_down = vox + 1 < count, vox > 0
    pieces = swap_send.shape[0]
    height = part_ref.shape[1] // pieces
    barrier = pltpu.get_barrier_semaphore()

    def greet(target):
        pl.semaphore_signal(barrier, inc=1, device_id=target, device_id_type=MESH)

    greet(beside)
    greet(mate)
    pl.when(can_up)(lambda: greet(above))
    pl.when(can_down)(lambda: greet(below))
    pl.semaphore_wait(barrier, 4 - jnp.where(can_up, 0, 1) - jnp.where(can_down, 0, 1))

    def remote(source, target, sent, received, device):
        return pltpu.make_async_remote_copy(
            src_ref=source, dst_ref=target, send_sem=sent, recv_sem=received, device_id=device, device_id_type=MESH
        )

    def rows(piece):
        return pl.ds(piece * height, height)

    def item(block, piece, sent, device):
        place = out_ref.at[block, frm, :, rows(piece)]
        return remote(place, place, sent, own_recv.at[block, piece], device)

    def to_mate(block, piece, owner=None):
        place = out_ref.at[block, frm if owner is None else owner, :, rows(piece)]
        return remote(place, place, mate_send.at[block, piece], mate_recv.at[block, piece], mate)

    def go_up(block, piece):
        return item(block, piece, up_send.at[block, piece], above)

    def go_down(block, piece):
        return item(block, piece, down_send.at[block, piece], below)

    def swap(piece):
        return remote(
            small_ref.at[:, rows(piece)], arrived.at[:, rows(piece)], swap_send.at[piece], swap_recv.at[piece], beside
        )

    def relay(step, piece):
        @pl.when(vox >= step)
        def _():
            item(vox - step, piece, up_send.at[0, piece], above).wait_recv()
            pl.when(can_up)(lambda: go_up(vox - step, piece).start())
            to_mate(vox - step, piece).start()

        @pl.when(vox + step < count)
        def _():
            item(vox + step, piece, down_send.at[0, piece], below).wait_recv()
            pl.when(can_down)(lambda: go_down(vox + step, piece).start())
            to_mate(vox + step, piece).start()

    for piece in range(pieces):
        swap(piece).start()
    for wave in range(pieces + count - 1):
        if wave < pieces:
            swap(wave).wait_recv()
            mine = part_ref[:, rows(wave)] + arrived[:, rows(wave)].astype(jnp.float32)
            out_ref[vox, frm, :, rows(wave)] = mine.astype(out_ref.dtype)
            pl.when(can_up)(lambda: go_up(vox, wave).start())
            pl.when(can_down)(lambda: go_down(vox, wave).start())
            to_mate(vox, wave).start()
        for step in range(1, count):
            piece = wave - step
            if 0 <= piece < pieces:
                relay(step, piece)

    for piece in range(pieces):
        swap(piece).wait_send()
        for block in range(count):
            to_mate(block, piece).wait_send()
            to_mate(block, piece, 1 - frm).wait_recv()
            pl.when(can_up & (vox >= block))(lambda: go_up(block, piece).wait_send())
            pl.when(can_down & (vox <= block))(lambda: go_down(block, piece).wait_send())


def filter_kernel(count, beams_ref, psf_ref, out_ref, high_ref, low_ref, padded):
    vox, chan, frm = lax.axis_index("vox"), lax.axis_index("chan"), lax.axis_index("frm")
    lat, depth, half = out_ref.shape
    cells = lat * depth
    pair = 2 * half
    total = count * 2 * cells
    left = beams_ref[:, 0].reshape(total, pair)
    right = beams_ref[:, 1].reshape(total, pair)

    def gram(first, second):
        block = lax.dot_general(first, second, (((0,), (0,)), ((), ())), preferred_element_type=jnp.float32)
        real = block[:half, :half] + block[half:, half:]
        imag = block[:half, half:] - block[half:, :half]
        return real, imag

    grams = {(0, 0): gram(left, left), (0, 1): gram(left, right), (1, 1): gram(right, right)}
    grams[1, 0] = (grams[0, 1][0].T, -grams[0, 1][1].T)
    eye = lax.broadcasted_iota(jnp.int32, (half, half), 0) == lax.broadcasted_iota(jnp.int32, (half, half), 1)
    diagonal = jnp.where(eye, grams[0, 0][0] + grams[1, 1][0], 0.0)
    trace = jnp.sum(jnp.sum(diagonal, axis=0, keepdims=True), axis=1, keepdims=True)
    factor = (2 * half) / trace
    for (row, column), (real, imag) in grams.items():
        real_parts, imag_parts = split(factor * real), split(factor * imag)
        for target, real_part, imag_part in zip((high_ref, low_ref), real_parts, imag_parts):
            top, side = row * pair, column * pair
            target[top : top + half, side : side + half] = real_part
            target[top : top + half, side + half : side + pair] = imag_part
            target[top + half : top + pair, side : side + half] = -imag_part
            target[top + half : top + pair, side + half : side + pair] = real_part

    before, after = jnp.maximum(vox - 1, 0), jnp.minimum(vox + 1, count - 1)
    edge = 2 * depth

    def both(block, side, rows):
        return jnp.concatenate([beams_ref[block, 0, side, rows], beams_ref[block, 1, side, rows]], axis=1)

    other = 1 - chan
    near = jnp.concatenate(
        [
            both(before, other, slice(cells - edge, cells)),
            both(vox, other, slice(0, cells)),
            both(after, other, slice(0, edge)),
        ],
        axis=0,
    )
    tall = lat + 4
    slots = -(-2 * tall // 16) * 16
    picked = lax.broadcasted_iota(jnp.int32, (slots, tall * depth), 0)
    source = lax.broadcasted_iota(jnp.int32, (slots, tall * depth), 1)
    wanted = (picked // 2) * depth + picked % 2 + jnp.where(chan == 0, 0, depth - 2)
    picks = ((source == wanted) & (picked < 2 * tall)).astype(jnp.float32).astype(jnp.bfloat16)
    near = jnp.dot(picks, near, preferred_element_type=jnp.float32).astype(jnp.bfloat16)
    beams = jnp.concatenate(
        [
            both(before, chan, slice(cells - edge, cells)),
            both(vox, chan, slice(0, cells)),
            both(after, chan, slice(0, edge)),
            near,
        ],
        axis=0,
    )

    def times(left, right_ref, columns):
        return jnp.dot(left, right_ref[:, columns], preferred_element_type=jnp.float32)

    echo = beams.astype(jnp.float32)
    whole = slice(0, 2 * pair)
    term = POLY_COEFFS[3] * times(beams, high_ref, whole) + POLY_COEFFS[2] * echo
    term = times(term.astype(jnp.bfloat16), high_ref, whole) + POLY_COEFFS[1] * echo
    own = pl.ds(pl.multiple_of(frm * pair, pair), pair)
    echo = jnp.where(frm == 0, echo[:, :pair], echo[:, pair:])
    high, low = split(term)
    term = times(high, high_ref, own) + times(high, low_ref, own) + times(low, high_ref, own) + POLY_COEFFS[0] * echo
    envelope = jnp.sqrt(term[:, :half] * term[:, :half] + term[:, half:] * term[:, half:] + 1e-06)

    padded[...] = jnp.zeros_like(padded)
    has_before, has_after = jnp.where(vox > 0, 1.0, 0.0), jnp.where(vox + 1 < count, 1.0, 0.0)
    right_side, left_side = jnp.where(chan == 0, 1.0, 0.0), jnp.where(chan == 0, 0.0, 1.0)
    for line in range(tall):
        scale = has_before if line < 2 else has_after if line >= lat + 2 else None
        middle = envelope[line * depth : (line + 1) * depth]
        start = tall * depth + 2 * line
        rim = envelope[start : start + 2]
        if scale is not None:
            middle, rim = middle * scale, rim * scale
        padded[line, 8 : 8 + depth, :] = middle
        padded[line, 6:8, :] = rim * left_side
        padded[line, 8 + depth : 10 + depth, :] = rim * right_side
    result = jnp.zeros((lat, depth, half), jnp.float32)
    for shift_b in range(5):
        for shift_a in range(5):
            result += psf_ref[shift_a, shift_b] * padded[shift_a : shift_a + lat, 6 + shift_b : 6 + shift_b + depth]
    out_ref[...] = result


def kernel_shards(count, echo_data, tile_weights, tile_target, tile_offset, tile_count, grid_map, psf_kernel):
    rows, half = echo_data.shape[2], echo_data.shape[4]
    slots, tile = tile_weights.shape[2], tile_weights.shape[4]
    voxels = grid_map.shape[1]
    cells, pair = voxels // 2, 2 * half
    depth = cells // LAT_DEV
    vmem, smem = pl.BlockSpec(memory_space=pltpu.VMEM), pl.BlockSpec(memory_space=pltpu.SMEM)
    parts, small = pl.pallas_call(
        beam_kernel,
        name="beam",
        out_shape=[
            jax.ShapeDtypeStruct((2, cells, pair), jnp.float32),
            jax.ShapeDtypeStruct((2, cells, pair), jnp.bfloat16),
        ],
        in_specs=[smem, smem, smem, vmem, vmem, vmem],
        out_specs=[vmem, vmem],
        scratch_shapes=[
            pltpu.VMEM((rows // tile + 1, voxels, tile), jnp.float32),
            pltpu.VMEM((voxels, rows), jnp.bfloat16),
            pltpu.VMEM((voxels, rows), jnp.bfloat16),
        ],
        compiler_params=pltpu.CompilerParams(vmem_limit_bytes=16 << 20),
    )(
        tile_target.reshape(-1),
        tile_offset.reshape(-1),
        tile_count.reshape(-1),
        tile_weights.reshape(slots, tile, tile),
        echo_data.reshape(rows, pair),
        grid_map,
    )
    pieces = PIECES
    each = (count, pieces)
    dma = pltpu.SemaphoreType.DMA
    beams = pl.pallas_call(
        functools.partial(gather_kernel, count),
        name="gather",
        out_shape=jax.ShapeDtypeStruct((count, 2, 2, cells, pair), jnp.bfloat16),
        in_specs=[vmem, vmem],
        out_specs=vmem,
        scratch_shapes=[pltpu.VMEM((2, cells, pair), jnp.bfloat16)] + [dma((pieces,))] * 2 + [dma(each)] * 5,
        compiler_params=pltpu.CompilerParams(collective_id=0, has_side_effects=True, vmem_limit_bytes=8 << 20),
    )(parts, small)
    return pl.pallas_call(
        functools.partial(filter_kernel, count),
        name="filter",
        out_shape=jax.ShapeDtypeStruct((LAT_DEV, depth, half), jnp.float32),
        in_specs=[vmem, smem],
        out_specs=vmem,
        scratch_shapes=[
            pltpu.VMEM((2 * pair, 2 * pair), jnp.bfloat16),
            pltpu.VMEM((2 * pair, 2 * pair), jnp.bfloat16),
            pltpu.VMEM((LAT_DEV + 4, depth + 16, half), jnp.float32),
        ],
        compiler_params=pltpu.CompilerParams(vmem_limit_bytes=24 << 20),
    )(beams, psf_kernel)


def solution(mesh):
    in_specs = (
        P(("groups", "vox"), "chan", None, None, "frm"),
        P("vox", "chan", None, None, None),
        P("vox", "chan", None),
        P("vox", "chan", None),
        P("vox", "chan"),
        P("vox", None),
        P(),
    )
    out_specs = P(("groups", "vox"), "chan", "frm")
    body = shards
    if mesh.shape["chan"] == 2 and mesh.shape["frm"] == 2:
        body = functools.partial(kernel_shards, mesh.shape["vox"])
    return jax.shard_map(body, mesh=mesh, in_specs=in_specs, out_specs=out_specs, check_vma=False)
```

```python
import functools

import jax
import jax.numpy as jnp
from jax import lax
from jax.experimental import pallas as pl
from jax.experimental.pallas import tpu as pltpu
from jax.sharding import PartitionSpec as P

MESH = pl.DeviceIdType.MESH
PIECES = 4
HOP = 3
GROUP = 8

TBATCH = 8
LAT_DEV = 8


POLY_COEFFS = (1.0, -0.6, 0.15, -0.03)


def with_halo(shard, sides, width):
    for axis, dim in sides:
        devices, length = (lax.axis_size(axis), shard.shape[dim])
        up = [(i, (i + 1) % devices) for i in range(devices - 1)]
        down = [(j, i) for i, j in up]
        last = lax.slice_in_dim(shard, length - width, length, axis=dim)
        leading = lax.slice_in_dim(shard, 0, width, axis=dim)
        before = lax.ppermute(last, axis, up)
        after = lax.ppermute(leading, axis, down)
        shard = jnp.concatenate([before, shard, after], axis=dim)
    return shard


def complex_times(left_real, left_imag, right_real, right_imag):
    level = lax.Precision.HIGH
    real_part = jnp.dot(
        left_real, right_real, precision=level, preferred_element_type=jnp.float32
    ) - jnp.dot(left_imag, right_imag, precision=level, preferred_element_type=jnp.float32)
    imag_part = jnp.dot(
        left_real, right_imag, precision=level, preferred_element_type=jnp.float32
    ) + jnp.dot(left_imag, right_real, precision=level, preferred_element_type=jnp.float32)
    return (real_part, imag_part)


def tile_pass(flat_echo, weights, tile_goal, tile_start, live_total, tiles_out):
    tile_size = weights.shape[-1]
    col_count = flat_echo.shape[-1]
    slot_count = weights.shape[0]
    lane_ids = jnp.arange(TBATCH, dtype=jnp.int32)
    target_ids = jnp.arange(tiles_out, dtype=jnp.int32)
    zero_index = jnp.zeros((), jnp.int32)

    def cut_rows(offset_id):
        return lax.dynamic_slice(flat_echo, (offset_id, zero_index), (tile_size, col_count))

    def one_turn(turn_index, totals):
        where_at = turn_index * TBATCH + lane_ids
        live_lane = where_at < live_total
        chosen = jnp.minimum(where_at, slot_count - 1)
        picked = weights[chosen]
        samples = jax.vmap(cut_rows)(tile_start[chosen])
        product = jnp.einsum("krs,ksc->krc", picked, samples, preferred_element_type=jnp.float32)
        placing = ((tile_goal[chosen][:, None] == target_ids[None, :]) & live_lane[:, None]).astype(
            jnp.float32
        )
        return totals + jnp.einsum(
            "kt,krc->trc", placing, product, precision=lax.Precision.HIGHEST
        )

    start_totals = jnp.zeros((tiles_out, tile_size, col_count), jnp.float32)
    turn_count = (live_total + TBATCH - 1) // TBATCH
    return lax.fori_loop(0, turn_count, one_turn, start_totals)


def shards(echo_data, tile_weights, tile_target, tile_offset, tile_count, grid_map, psf_kernel):
    row_count = echo_data.shape[2]
    half_frames = echo_data.shape[4]
    tile_size = tile_weights.shape[-1]
    slot_count = tile_weights.shape[2]
    voxels = grid_map.shape[1]
    tiles_out = voxels // tile_size
    flat_echo = echo_data.reshape(row_count, 2 * half_frames)
    weights = tile_weights.reshape(slot_count, tile_size, tile_size)
    tile_sums = tile_pass(
        flat_echo,
        weights,
        tile_target.reshape(-1),
        tile_offset.reshape(-1),
        tile_count[0, 0],
        tiles_out,
    )
    arranged = jnp.take(tile_sums.reshape(voxels, 2, half_frames), grid_map[0], axis=0)
    arranged = arranged.reshape(LAT_DEV, voxels // LAT_DEV, 2, half_frames)
    beamformed = lax.psum_scatter(arranged, "chan", scatter_dimension=1, tiled=True).astype(
        jnp.bfloat16
    )
    lat_count = beamformed.shape[0]
    depth_count = beamformed.shape[1]
    cell_count = lat_count * depth_count
    own_frames = beamformed.reshape(cell_count, 2, half_frames)
    all_frames = lax.all_gather(own_frames, "frm", axis=2, tiled=True)
    frames = all_frames.shape[2]
    own_flat = own_frames.reshape(cell_count, 2 * half_frames)
    all_flat = all_frames.reshape(cell_count, 2 * frames)
    gram_block = lax.dot_general(
        own_flat, all_flat, (((0,), (0,)), ((), ())), preferred_element_type=jnp.float32
    )
    gram_real = gram_block[:half_frames, :frames] + gram_block[half_frames:, frames:]
    gram_imag = gram_block[:half_frames, frames:] - gram_block[half_frames:, :frames]
    frame_start = lax.axis_index("frm") * half_frames
    echo_real = all_frames[:, 0, :].astype(jnp.float32)
    echo_imag = all_frames[:, 1, :].astype(jnp.float32)
    energy = jnp.sum(echo_real * echo_real + echo_imag * echo_imag)
    gram_real, gram_imag, trace_value = lax.psum((gram_real, gram_imag, energy), ("vox", "chan"))
    factor = frames / trace_value
    norm_real = factor * gram_real
    norm_imag = factor * gram_imag
    full_real, full_imag = (
        lax.all_gather(norm_real, "frm", axis=0, tiled=True),
        lax.all_gather(norm_imag, "frm", axis=0, tiled=True),
    )
    identity = jnp.eye(frames, dtype=jnp.float32)
    poly_real = POLY_COEFFS[3] * full_real + POLY_COEFFS[2] * identity
    poly_imag = POLY_COEFFS[3] * full_imag
    poly_real, poly_imag = complex_times(poly_real, poly_imag, full_real, full_imag)
    poly_real = poly_real + POLY_COEFFS[1] * identity
    cols_real = lax.dynamic_slice_in_dim(full_real, frame_start, half_frames, 1)
    cols_imag = lax.dynamic_slice_in_dim(full_imag, frame_start, half_frames, 1)
    filter_real, filter_imag = complex_times(poly_real, poly_imag, cols_real, cols_imag)
    filter_real = filter_real + POLY_COEFFS[0] * lax.dynamic_slice_in_dim(
        identity, frame_start, half_frames, 1
    )
    out_real, out_imag = complex_times(echo_real, echo_imag, filter_real, filter_imag)
    envelope = jnp.sqrt(out_real * out_real + out_imag * out_imag + 1e-06)
    envelope = envelope.reshape(lat_count, depth_count, half_frames)
    padded = with_halo(envelope, (("vox", 0), ("chan", 1)), 2)
    psf_image = jnp.zeros_like(envelope)
    for shift_a in range(5):
        for shift_b in range(5):
            psf_image = (
                psf_image
                + psf_kernel[shift_a, shift_b]
                * padded[shift_a : shift_a + lat_count, shift_b : shift_b + depth_count]
            )
    return psf_image


def split(value):
    high = value.astype(jnp.bfloat16)
    return high, (value - high.astype(jnp.float32)).astype(jnp.bfloat16)


def beam_kernel(goal_ref, start_ref, live_ref, weights_ref, map_ref, out_ref, operator):
    blocks, voxels, tile = operator.shape
    operator[...] = jnp.zeros_like(operator)
    lane = lax.broadcasted_iota(jnp.int32, (tile, tile), 1)

    slots = weights_ref.shape[0]
    live = live_ref[0, 0]

    def place(turn, carry):
        ready = []
        for index in range(GROUP):
            slot = turn * GROUP + index
            kept = jnp.minimum(slot, slots - 1)
            first = start_ref[kept]
            block = first // tile
            shift = first - block * tile
            rows = pl.ds(pl.multiple_of(goal_ref[kept] * tile, tile), tile)
            turned = pltpu.roll(weights_ref[kept].astype(jnp.float32), shift, 1)
            limit = jnp.where(slot < live, shift, tile)
            least = jnp.where(slot < live, 0, tile)
            ready.append((block, rows, jnp.where(lane >= limit, turned, 0.0), turned, shift, least))
        for block, rows, high, turned, shift, least in ready:
            operator[block, rows, :] += high
            operator[block + 1, rows, :] += jnp.where((lane < shift) & (lane >= least), turned, 0.0)
        return carry

    lax.fori_loop(0, (live + GROUP - 1) // GROUP, place, 0)
    picks = lax.broadcasted_iota(jnp.int32, (voxels, voxels), 0) == map_ref[...]
    picks = picks.astype(jnp.float32).T.astype(jnp.bfloat16)
    cells = voxels // 2
    width = cells // LAT_DEV
    for block in range(blocks - 1):
        columns = slice(block * tile, (block + 1) * tile)
        for level, value in enumerate(split(operator[block])):
            moved = jnp.dot(picks, value, preferred_element_type=jnp.float32).astype(jnp.bfloat16)
            for lat in range(LAT_DEV):
                for half in range(2):
                    source = (lat * 2 + half) * width
                    target = level * cells + lat * width
                    out_ref[half, target : target + width, columns] = moved[source : source + width]


def gather_kernel(
    count, operator_ref, echo_ref, psf_ref, rows_ref, gram_ref, near_ref, fine_ref, part, small, arrived, beams,
    swap_send, swap_recv, own_recv, mate_recv, up_send, down_send, mate_send, side_send, side_recv,
):
    vox, chan, frm = lax.axis_index("vox"), lax.axis_index("chan"), lax.axis_index("frm")
    beside, mate = {"chan": 1 - chan}, {"frm": 1 - frm}
    above, below = {"vox": vox + 1}, {"vox": vox - 1}
    can_up, can_down = vox + 1 < count, vox > 0
    at_end = (vox == 0) | (vox == count - 1)
    pieces = PIECES
    units = 2 * pieces
    cells, pair = beams.shape[3], beams.shape[4]
    half = pair // 2
    height = cells // pieces
    depth = cells // LAT_DEV
    barrier = pltpu.get_barrier_semaphore()

    def greet(target):
        pl.semaphore_signal(barrier, inc=1, device_id=target, device_id_type=MESH)

    greet(beside)
    greet(mate)
    pl.when(can_up)(lambda: greet(above))
    pl.when(can_down)(lambda: greet(below))

    def sums(side):
        value = jnp.dot(operator_ref[side], echo_ref[...], preferred_element_type=jnp.float32)
        value = value[:cells] + value[cells:]
        part[side] = value
        small[side] = value.astype(small.dtype)

    def remote(source, target, sent, received, device):
        return pltpu.make_async_remote_copy(
            src_ref=source, dst_ref=target, send_sem=sent, recv_sem=received, device_id=device, device_id_type=MESH
        )

    def rows(unit):
        return pl.ds((unit % pieces) * height, height)

    def side_of(unit):
        return chan if unit < pieces else 1 - chan

    def swap(unit, side):
        return remote(
            small.at[side, rows(unit)], arrived.at[side, rows(unit)], swap_send.at[unit], swap_recv.at[unit], beside
        )

    def item(block, unit, sent, device):
        place = beams.at[block, frm, side_of(unit), rows(unit)]
        return remote(place, place, sent, own_recv.at[block, unit], device)

    def to_mate(block, unit, owner=None):
        place = beams.at[block, frm if owner is None else owner, side_of(unit), rows(unit)]
        return remote(place, place, mate_send.at[block, unit], mate_recv.at[block, unit], mate)

    def go_up(block, unit):
        return item(block, unit, up_send.at[block, unit], above)

    def go_down(block, unit):
        return item(block, unit, down_send.at[block, unit], below)

    def cross(block, unit, side=None):
        place = beams.at[block, frm, chan if side is None else side, rows(unit)]
        return remote(place, place, side_send.at[block, unit], side_recv.at[block, unit], beside)

    def own(unit):
        swap(unit, side_of(unit)).wait_recv()
        mine = part[side_of(unit), rows(unit)] + arrived[side_of(unit), rows(unit)].astype(jnp.float32)
        beams[vox, frm, side_of(unit), rows(unit)] = mine.astype(beams.dtype)
        sends = True if unit < pieces else at_end
        pl.when(can_up & sends)(lambda: go_up(vox, unit).start())
        pl.when(can_down & sends)(lambda: go_down(vox, unit).start())
        to_mate(vox, unit).start()

    def relay(step, unit):
        from_below, from_above = vox >= step, vox + step < count
        low, high = vox - step, vox + step
        if unit >= pieces:
            from_below, from_above = from_below & (low == 0), from_above & (high == count - 1)

        @pl.when(from_below)
        def _():
            item(low, unit, up_send.at[0, unit], above).wait_recv()
            pl.when(can_up)(lambda: go_up(low, unit).start())
            if unit < pieces:
                pl.when(low > 0)(lambda: cross(low, unit).start())
            to_mate(low, unit).start()

        @pl.when(from_above)
        def _():
            item(high, unit, down_send.at[0, unit], below).wait_recv()
            pl.when(can_down)(lambda: go_down(high, unit).start())
            if unit < pieces:
                pl.when(high < count - 1)(lambda: cross(high, unit).start())
            to_mate(high, unit).start()

    def crossed(step, unit):
        low, high = vox - step, vox + step

        @pl.when(low > 0)
        def _():
            cross(low, unit, 1 - chan).wait_recv()
            to_mate(low, pieces + unit).start()

        @pl.when(high < count - 1)
        def _():
            cross(high, unit, 1 - chan).wait_recv()
            to_mate(high, pieces + unit).start()

    def from_mate(step):
        def settle(block):
            for unit in range(units):
                to_mate(block, unit, 1 - frm).wait_recv()

        if step == 0:
            settle(vox)
        else:
            pl.when(vox >= step)(lambda: settle(vox - step))
            pl.when(vox + step < count)(lambda: settle(vox + step))

    def gram(block, index, first=False):
        left, right = ((0, 0), (0, 1), (1, 1))[index]
        value = lax.dot_general(
            beams[block, left].reshape(2 * cells, pair),
            beams[block, right].reshape(2 * cells, pair),
            (((0,), (0,)), ((), ())),
            preferred_element_type=jnp.float32,
        )
        if first:
            gram_ref[index] = value
        else:
            gram_ref[index] += value

    def nth(step):
        return jnp.where(2 * vox < count, (vox + step) % count, (vox + count - step) % count)

    tall = LAT_DEV + 4
    slots = near_ref.shape[1] - tall * depth

    def correlation():
        shape = near_ref.shape
        place = lax.broadcasted_iota(jnp.int32, shape, 0)
        source = lax.broadcasted_iota(jnp.int32, shape, 1)
        inside = source < tall * depth
        extra = source - tall * depth
        line = jnp.where(inside, source // depth, extra // 2)
        column = jnp.where(inside, source % depth, extra % 2 + jnp.where(chan == 0, depth, -2))
        down, across = line - place // depth, column - place % depth + 2
        least, most = jnp.where(vox > 0, 0, 2), jnp.where(vox + 1 < count, tall, tall - 2)
        valid = (line >= least) & (line < most) & (across >= 0) & (across < 5)
        key = jnp.where(valid, down * 5 + across, -1)
        value = jnp.zeros(shape, jnp.float32)
        for shift_a in range(5):
            for shift_b in range(5):
                value = jnp.where(key == shift_a * 5 + shift_b, psf_ref[shift_a, shift_b], value)
        near_ref[...], fine_ref[...] = split(value)

    def collect():
        before, after = jnp.maximum(vox - 1, 0), jnp.minimum(vox + 1, count - 1)
        edge = 2 * depth
        total = rows_ref.shape[0] // 2

        def both(side):
            def lines(block, where):
                parts = [beams[block, owner, side, where] for owner in (0, 1)]
                return jnp.concatenate([parts[0][:, :half], parts[1][:, :half], parts[0][:, half:], parts[1][:, half:]], axis=1)

            return [
                lines(before, slice(cells - edge, cells)),
                lines(vox, slice(0, cells)),
                lines(after, slice(0, edge)),
            ]

        other = jnp.concatenate(both(1 - chan), axis=0)
        picked = lax.broadcasted_iota(jnp.int32, (slots, tall * depth), 0)
        source = lax.broadcasted_iota(jnp.int32, (slots, tall * depth), 1)
        wanted = (picked // 2) * depth + picked % 2 + jnp.where(chan == 0, 0, depth - 2)
        picks = ((source == wanted) & (picked < 2 * tall)).astype(jnp.float32).astype(jnp.bfloat16)
        extra = jnp.dot(picks, other, preferred_element_type=jnp.float32).astype(jnp.bfloat16)
        start = 0
        for value in both(chan) + [extra]:
            size = value.shape[0]
            rows_ref[start : start + size, :] = value[:, :pair]
            rows_ref[total + start : total + start + size, :] = value[:, pair:]
            start += size

    def first_stage(index):
        if index == 0:
            from_mate(0)
        gram(vox, index, True)

    def stage(step):
        from_mate(step)
        if step == 1:
            collect()
        for index in range(3):
            gram(nth(step), index)

    events = [(unit, 0, functools.partial(own, unit)) for unit in range(units)]
    events += [(units + 1 + index, 3, functools.partial(first_stage, index)) for index in range(3)]
    events += [(units - 2, 2, correlation)]
    for step in range(1, count):
        last = step * HOP + units - 1
        events += [(step * HOP + unit, 1, functools.partial(relay, step, unit)) for unit in range(units)]
        if step < count - 1:
            start = units + (step - 1) * pieces + HOP - 1
            last = max(last, start + pieces - 1)
            events += [(start + unit, 2, functools.partial(crossed, step, unit)) for unit in range(pieces)]
        events += [(max(last, units + step * pieces + 1) + 1, 4, functools.partial(stage, step))]

    sums(1 - chan)
    pl.semaphore_wait(barrier, 4 - jnp.where(can_up, 0, 1) - jnp.where(can_down, 0, 1))
    for unit in range(pieces):
        swap(unit, 1 - chan).start()
    sums(chan)
    for unit in range(pieces, units):
        swap(unit, chan).start()
    for _, _, action in sorted(events, key=lambda event: event[:2]):
        action()

    for unit in range(units):
        swap(unit, 1 - chan if unit < pieces else chan).wait_send()
        for block in range(count):
            end = block == 0 or block == count - 1
            to_mate(block, unit).wait_send()
            if unit < pieces or end:
                pl.when(can_up & (vox >= block))(lambda: go_up(block, unit).wait_send())
                pl.when(can_down & (vox <= block))(lambda: go_down(block, unit).wait_send())
            if unit < pieces and not end:
                pl.when(vox != block)(lambda: cross(block, unit).wait_send())


def filter_kernel(rows_ref, gram_ref, near_ref, fine_ref, out_ref, real_ref, imag_ref):
    frm = lax.axis_index("frm")
    lat, depth, half = out_ref.shape
    total = rows_ref.shape[0] // 2

    def parts(index):
        block = gram_ref[index]
        return block[:half, :half] + block[half:, half:], block[:half, half:] - block[half:, :half]

    grams = {(0, 0): parts(0), (0, 1): parts(1), (1, 1): parts(2)}
    grams[1, 0] = (grams[0, 1][0].T, -grams[0, 1][1].T)
    eye = lax.broadcasted_iota(jnp.int32, (half, half), 0) == lax.broadcasted_iota(jnp.int32, (half, half), 1)
    diagonal = []
    for (row, column), (real, imag) in grams.items():
        if row == column:
            diagonal.append(jnp.sum(jnp.where(eye, real, 0.0), axis=0, keepdims=True))
            real = jnp.where(eye, 0.0, real)
        place = (slice(row * half, (row + 1) * half), slice(column * half, (column + 1) * half))
        real_ref[place] = real.astype(jnp.bfloat16)
        imag_ref[place] = imag.astype(jnp.bfloat16)
    trace = jnp.sum(diagonal[0] + diagonal[1], axis=1, keepdims=True)
    factor = (2 * half) / trace
    weight = jnp.concatenate(diagonal, axis=1)

    def mine(value):
        return jnp.where(frm == 0, value[:, :half], value[:, half:])

    def times(value, columns):
        value = value.astype(jnp.bfloat16)
        by_real = jnp.dot(value, real_ref[:, columns], preferred_element_type=jnp.float32)
        by_imag = jnp.dot(value, imag_ref[:, columns], preferred_element_type=jnp.float32)
        return jnp.concatenate([by_real[:total] - by_imag[total:], by_imag[:total] + by_real[total:]], axis=0)

    rows = rows_ref[...]
    echo = rows.astype(jnp.float32)
    every = slice(0, 2 * half)
    once = factor * (times(rows, every) + weight * echo)
    twice = factor * (times(once, every) + weight * once)
    mixed = POLY_COEFFS[2] * once + POLY_COEFFS[3] * twice
    own = pl.ds(pl.multiple_of(frm * half, half), half)
    term = factor * (times(mixed, own) + mine(weight) * mine(mixed))
    term += POLY_COEFFS[0] * mine(echo) + POLY_COEFFS[1] * mine(once)
    real, imag = term[:total], term[total:]
    high, low = split(jnp.sqrt(real * real + imag * imag + 1e-06))
    result = jnp.dot(near_ref[...], high, preferred_element_type=jnp.float32)
    result += jnp.dot(near_ref[...], low, preferred_element_type=jnp.float32)
    result += jnp.dot(fine_ref[...], high, preferred_element_type=jnp.float32)
    out_ref[...] = result.reshape(lat, depth, half)


def kernel_shards(count, echo_data, tile_weights, tile_target, tile_offset, tile_count, grid_map, psf_kernel):
    rows, half = echo_data.shape[2], echo_data.shape[4]
    slots, tile = tile_weights.shape[2], tile_weights.shape[4]
    voxels = grid_map.shape[1]
    cells, pair = voxels // 2, 2 * half
    depth = cells // LAT_DEV
    tall = LAT_DEV + 4
    total = tall * depth + -(-2 * tall // 16) * 16
    vmem, smem = pl.BlockSpec(memory_space=pltpu.VMEM), pl.BlockSpec(memory_space=pltpu.SMEM)
    operator = pl.pallas_call(
        beam_kernel,
        name="beam",
        out_shape=jax.ShapeDtypeStruct((2, voxels, rows), jnp.bfloat16),
        in_specs=[smem, smem, smem, vmem, vmem],
        out_specs=vmem,
        scratch_shapes=[pltpu.VMEM((rows // tile + 1, voxels, tile), jnp.float32)],
        compiler_params=pltpu.CompilerParams(vmem_limit_bytes=8 << 20),
    )(
        tile_target.reshape(-1),
        tile_offset.reshape(-1),
        tile_count,
        tile_weights.reshape(slots, tile, tile),
        grid_map,
    )
    dma = pltpu.SemaphoreType.DMA
    units, each, some = (2 * PIECES,), (count, 2 * PIECES), (count, PIECES)
    gathered = pl.pallas_call(
        functools.partial(gather_kernel, count),
        name="gather",
        out_shape=[
            jax.ShapeDtypeStruct((2 * total, pair), jnp.bfloat16),
            jax.ShapeDtypeStruct((3, pair, pair), jnp.float32),
            jax.ShapeDtypeStruct((cells, total), jnp.bfloat16),
            jax.ShapeDtypeStruct((cells, total), jnp.bfloat16),
        ],
        in_specs=[vmem, vmem, smem],
        out_specs=[vmem] * 4,
        scratch_shapes=[
            pltpu.VMEM((2, cells, pair), jnp.float32),
            pltpu.VMEM((2, cells, pair), jnp.bfloat16),
            pltpu.VMEM((2, cells, pair), jnp.bfloat16),
            pltpu.VMEM((count, 2, 2, cells, pair), jnp.bfloat16),
        ]
        + [dma(units)] * 2
        + [dma(each)] * 5
        + [dma(some)] * 2,
        compiler_params=pltpu.CompilerParams(collective_id=0, has_side_effects=True, vmem_limit_bytes=16 << 20),
    )(operator, echo_data.reshape(rows, pair), psf_kernel)
    return pl.pallas_call(
        filter_kernel,
        name="filter",
        out_shape=jax.ShapeDtypeStruct((LAT_DEV, depth, half), jnp.float32),
        in_specs=[vmem] * 4,
        out_specs=vmem,
        scratch_shapes=[pltpu.VMEM((pair, pair), jnp.bfloat16)] * 2,
        compiler_params=pltpu.CompilerParams(vmem_limit_bytes=16 << 20),
    )(*gathered)


def solution(mesh):
    in_specs = (
        P(("groups", "vox"), "chan", None, None, "frm"),
        P("vox", "chan", None, None, None),
        P("vox", "chan", None),
        P("vox", "chan", None),
        P("vox", "chan"),
        P("vox", None),
        P(),
    )
    out_specs = P(("groups", "vox"), "chan", "frm")
    body = shards
    if mesh.shape["chan"] == 2 and mesh.shape["frm"] == 2:
        body = functools.partial(kernel_shards, mesh.shape["vox"])
    return jax.shard_map(body, mesh=mesh, in_specs=in_specs, out_specs=out_specs, check_vma=False)
```

```python
import functools

import jax
import jax.numpy as jnp
from jax import lax
from jax.experimental import pallas as pl
from jax.experimental.pallas import tpu as pltpu
from jax.sharding import PartitionSpec as P

MESH = pl.DeviceIdType.MESH
PIECES = 4
HOP = 3
GROUP = 8

TBATCH = 8
LAT_DEV = 8


POLY_COEFFS = (1.0, -0.6, 0.15, -0.03)


def with_halo(shard, sides, width):
    for axis, dim in sides:
        devices, length = (lax.axis_size(axis), shard.shape[dim])
        up = [(i, (i + 1) % devices) for i in range(devices - 1)]
        down = [(j, i) for i, j in up]
        last = lax.slice_in_dim(shard, length - width, length, axis=dim)
        leading = lax.slice_in_dim(shard, 0, width, axis=dim)
        before = lax.ppermute(last, axis, up)
        after = lax.ppermute(leading, axis, down)
        shard = jnp.concatenate([before, shard, after], axis=dim)
    return shard


def complex_times(left_real, left_imag, right_real, right_imag):
    level = lax.Precision.HIGH
    real_part = jnp.dot(
        left_real, right_real, precision=level, preferred_element_type=jnp.float32
    ) - jnp.dot(left_imag, right_imag, precision=level, preferred_element_type=jnp.float32)
    imag_part = jnp.dot(
        left_real, right_imag, precision=level, preferred_element_type=jnp.float32
    ) + jnp.dot(left_imag, right_real, precision=level, preferred_element_type=jnp.float32)
    return (real_part, imag_part)


def tile_pass(flat_echo, weights, tile_goal, tile_start, live_total, tiles_out):
    tile_size = weights.shape[-1]
    col_count = flat_echo.shape[-1]
    slot_count = weights.shape[0]
    lane_ids = jnp.arange(TBATCH, dtype=jnp.int32)
    target_ids = jnp.arange(tiles_out, dtype=jnp.int32)
    zero_index = jnp.zeros((), jnp.int32)

    def cut_rows(offset_id):
        return lax.dynamic_slice(flat_echo, (offset_id, zero_index), (tile_size, col_count))

    def one_turn(turn_index, totals):
        where_at = turn_index * TBATCH + lane_ids
        live_lane = where_at < live_total
        chosen = jnp.minimum(where_at, slot_count - 1)
        picked = weights[chosen]
        samples = jax.vmap(cut_rows)(tile_start[chosen])
        product = jnp.einsum("krs,ksc->krc", picked, samples, preferred_element_type=jnp.float32)
        placing = ((tile_goal[chosen][:, None] == target_ids[None, :]) & live_lane[:, None]).astype(
            jnp.float32
        )
        return totals + jnp.einsum(
            "kt,krc->trc", placing, product, precision=lax.Precision.HIGHEST
        )

    start_totals = jnp.zeros((tiles_out, tile_size, col_count), jnp.float32)
    turn_count = (live_total + TBATCH - 1) // TBATCH
    return lax.fori_loop(0, turn_count, one_turn, start_totals)


def shards(echo_data, tile_weights, tile_target, tile_offset, tile_count, grid_map, psf_kernel):
    row_count = echo_data.shape[2]
    half_frames = echo_data.shape[4]
    tile_size = tile_weights.shape[-1]
    slot_count = tile_weights.shape[2]
    voxels = grid_map.shape[1]
    tiles_out = voxels // tile_size
    flat_echo = echo_data.reshape(row_count, 2 * half_frames)
    weights = tile_weights.reshape(slot_count, tile_size, tile_size)
    tile_sums = tile_pass(
        flat_echo,
        weights,
        tile_target.reshape(-1),
        tile_offset.reshape(-1),
        tile_count[0, 0],
        tiles_out,
    )
    arranged = jnp.take(tile_sums.reshape(voxels, 2, half_frames), grid_map[0], axis=0)
    arranged = arranged.reshape(LAT_DEV, voxels // LAT_DEV, 2, half_frames)
    beamformed = lax.psum_scatter(arranged, "chan", scatter_dimension=1, tiled=True).astype(
        jnp.bfloat16
    )
    lat_count = beamformed.shape[0]
    depth_count = beamformed.shape[1]
    cell_count = lat_count * depth_count
    own_frames = beamformed.reshape(cell_count, 2, half_frames)
    all_frames = lax.all_gather(own_frames, "frm", axis=2, tiled=True)
    frames = all_frames.shape[2]
    own_flat = own_frames.reshape(cell_count, 2 * half_frames)
    all_flat = all_frames.reshape(cell_count, 2 * frames)
    gram_block = lax.dot_general(
        own_flat, all_flat, (((0,), (0,)), ((), ())), preferred_element_type=jnp.float32
    )
    gram_real = gram_block[:half_frames, :frames] + gram_block[half_frames:, frames:]
    gram_imag = gram_block[:half_frames, frames:] - gram_block[half_frames:, :frames]
    frame_start = lax.axis_index("frm") * half_frames
    echo_real = all_frames[:, 0, :].astype(jnp.float32)
    echo_imag = all_frames[:, 1, :].astype(jnp.float32)
    energy = jnp.sum(echo_real * echo_real + echo_imag * echo_imag)
    gram_real, gram_imag, trace_value = lax.psum((gram_real, gram_imag, energy), ("vox", "chan"))
    factor = frames / trace_value
    norm_real = factor * gram_real
    norm_imag = factor * gram_imag
    full_real, full_imag = (
        lax.all_gather(norm_real, "frm", axis=0, tiled=True),
        lax.all_gather(norm_imag, "frm", axis=0, tiled=True),
    )
    identity = jnp.eye(frames, dtype=jnp.float32)
    poly_real = POLY_COEFFS[3] * full_real + POLY_COEFFS[2] * identity
    poly_imag = POLY_COEFFS[3] * full_imag
    poly_real, poly_imag = complex_times(poly_real, poly_imag, full_real, full_imag)
    poly_real = poly_real + POLY_COEFFS[1] * identity
    cols_real = lax.dynamic_slice_in_dim(full_real, frame_start, half_frames, 1)
    cols_imag = lax.dynamic_slice_in_dim(full_imag, frame_start, half_frames, 1)
    filter_real, filter_imag = complex_times(poly_real, poly_imag, cols_real, cols_imag)
    filter_real = filter_real + POLY_COEFFS[0] * lax.dynamic_slice_in_dim(
        identity, frame_start, half_frames, 1
    )
    out_real, out_imag = complex_times(echo_real, echo_imag, filter_real, filter_imag)
    envelope = jnp.sqrt(out_real * out_real + out_imag * out_imag + 1e-06)
    envelope = envelope.reshape(lat_count, depth_count, half_frames)
    padded = with_halo(envelope, (("vox", 0), ("chan", 1)), 2)
    psf_image = jnp.zeros_like(envelope)
    for shift_a in range(5):
        for shift_b in range(5):
            psf_image = (
                psf_image
                + psf_kernel[shift_a, shift_b]
                * padded[shift_a : shift_a + lat_count, shift_b : shift_b + depth_count]
            )
    return psf_image


def split(value):
    high = value.astype(jnp.bfloat16)
    return high, (value - high.astype(jnp.float32)).astype(jnp.bfloat16)


def beam_kernel(
    goal_hbm, start_hbm, live_hbm, weights_hbm, map_hbm, out_ref, operator, goal_ref, start_ref, live_ref, weights_ref, map_ref, few, many
):
    blocks, voxels, tile = operator.shape
    slots = weights_ref.shape[0]
    turns = slots // GROUP
    small = [
        pltpu.make_async_copy(source, target, few.at[index])
        for index, (source, target) in enumerate(
            ((live_hbm, live_ref), (start_hbm, start_ref), (goal_hbm, goal_ref), (map_hbm, map_ref))
        )
    ]

    def fetch(turn):
        span = pl.ds(turn * GROUP, GROUP)
        return pltpu.make_async_copy(weights_hbm.at[span], weights_ref.at[span], many.at[turn])

    for copy in small:
        copy.start()
    for turn in range(turns):
        fetch(turn).start()
    operator[...] = jnp.zeros_like(operator)
    lane = lax.broadcasted_iota(jnp.int32, (tile, tile), 1)
    for copy in small:
        copy.wait()
    live = live_ref[0, 0]
    used = (live + GROUP - 1) // GROUP

    def place(turn, carry):
        fetch(turn).wait()
        ready = []
        for index in range(GROUP):
            kept = turn * GROUP + index
            slot = kept
            first = start_ref[0, kept]
            block = first // tile
            shift = first - block * tile
            rows = pl.ds(pl.multiple_of(goal_ref[0, kept] * tile, tile), tile)
            turned = pltpu.roll(weights_ref[kept].astype(jnp.float32), shift, 1)
            limit = jnp.where(slot < live, shift, tile)
            least = jnp.where(slot < live, 0, tile)
            ready.append((block, rows, jnp.where(lane >= limit, turned, 0.0), turned, shift, least))
        for block, rows, high, turned, shift, least in ready:
            operator[block, rows, :] += high
            operator[block + 1, rows, :] += jnp.where((lane < shift) & (lane >= least), turned, 0.0)
        return carry

    lax.fori_loop(0, used, place, 0)
    picks = lax.broadcasted_iota(jnp.int32, (voxels, voxels), 0) == map_ref[...]
    picks = picks.astype(jnp.float32).T.astype(jnp.bfloat16)
    cells = voxels // 2
    width = cells // LAT_DEV
    for block in range(blocks - 1):
        columns = slice(block * tile, (block + 1) * tile)
        for level, value in enumerate(split(operator[block])):
            moved = jnp.dot(picks, value, preferred_element_type=jnp.float32).astype(jnp.bfloat16)
            for lat in range(LAT_DEV):
                for half in range(2):
                    source = (lat * 2 + half) * width
                    target = level * cells + lat * width
                    out_ref[half, target : target + width, columns] = moved[source : source + width]

    def settle(turn, carry):
        fetch(turn).wait()
        return carry

    lax.fori_loop(used, turns, settle, 0)


def gather_kernel(
    count, operator_ref, echo_ref, psf_ref, rows_ref, gram_ref, near_ref, fine_ref, part, arrived, beams,
    swap_send, swap_recv, own_recv, mate_recv, up_send, down_send, mate_send, side_send, twin_send, side_recv,
):
    vox, chan, frm = lax.axis_index("vox"), lax.axis_index("chan"), lax.axis_index("frm")
    beside, mate = {"chan": 1 - chan}, {"frm": 1 - frm}
    above, below = {"vox": vox + 1}, {"vox": vox - 1}
    can_up, can_down = vox + 1 < count, vox > 0
    pieces = PIECES
    cells, pair = beams.shape[3], beams.shape[4]
    half = pair // 2
    height = cells // pieces
    depth = cells // LAT_DEV
    barrier = pltpu.get_barrier_semaphore()

    def greet(target):
        pl.semaphore_signal(barrier, inc=1, device_id=target, device_id_type=MESH)

    greet(beside)
    greet(mate)
    pl.when(can_up)(lambda: greet(above))
    pl.when(can_down)(lambda: greet(below))

    def sums(side):
        value = jnp.dot(operator_ref[side], echo_ref[...], preferred_element_type=jnp.float32)
        part[side] = value[:cells] + value[cells:]

    def remote(source, target, sent, received, device):
        return pltpu.make_async_remote_copy(
            src_ref=source, dst_ref=target, send_sem=sent, recv_sem=received, device_id=device, device_id_type=MESH
        )

    def rows(unit):
        return pl.ds((unit % pieces) * height, height)

    def side_of(unit):
        return chan if unit < pieces else 1 - chan

    def swap(unit):
        return remote(part.at[1 - chan, rows(unit)], arrived.at[rows(unit)], swap_send.at[0], swap_recv.at[unit], beside)

    def item(block, unit, sent, device):
        place = beams.at[block, frm, side_of(unit), rows(unit)]
        return remote(place, place, sent, own_recv.at[block, unit], device)

    def to_mate(block, unit):
        place = beams.at[block, frm, side_of(unit), rows(unit)]
        return remote(place, place, mate_send.at[block], mate_recv.at[block, side_of(unit)], mate)

    def mated(block, owner, side):
        place = beams.at[block, owner, side]
        return remote(place, place, mate_send.at[block], mate_recv.at[block, side], mate)

    def go_up(block, unit):
        return item(block, unit, up_send.at[block] if unit < pieces else twin_send.at[0], above)

    def go_down(block, unit):
        return item(block, unit, down_send.at[block] if unit < pieces else twin_send.at[1], below)

    def cross(block, unit, side=None):
        place = beams.at[block, frm, chan if side is None else side, rows(unit)]
        return remote(place, place, side_send.at[block], side_recv.at[block, unit], beside)

    def own(unit):
        swap(unit).wait_recv()
        mine = part[chan, rows(unit)] + arrived[rows(unit)]
        beams[vox, frm, chan, rows(unit)] = mine.astype(beams.dtype)
        pl.when(can_up)(lambda: go_up(vox, unit).start())
        pl.when(can_down)(lambda: go_down(vox, unit).start())
        cross(vox, unit).start()
        to_mate(vox, unit).start()

    def own_other(unit):
        cross(vox, unit, 1 - chan).wait_recv()
        pl.when(can_up)(lambda: go_up(vox, pieces + unit).start())
        pl.when(can_down)(lambda: go_down(vox, pieces + unit).start())
        to_mate(vox, pieces + unit).start()

    def relay(step, unit):
        low, high = vox - step, vox + step

        @pl.when(vox >= step)
        def _():
            item(low, unit, up_send.at[0], above).wait_recv()
            pl.when(can_up)(lambda: go_up(low, unit).start())
            if step > 1:
                cross(low, unit).start()
            to_mate(low, unit).start()

        @pl.when(vox + step < count)
        def _():
            item(high, unit, down_send.at[0], below).wait_recv()
            pl.when(can_down)(lambda: go_down(high, unit).start())
            if step > 1:
                cross(high, unit).start()
            to_mate(high, unit).start()

    def other(step, unit):
        low, high = vox - step, vox + step

        @pl.when(vox >= step)
        def _():
            if step > 1:
                cross(low, unit, 1 - chan).wait_recv()
            else:
                item(low, pieces + unit, up_send.at[0], above).wait_recv()
            to_mate(low, pieces + unit).start()

        @pl.when(vox + step < count)
        def _():
            if step > 1:
                cross(high, unit, 1 - chan).wait_recv()
            else:
                item(high, pieces + unit, down_send.at[0], below).wait_recv()
            to_mate(high, pieces + unit).start()

    def from_mate(step, side):
        def settle(block):
            mated(block, 1 - frm, side).wait_recv()

        if step == 0:
            settle(vox)
        else:
            pl.when(vox >= step)(lambda: settle(vox - step))
            pl.when(vox + step < count)(lambda: settle(vox + step))

    def gram(halves, index, first=False):
        left, right = ((0, 0), (0, 1), (1, 1))[index]

        def take(owner):
            return jnp.concatenate([beams[block, owner, side] for block, side in halves], axis=0)

        value = lax.dot_general(
            take(left), take(right), (((0,), (0,)), ((), ())), preferred_element_type=jnp.float32
        )
        if first:
            gram_ref[index] = value
        else:
            gram_ref[index] += value

    def nth(step):
        return jnp.where(2 * vox < count, (vox + step) % count, (vox + count - step) % count)

    tall = LAT_DEV + 4
    slots = near_ref.shape[1] - tall * depth

    def correlation():
        shape = near_ref.shape
        place = lax.broadcasted_iota(jnp.int32, shape, 0)
        source = lax.broadcasted_iota(jnp.int32, shape, 1)
        inside = source < tall * depth
        extra = source - tall * depth
        line = jnp.where(inside, source // depth, extra // 2)
        column = jnp.where(inside, source % depth, extra % 2 + jnp.where(chan == 0, depth, -2))
        down, across = line - place // depth, column - place % depth + 2
        least, most = jnp.where(vox > 0, 0, 2), jnp.where(vox + 1 < count, tall, tall - 2)
        valid = (line >= least) & (line < most) & (across >= 0) & (across < 5)
        key = jnp.where(valid, down * 5 + across, -1)
        value = jnp.zeros(shape, jnp.float32)
        taps = psf_ref[...]
        for shift_a in range(5):
            for shift_b in range(5):
                value = jnp.where(key == shift_a * 5 + shift_b, taps[shift_a : shift_a + 1, shift_b : shift_b + 1], value)
        near_ref[...], fine_ref[...] = split(value)

    def place_rows(start, value):
        total = rows_ref.shape[0] // 2
        size = value.shape[0]
        rows_ref[start : start + size, :] = value[:, :pair]
        rows_ref[total + start : total + start + size, :] = value[:, pair:]

    def collect():
        before, after = jnp.maximum(vox - 1, 0), jnp.minimum(vox + 1, count - 1)
        edge = 2 * depth

        def both(side):
            def lines(block, where):
                parts = [beams[block, owner, side, where] for owner in (0, 1)]
                return jnp.concatenate(
                    [parts[0][:, :half], parts[1][:, :half], parts[0][:, half:], parts[1][:, half:]], axis=1
                )

            return jnp.concatenate(
                [
                    lines(before, slice(cells - edge, cells)),
                    lines(vox, slice(0, cells)),
                    lines(after, slice(0, edge)),
                ],
                axis=0,
            )

        picked = lax.broadcasted_iota(jnp.int32, (slots, tall * depth), 0)
        source = lax.broadcasted_iota(jnp.int32, (slots, tall * depth), 1)
        wanted = (picked // 2) * depth + picked % 2 + jnp.where(chan == 0, 0, depth - 2)
        picks = ((source == wanted) & (picked < 2 * tall)).astype(jnp.float32).astype(jnp.bfloat16)
        extra = jnp.dot(picks, both(1 - chan), preferred_element_type=jnp.float32).astype(jnp.bfloat16)
        place_rows(0, both(chan))
        place_rows(tall * depth, extra)

    def first_stage(index):
        if index == 0:
            from_mate(0, chan)
            from_mate(0, 1 - chan)
        gram([(vox, 0), (vox, 1)], index, True)

    def stage(members):
        for step, far in members:
            from_mate(step, 1 - chan if far else chan)
        if (1, 1) in members:
            collect()
        for index in range(3):
            gram([(nth(step), 1 - chan if far else chan) for step, far in members], index)

    def ready(step, far):
        if far:
            return 4 * pieces - 1 if step == 1 else 2 * pieces + 3 * step + 2
        return 2 * (pieces - 1) + HOP * step

    events = [(2 * pieces - 2, 2, correlation)]
    for unit in range(pieces):
        events += [(2 * unit, 0, functools.partial(own, unit))]
        events += [(2 * pieces - 1 + unit, 1, functools.partial(own_other, unit))]
        for step in range(1, count):
            events += [(2 * unit + HOP * step, 1, functools.partial(relay, step, unit))]
            when = 3 * pieces + unit if step == 1 else 2 * unit + HOP * step + 4
            events += [(when, 1, functools.partial(other, step, unit))]
    events += [(3 * pieces - 1, 3, functools.partial(first_stage, index)) for index in range(3)]
    order = [(step, far) for far in (0, 1) for step in range(1, count)]
    latest = 0
    for turn in range(count - 1):
        members = order[2 * turn : 2 * turn + 2]
        latest = max([latest] + [ready(*member) for member in members]) + 1
        events += [(latest, 4, functools.partial(stage, members))]

    sums(1 - chan)
    pl.semaphore_wait(barrier, 4 - jnp.where(can_up, 0, 1) - jnp.where(can_down, 0, 1))
    for unit in range(pieces):
        swap(unit).start()
    sums(chan)
    for _, _, action in sorted(events, key=lambda event: event[:2]):
        action()

    remote(part.at[1 - chan], arrived, swap_send.at[0], swap_recv.at[0], beside).wait_send()
    twin = beams.at[vox, frm, 1 - chan]
    pl.when(can_up)(remote(twin, twin, twin_send.at[0], own_recv.at[0, 0], above).wait_send)
    pl.when(can_down)(remote(twin, twin, twin_send.at[1], own_recv.at[0, 0], below).wait_send)
    for block in range(count):
        mated(block, frm, 0).wait_send()
        mated(block, frm, 1).wait_send()
        place = beams.at[block, frm, chan]
        up = remote(place, place, up_send.at[block], own_recv.at[block, 0], above)
        down = remote(place, place, down_send.at[block], own_recv.at[block, 0], below)
        side = remote(place, place, side_send.at[block], side_recv.at[block, 0], beside)
        pl.when(can_up & (vox >= block))(up.wait_send)
        pl.when(can_down & (vox <= block))(down.wait_send)
        pl.when((vox != block + 1) & (vox != block - 1))(side.wait_send)


def filter_kernel(rows_ref, gram_ref, near_ref, fine_ref, out_ref, real_ref, imag_ref):
    frm = lax.axis_index("frm")
    lat, depth, half = out_ref.shape
    total = rows_ref.shape[0] // 2

    def parts(index):
        block = gram_ref[index]
        return block[:half, :half] + block[half:, half:], block[:half, half:] - block[half:, :half]

    grams = {(0, 0): parts(0), (0, 1): parts(1), (1, 1): parts(2)}
    grams[1, 0] = (grams[0, 1][0].T, -grams[0, 1][1].T)
    eye = lax.broadcasted_iota(jnp.int32, (half, half), 0) == lax.broadcasted_iota(jnp.int32, (half, half), 1)
    diagonal = []
    for (row, column), (real, imag) in grams.items():
        if row == column:
            diagonal.append(jnp.sum(jnp.where(eye, real, 0.0), axis=0, keepdims=True))
            real = jnp.where(eye, 0.0, real)
        place = (slice(row * half, (row + 1) * half), slice(column * half, (column + 1) * half))
        real_ref[place] = real.astype(jnp.bfloat16)
        imag_ref[place] = imag.astype(jnp.bfloat16)
    trace = jnp.sum(diagonal[0] + diagonal[1], axis=1, keepdims=True)
    factor = (2 * half) / trace
    weight = jnp.concatenate(diagonal, axis=1)

    def mine(value):
        return jnp.where(frm == 0, value[:, :half], value[:, half:])

    def times(value, columns):
        value = value.astype(jnp.bfloat16)
        by_real = jnp.dot(value, real_ref[:, columns], preferred_element_type=jnp.float32)
        by_imag = jnp.dot(value, imag_ref[:, columns], preferred_element_type=jnp.float32)
        return jnp.concatenate([by_real[:total] - by_imag[total:], by_imag[:total] + by_real[total:]], axis=0)

    rows = rows_ref[...]
    echo = rows.astype(jnp.float32)
    every = slice(0, 2 * half)
    once = factor * (times(rows, every) + weight * echo)
    twice = factor * (times(once, every) + weight * once)
    mixed = POLY_COEFFS[2] * once + POLY_COEFFS[3] * twice
    own = pl.ds(pl.multiple_of(frm * half, half), half)
    term = factor * (times(mixed, own) + mine(weight) * mine(mixed))
    term += POLY_COEFFS[0] * mine(echo) + POLY_COEFFS[1] * mine(once)
    real, imag = term[:total], term[total:]
    high, low = split(jnp.sqrt(real * real + imag * imag + 1e-06))
    result = jnp.dot(near_ref[...], high, preferred_element_type=jnp.float32)
    result += jnp.dot(near_ref[...], low, preferred_element_type=jnp.float32)
    result += jnp.dot(fine_ref[...], high, preferred_element_type=jnp.float32)
    out_ref[...] = result.reshape(lat, depth, half)


def kernel_shards(count, echo_data, tile_weights, tile_target, tile_offset, tile_count, grid_map, psf_kernel):
    rows, half = echo_data.shape[2], echo_data.shape[4]
    slots, tile = tile_weights.shape[2], tile_weights.shape[4]
    voxels = grid_map.shape[1]
    cells, pair = voxels // 2, 2 * half
    depth = cells // LAT_DEV
    tall = LAT_DEV + 4
    total = tall * depth + -(-2 * tall // 16) * 16
    vmem = pl.BlockSpec(memory_space=pltpu.VMEM)
    operator = pl.pallas_call(
        beam_kernel,
        name="beam",
        out_shape=jax.ShapeDtypeStruct((2, voxels, rows), jnp.bfloat16),
        in_specs=[pl.BlockSpec(memory_space=pltpu.HBM)] * 5,
        out_specs=vmem,
        scratch_shapes=[
            pltpu.VMEM((rows // tile + 1, voxels, tile), jnp.float32),
            pltpu.SMEM((1, slots), jnp.int32),
            pltpu.SMEM((1, slots), jnp.int32),
            pltpu.SMEM((1, 1), jnp.int32),
            pltpu.VMEM((slots, tile, tile), jnp.bfloat16),
            pltpu.VMEM((1, voxels), jnp.int32),
            pltpu.SemaphoreType.DMA((4,)),
            pltpu.SemaphoreType.DMA((slots // GROUP,)),
        ],
        compiler_params=pltpu.CompilerParams(vmem_limit_bytes=8 << 20),
    )(
        *[
            pltpu.with_memory_space_constraint(value, pltpu.HBM) if value.size > 1 else value
            for value in (
                tile_target.reshape(1, slots),
                tile_offset.reshape(1, slots),
                tile_count,
                tile_weights.reshape(slots, tile, tile),
                grid_map,
            )
        ]
    )
    dma = pltpu.SemaphoreType.DMA
    gathered = pl.pallas_call(
        functools.partial(gather_kernel, count),
        name="gather",
        out_shape=[
            jax.ShapeDtypeStruct((2 * total, pair), jnp.bfloat16),
            jax.ShapeDtypeStruct((3, pair, pair), jnp.float32),
            jax.ShapeDtypeStruct((cells, total), jnp.bfloat16),
            jax.ShapeDtypeStruct((cells, total), jnp.bfloat16),
        ],
        in_specs=[vmem] * 3,
        out_specs=[vmem] * 4,
        scratch_shapes=[
            pltpu.VMEM((2, cells, pair), jnp.float32),
            pltpu.VMEM((cells, pair), jnp.float32),
            pltpu.VMEM((count, 2, 2, cells, pair), jnp.bfloat16),
            dma((1,)),
            dma((PIECES,)),
            dma((count, 2 * PIECES)),
            dma((count, 2)),
        ]
        + [dma((count,))] * 4
        + [dma((2,)), dma((count, PIECES))],
        compiler_params=pltpu.CompilerParams(collective_id=0, has_side_effects=True, vmem_limit_bytes=16 << 20),
    )(operator, echo_data.reshape(rows, pair), psf_kernel)
    return pl.pallas_call(
        filter_kernel,
        name="filter",
        out_shape=jax.ShapeDtypeStruct((LAT_DEV, depth, half), jnp.float32),
        in_specs=[vmem] * 4,
        out_specs=vmem,
        scratch_shapes=[pltpu.VMEM((pair, pair), jnp.bfloat16)] * 2,
        compiler_params=pltpu.CompilerParams(vmem_limit_bytes=16 << 20),
    )(*gathered)


def solution(mesh):
    in_specs = (
        P(("groups", "vox"), "chan", None, None, "frm"),
        P("vox", "chan", None, None, None),
        P("vox", "chan", None),
        P("vox", "chan", None),
        P("vox", "chan"),
        P("vox", None),
        P(),
    )
    out_specs = P(("groups", "vox"), "chan", "frm")
    body = shards
    if mesh.shape["chan"] == 2 and mesh.shape["frm"] == 2:
        body = functools.partial(kernel_shards, mesh.shape["vox"])
    return jax.shard_map(body, mesh=mesh, in_specs=in_specs, out_specs=out_specs, check_vma=False)
```

```python
import functools

import jax
import jax.numpy as jnp
from jax import lax
from jax.experimental import pallas as pl
from jax.experimental.pallas import tpu as pltpu
from jax.sharding import PartitionSpec as P

MESH = pl.DeviceIdType.MESH
PIECES = 4
HOP = 1
PACE = 2
LAG = 5
TWIN = (7, 1)
SIDE = (12, 1)
FIRST = 2
GROUP = 8

TBATCH = 8
LAT_DEV = 8


POLY_COEFFS = (1.0, -0.6, 0.15, -0.03)


def with_halo(shard, sides, width):
    for axis, dim in sides:
        devices, length = (lax.axis_size(axis), shard.shape[dim])
        up = [(i, (i + 1) % devices) for i in range(devices - 1)]
        down = [(j, i) for i, j in up]
        last = lax.slice_in_dim(shard, length - width, length, axis=dim)
        leading = lax.slice_in_dim(shard, 0, width, axis=dim)
        before = lax.ppermute(last, axis, up)
        after = lax.ppermute(leading, axis, down)
        shard = jnp.concatenate([before, shard, after], axis=dim)
    return shard


def complex_times(left_real, left_imag, right_real, right_imag):
    level = lax.Precision.HIGH
    real_part = jnp.dot(
        left_real, right_real, precision=level, preferred_element_type=jnp.float32
    ) - jnp.dot(left_imag, right_imag, precision=level, preferred_element_type=jnp.float32)
    imag_part = jnp.dot(
        left_real, right_imag, precision=level, preferred_element_type=jnp.float32
    ) + jnp.dot(left_imag, right_real, precision=level, preferred_element_type=jnp.float32)
    return (real_part, imag_part)


def tile_pass(flat_echo, weights, tile_goal, tile_start, live_total, tiles_out):
    tile_size = weights.shape[-1]
    col_count = flat_echo.shape[-1]
    slot_count = weights.shape[0]
    lane_ids = jnp.arange(TBATCH, dtype=jnp.int32)
    target_ids = jnp.arange(tiles_out, dtype=jnp.int32)
    zero_index = jnp.zeros((), jnp.int32)

    def cut_rows(offset_id):
        return lax.dynamic_slice(flat_echo, (offset_id, zero_index), (tile_size, col_count))

    def one_turn(turn_index, totals):
        where_at = turn_index * TBATCH + lane_ids
        live_lane = where_at < live_total
        chosen = jnp.minimum(where_at, slot_count - 1)
        picked = weights[chosen]
        samples = jax.vmap(cut_rows)(tile_start[chosen])
        product = jnp.einsum("krs,ksc->krc", picked, samples, preferred_element_type=jnp.float32)
        placing = ((tile_goal[chosen][:, None] == target_ids[None, :]) & live_lane[:, None]).astype(
            jnp.float32
        )
        return totals + jnp.einsum(
            "kt,krc->trc", placing, product, precision=lax.Precision.HIGHEST
        )

    start_totals = jnp.zeros((tiles_out, tile_size, col_count), jnp.float32)
    turn_count = (live_total + TBATCH - 1) // TBATCH
    return lax.fori_loop(0, turn_count, one_turn, start_totals)


def shards(echo_data, tile_weights, tile_target, tile_offset, tile_count, grid_map, psf_kernel):
    row_count = echo_data.shape[2]
    half_frames = echo_data.shape[4]
    tile_size = tile_weights.shape[-1]
    slot_count = tile_weights.shape[2]
    voxels = grid_map.shape[1]
    tiles_out = voxels // tile_size
    flat_echo = echo_data.reshape(row_count, 2 * half_frames)
    weights = tile_weights.reshape(slot_count, tile_size, tile_size)
    tile_sums = tile_pass(
        flat_echo,
        weights,
        tile_target.reshape(-1),
        tile_offset.reshape(-1),
        tile_count[0, 0],
        tiles_out,
    )
    arranged = jnp.take(tile_sums.reshape(voxels, 2, half_frames), grid_map[0], axis=0)
    arranged = arranged.reshape(LAT_DEV, voxels // LAT_DEV, 2, half_frames)
    beamformed = lax.psum_scatter(arranged, "chan", scatter_dimension=1, tiled=True).astype(
        jnp.bfloat16
    )
    lat_count = beamformed.shape[0]
    depth_count = beamformed.shape[1]
    cell_count = lat_count * depth_count
    own_frames = beamformed.reshape(cell_count, 2, half_frames)
    all_frames = lax.all_gather(own_frames, "frm", axis=2, tiled=True)
    frames = all_frames.shape[2]
    own_flat = own_frames.reshape(cell_count, 2 * half_frames)
    all_flat = all_frames.reshape(cell_count, 2 * frames)
    gram_block = lax.dot_general(
        own_flat, all_flat, (((0,), (0,)), ((), ())), preferred_element_type=jnp.float32
    )
    gram_real = gram_block[:half_frames, :frames] + gram_block[half_frames:, frames:]
    gram_imag = gram_block[:half_frames, frames:] - gram_block[half_frames:, :frames]
    frame_start = lax.axis_index("frm") * half_frames
    echo_real = all_frames[:, 0, :].astype(jnp.float32)
    echo_imag = all_frames[:, 1, :].astype(jnp.float32)
    energy = jnp.sum(echo_real * echo_real + echo_imag * echo_imag)
    gram_real, gram_imag, trace_value = lax.psum((gram_real, gram_imag, energy), ("vox", "chan"))
    factor = frames / trace_value
    norm_real = factor * gram_real
    norm_imag = factor * gram_imag
    full_real, full_imag = (
        lax.all_gather(norm_real, "frm", axis=0, tiled=True),
        lax.all_gather(norm_imag, "frm", axis=0, tiled=True),
    )
    identity = jnp.eye(frames, dtype=jnp.float32)
    poly_real = POLY_COEFFS[3] * full_real + POLY_COEFFS[2] * identity
    poly_imag = POLY_COEFFS[3] * full_imag
    poly_real, poly_imag = complex_times(poly_real, poly_imag, full_real, full_imag)
    poly_real = poly_real + POLY_COEFFS[1] * identity
    cols_real = lax.dynamic_slice_in_dim(full_real, frame_start, half_frames, 1)
    cols_imag = lax.dynamic_slice_in_dim(full_imag, frame_start, half_frames, 1)
    filter_real, filter_imag = complex_times(poly_real, poly_imag, cols_real, cols_imag)
    filter_real = filter_real + POLY_COEFFS[0] * lax.dynamic_slice_in_dim(
        identity, frame_start, half_frames, 1
    )
    out_real, out_imag = complex_times(echo_real, echo_imag, filter_real, filter_imag)
    envelope = jnp.sqrt(out_real * out_real + out_imag * out_imag + 1e-06)
    envelope = envelope.reshape(lat_count, depth_count, half_frames)
    padded = with_halo(envelope, (("vox", 0), ("chan", 1)), 2)
    psf_image = jnp.zeros_like(envelope)
    for shift_a in range(5):
        for shift_b in range(5):
            psf_image = (
                psf_image
                + psf_kernel[shift_a, shift_b]
                * padded[shift_a : shift_a + lat_count, shift_b : shift_b + depth_count]
            )
    return psf_image


def split(value):
    high = value.astype(jnp.bfloat16)
    return high, (value - high.astype(jnp.float32)).astype(jnp.bfloat16)


def beam_kernel(
    goal_hbm, start_hbm, live_hbm, weights_hbm, map_hbm, out_ref, operator, goal_ref, start_ref, live_ref, weights_ref, map_ref, few, many
):
    blocks, voxels, tile = operator.shape
    slots = weights_ref.shape[0]
    turns = slots // GROUP
    small = [
        pltpu.make_async_copy(source, target, few.at[index])
        for index, (source, target) in enumerate(
            ((live_hbm, live_ref), (start_hbm, start_ref), (goal_hbm, goal_ref), (map_hbm, map_ref))
        )
    ]

    def fetch(turn):
        span = pl.ds(turn * GROUP, GROUP)
        return pltpu.make_async_copy(weights_hbm.at[span], weights_ref.at[span], many.at[turn])

    for copy in small:
        copy.start()
    for turn in range(turns):
        fetch(turn).start()
    operator[...] = jnp.zeros_like(operator)
    lane = lax.broadcasted_iota(jnp.int32, (tile, tile), 1)
    for copy in small:
        copy.wait()
    live = live_ref[0, 0]
    used = (live + GROUP - 1) // GROUP

    def place(turn, carry):
        fetch(turn).wait()
        ready = []
        for index in range(GROUP):
            kept = turn * GROUP + index
            slot = kept
            first = start_ref[0, kept]
            block = first // tile
            shift = first - block * tile
            rows = pl.ds(pl.multiple_of(goal_ref[0, kept] * tile, tile), tile)
            turned = pltpu.roll(weights_ref[kept].astype(jnp.float32), shift, 1)
            limit = jnp.where(slot < live, shift, tile)
            least = jnp.where(slot < live, 0, tile)
            ready.append((block, rows, jnp.where(lane >= limit, turned, 0.0), turned, shift, least))
        for block, rows, high, turned, shift, least in ready:
            operator[block, rows, :] += high
            operator[block + 1, rows, :] += jnp.where((lane < shift) & (lane >= least), turned, 0.0)
        return carry

    lax.fori_loop(0, used, place, 0)
    picks = lax.broadcasted_iota(jnp.int32, (voxels, voxels), 0) == map_ref[...]
    picks = picks.astype(jnp.float32).T.astype(jnp.bfloat16)
    cells = voxels // 2
    width = cells // LAT_DEV
    for block in range(blocks - 1):
        columns = slice(block * tile, (block + 1) * tile)
        for level, value in enumerate(split(operator[block])):
            moved = jnp.dot(picks, value, preferred_element_type=jnp.float32).astype(jnp.bfloat16)
            for lat in range(LAT_DEV):
                for half in range(2):
                    source = (lat * 2 + half) * width
                    target = level * cells + lat * width
                    out_ref[half, target : target + width, columns] = moved[source : source + width]

    def settle(turn, carry):
        fetch(turn).wait()
        return carry

    lax.fori_loop(used, turns, settle, 0)


def gather_kernel(
    count, operator_ref, echo_ref, psf_ref, rows_ref, gram_ref, near_ref, fine_ref, part, arrived, beams,
    swap_send, swap_recv, own_recv, mate_recv, up_send, down_send, mate_send, side_send, side_recv,
):
    vox, chan, frm = lax.axis_index("vox"), lax.axis_index("chan"), lax.axis_index("frm")
    beside, mate = {"chan": 1 - chan}, {"frm": 1 - frm}
    above, below = {"vox": vox + 1}, {"vox": vox - 1}
    can_up, can_down = vox + 1 < count, vox > 0
    pieces = PIECES
    cells, pair = beams.shape[3], beams.shape[4]
    half = pair // 2
    height = cells // pieces
    depth = cells // LAT_DEV
    barrier = pltpu.get_barrier_semaphore()

    def greet(target):
        pl.semaphore_signal(barrier, inc=1, device_id=target, device_id_type=MESH)

    greet(beside)
    greet(mate)
    for step in range(1, count):
        pl.when(vox + step < count)(functools.partial(greet, {"vox": vox + step}))
        pl.when(vox >= step)(functools.partial(greet, {"vox": vox - step}))

    def sums(side):
        value = jnp.dot(operator_ref[side], echo_ref[...], preferred_element_type=jnp.float32)
        part[side] = value[:cells] + value[cells:]

    def remote(source, target, sent, received, device):
        return pltpu.make_async_remote_copy(
            src_ref=source, dst_ref=target, send_sem=sent, recv_sem=received, device_id=device, device_id_type=MESH
        )

    def rows(unit):
        return pl.ds((unit % pieces) * height, height)

    def side_of(unit):
        return chan if unit < pieces else 1 - chan

    def swap(unit):
        return remote(part.at[1 - chan, rows(unit)], arrived.at[rows(unit)], swap_send.at[0], swap_recv.at[unit], beside)

    def item(block, unit, sent, device):
        place = beams.at[block, frm, side_of(unit), rows(unit)]
        return remote(place, place, sent, own_recv.at[block, unit], device)

    def to_mate(block, unit):
        place = beams.at[block, frm, side_of(unit), rows(unit)]
        return remote(place, place, mate_send.at[block], mate_recv.at[block, side_of(unit)], mate)

    def mated(block, owner, side):
        place = beams.at[block, owner, side]
        return remote(place, place, mate_send.at[block], mate_recv.at[block, side], mate)

    def go_up(step, unit):
        return item(vox, unit, up_send.at[step] if unit < pieces else up_send.at[0], {"vox": vox + step})

    def go_down(step, unit):
        return item(vox, unit, down_send.at[step] if unit < pieces else down_send.at[0], {"vox": vox - step})

    twin_up = can_up & ((vox == 0) | (vox + 2 == count))
    twin_down = can_down & ((vox == count - 1) | (vox == 1))

    def cross(block, unit, side=None):
        place = beams.at[block, frm, chan if side is None else side, rows(unit)]
        return remote(place, place, side_send.at[block], side_recv.at[block, unit], beside)

    def own(unit):
        swap(unit).wait_recv()
        mine = part[chan, rows(unit)] + arrived[rows(unit)]
        beams[vox, frm, chan, rows(unit)] = mine.astype(beams.dtype)
        for step in range(count - 1, 0, -1):
            pl.when(vox + step < count)(lambda: go_up(step, unit).start())
            pl.when(vox >= step)(lambda: go_down(step, unit).start())
        cross(vox, unit).start()
        to_mate(vox, unit).start()

    def own_other(unit):
        cross(vox, unit, 1 - chan).wait_recv()
        pl.when(twin_up)(lambda: go_up(1, pieces + unit).start())
        pl.when(twin_down)(lambda: go_down(1, pieces + unit).start())
        to_mate(vox, pieces + unit).start()

    def relay(step, unit):
        low, high = vox - step, vox + step

        @pl.when(vox >= step)
        def _():
            item(low, unit, up_send.at[0], above).wait_recv()
            if step > 1:
                cross(low, unit).start()
            else:
                pl.when(~twin_down)(lambda: cross(low, unit).start())
            to_mate(low, unit).start()

        @pl.when(vox + step < count)
        def _():
            item(high, unit, down_send.at[0], below).wait_recv()
            if step > 1:
                cross(high, unit).start()
            else:
                pl.when(~twin_up)(lambda: cross(high, unit).start())
            to_mate(high, unit).start()

    def other(step, unit):
        low, high = vox - step, vox + step

        @pl.when(vox >= step)
        def _():
            if step > 1:
                cross(low, unit, 1 - chan).wait_recv()
            else:
                pl.when(twin_down)(item(low, pieces + unit, up_send.at[0], above).wait_recv)
                pl.when(~twin_down)(cross(low, unit, 1 - chan).wait_recv)
            to_mate(low, pieces + unit).start()

        @pl.when(vox + step < count)
        def _():
            if step > 1:
                cross(high, unit, 1 - chan).wait_recv()
            else:
                pl.when(twin_up)(item(high, pieces + unit, down_send.at[0], below).wait_recv)
                pl.when(~twin_up)(cross(high, unit, 1 - chan).wait_recv)
            to_mate(high, pieces + unit).start()

    def from_mate(step, side):
        def settle(block):
            mated(block, 1 - frm, side).wait_recv()

        if step == 0:
            settle(vox)
        else:
            pl.when(vox >= step)(lambda: settle(vox - step))
            pl.when(vox + step < count)(lambda: settle(vox + step))

    def gram(halves, index, first=False):
        left, right = ((0, 0), (0, 1), (1, 1))[index]

        def take(owner):
            return jnp.concatenate([beams[block, owner, side] for block, side in halves], axis=0)

        value = lax.dot_general(
            take(left), take(right), (((0,), (0,)), ((), ())), preferred_element_type=jnp.float32
        )
        if first:
            gram_ref[index] = value
        else:
            gram_ref[index] += value

    def nth(step):
        return jnp.where(2 * vox < count, (vox + step) % count, (vox + count - step) % count)

    tall = LAT_DEV + 4
    slots = near_ref.shape[1] - tall * depth

    def correlation():
        shape = near_ref.shape
        place = lax.broadcasted_iota(jnp.int32, shape, 0)
        source = lax.broadcasted_iota(jnp.int32, shape, 1)
        inside = source < tall * depth
        extra = source - tall * depth
        line = jnp.where(inside, source // depth, extra // 2)
        column = jnp.where(inside, source % depth, extra % 2 + jnp.where(chan == 0, depth, -2))
        down, across = line - place // depth, column - place % depth + 2
        least, most = jnp.where(vox > 0, 0, 2), jnp.where(vox + 1 < count, tall, tall - 2)
        valid = (line >= least) & (line < most) & (across >= 0) & (across < 5)
        key = jnp.where(valid, down * 5 + across, -1)
        value = jnp.zeros(shape, jnp.float32)
        taps = psf_ref[...]
        for shift_a in range(5):
            for shift_b in range(5):
                value = jnp.where(key == shift_a * 5 + shift_b, taps[shift_a : shift_a + 1, shift_b : shift_b + 1], value)
        near_ref[...], fine_ref[...] = split(value)

    def place_rows(start, value):
        total = rows_ref.shape[0] // 2
        size = value.shape[0]
        rows_ref[start : start + size, :] = value[:, :pair]
        rows_ref[total + start : total + start + size, :] = value[:, pair:]

    def collect():
        before, after = jnp.maximum(vox - 1, 0), jnp.minimum(vox + 1, count - 1)
        edge = 2 * depth

        def both(side):
            def lines(block, where):
                parts = [beams[block, owner, side, where] for owner in (0, 1)]
                return jnp.concatenate(
                    [parts[0][:, :half], parts[1][:, :half], parts[0][:, half:], parts[1][:, half:]], axis=1
                )

            return jnp.concatenate(
                [
                    lines(before, slice(cells - edge, cells)),
                    lines(vox, slice(0, cells)),
                    lines(after, slice(0, edge)),
                ],
                axis=0,
            )

        picked = lax.broadcasted_iota(jnp.int32, (slots, tall * depth), 0)
        source = lax.broadcasted_iota(jnp.int32, (slots, tall * depth), 1)
        wanted = (picked // 2) * depth + picked % 2 + jnp.where(chan == 0, 0, depth - 2)
        picks = ((source == wanted) & (picked < 2 * tall)).astype(jnp.float32).astype(jnp.bfloat16)
        extra = jnp.dot(picks, both(1 - chan), preferred_element_type=jnp.float32).astype(jnp.bfloat16)
        place_rows(0, both(chan))
        place_rows(tall * depth, extra)

    def first_stage(index):
        if index == 0:
            from_mate(0, chan)
            from_mate(0, 1 - chan)
        gram([(vox, 0), (vox, 1)], index, True)

    def stage(members):
        for step, far in members:
            from_mate(step, 1 - chan if far else chan)
        if (1, 1) in members:
            collect()
        for index in range(3):
            gram([(nth(step), 1 - chan if far else chan) for step, far in members], index)

    def wave(step, far, unit):
        if step == 0:
            return TWIN[0] + TWIN[1] * unit if far else PACE * unit
        if far and step == 1:
            return SIDE[0] + SIDE[1] * unit
        return PACE * unit + FIRST + HOP * step + (LAG if far else 0)

    def ready(step, far):
        return wave(step, far, pieces - 1)

    events = [(wave(0, 0, pieces - 1), 2, correlation)]
    for unit in range(pieces):
        events += [(wave(0, 0, unit), 0, functools.partial(own, unit))]
        events += [(wave(0, 1, unit), 1, functools.partial(own_other, unit))]
        for step in range(1, count):
            events += [(wave(step, 0, unit), 1, functools.partial(relay, step, unit))]
            events += [(wave(step, 1, unit), 1, functools.partial(other, step, unit))]
    begin = wave(0, 1, pieces - 1) + 1
    events += [(begin, 3, functools.partial(first_stage, index)) for index in range(3)]
    order = [(step, far) for far in (0, 1) for step in range(1, count)]
    latest = begin
    for turn in range(count - 1):
        members = order[2 * turn : 2 * turn + 2]
        latest = max([latest] + [ready(*member) for member in members]) + 1
        events += [(latest, 4, functools.partial(stage, members))]

    sums(1 - chan)
    pl.semaphore_wait(barrier, count + 1)
    for unit in range(pieces):
        swap(unit).start()
    sums(chan)
    for _, _, action in sorted(events, key=lambda event: event[:2]):
        action()

    remote(part.at[1 - chan], arrived, swap_send.at[0], swap_recv.at[0], beside).wait_send()
    twin = beams.at[vox, frm, 1 - chan]
    pl.when(twin_up)(remote(twin, twin, up_send.at[0], own_recv.at[0, 0], above).wait_send)
    pl.when(twin_down)(remote(twin, twin, down_send.at[0], own_recv.at[0, 0], below).wait_send)
    place = beams.at[vox, frm, chan]
    for step in range(1, count):
        up = remote(place, place, up_send.at[step], own_recv.at[0, 0], {"vox": vox + step})
        down = remote(place, place, down_send.at[step], own_recv.at[0, 0], {"vox": vox - step})
        pl.when(vox + step < count)(up.wait_send)
        pl.when(vox >= step)(down.wait_send)
    for block in range(count):
        mated(block, frm, 0).wait_send()
        mated(block, frm, 1).wait_send()
        side = remote(place, place, side_send.at[block], side_recv.at[block, 0], beside)
        by_twin = (twin_down & (vox == block + 1)) | (twin_up & (vox + 1 == block))
        pl.when(~by_twin)(side.wait_send)


def filter_kernel(rows_ref, gram_ref, near_ref, fine_ref, out_ref, real_ref, imag_ref):
    frm = lax.axis_index("frm")
    lat, depth, half = out_ref.shape
    total = rows_ref.shape[0] // 2

    def parts(index):
        block = gram_ref[index]
        return block[:half, :half] + block[half:, half:], block[:half, half:] - block[half:, :half]

    grams = {(0, 0): parts(0), (0, 1): parts(1), (1, 1): parts(2)}
    grams[1, 0] = (grams[0, 1][0].T, -grams[0, 1][1].T)
    eye = lax.broadcasted_iota(jnp.int32, (half, half), 0) == lax.broadcasted_iota(jnp.int32, (half, half), 1)
    diagonal = []
    for (row, column), (real, imag) in grams.items():
        if row == column:
            diagonal.append(jnp.sum(jnp.where(eye, real, 0.0), axis=0, keepdims=True))
            real = jnp.where(eye, 0.0, real)
        place = (slice(row * half, (row + 1) * half), slice(column * half, (column + 1) * half))
        real_ref[place] = real.astype(jnp.bfloat16)
        imag_ref[place] = imag.astype(jnp.bfloat16)
    trace = jnp.sum(diagonal[0] + diagonal[1], axis=1, keepdims=True)
    factor = (2 * half) / trace
    weight = jnp.concatenate(diagonal, axis=1)

    def mine(value):
        return jnp.where(frm == 0, value[:, :half], value[:, half:])

    def times(value, columns):
        value = value.astype(jnp.bfloat16)
        by_real = jnp.dot(value, real_ref[:, columns], preferred_element_type=jnp.float32)
        by_imag = jnp.dot(value, imag_ref[:, columns], preferred_element_type=jnp.float32)
        return jnp.concatenate([by_real[:total] - by_imag[total:], by_imag[:total] + by_real[total:]], axis=0)

    rows = rows_ref[...]
    echo = rows.astype(jnp.float32)
    every = slice(0, 2 * half)
    once = factor * (times(rows, every) + weight * echo)
    twice = factor * (times(once, every) + weight * once)
    mixed = POLY_COEFFS[2] * once + POLY_COEFFS[3] * twice
    own = pl.ds(pl.multiple_of(frm * half, half), half)
    term = factor * (times(mixed, own) + mine(weight) * mine(mixed))
    term += POLY_COEFFS[0] * mine(echo) + POLY_COEFFS[1] * mine(once)
    real, imag = term[:total], term[total:]
    high, low = split(jnp.sqrt(real * real + imag * imag + 1e-06))
    result = jnp.dot(near_ref[...], high, preferred_element_type=jnp.float32)
    result += jnp.dot(near_ref[...], low, preferred_element_type=jnp.float32)
    result += jnp.dot(fine_ref[...], high, preferred_element_type=jnp.float32)
    out_ref[...] = result.reshape(lat, depth, half)


def kernel_shards(count, echo_data, tile_weights, tile_target, tile_offset, tile_count, grid_map, psf_kernel):
    rows, half = echo_data.shape[2], echo_data.shape[4]
    slots, tile = tile_weights.shape[2], tile_weights.shape[4]
    voxels = grid_map.shape[1]
    cells, pair = voxels // 2, 2 * half
    depth = cells // LAT_DEV
    tall = LAT_DEV + 4
    total = tall * depth + -(-2 * tall // 16) * 16
    vmem = pl.BlockSpec(memory_space=pltpu.VMEM)
    operator = pl.pallas_call(
        beam_kernel,
        name="beam",
        out_shape=jax.ShapeDtypeStruct((2, voxels, rows), jnp.bfloat16),
        in_specs=[pl.BlockSpec(memory_space=pltpu.HBM)] * 5,
        out_specs=vmem,
        scratch_shapes=[
            pltpu.VMEM((rows // tile + 1, voxels, tile), jnp.float32),
            pltpu.SMEM((1, slots), jnp.int32),
            pltpu.SMEM((1, slots), jnp.int32),
            pltpu.SMEM((1, 1), jnp.int32),
            pltpu.VMEM((slots, tile, tile), jnp.bfloat16),
            pltpu.VMEM((1, voxels), jnp.int32),
            pltpu.SemaphoreType.DMA((4,)),
            pltpu.SemaphoreType.DMA((slots // GROUP,)),
        ],
        compiler_params=pltpu.CompilerParams(vmem_limit_bytes=8 << 20),
    )(
        *[
            pltpu.with_memory_space_constraint(value, pltpu.HBM) if value.size > 1 else value
            for value in (
                tile_target.reshape(1, slots),
                tile_offset.reshape(1, slots),
                tile_count,
                tile_weights.reshape(slots, tile, tile),
                grid_map,
            )
        ]
    )
    dma = pltpu.SemaphoreType.DMA
    gathered = pl.pallas_call(
        functools.partial(gather_kernel, count),
        name="gather",
        out_shape=[
            jax.ShapeDtypeStruct((2 * total, pair), jnp.bfloat16),
            jax.ShapeDtypeStruct((3, pair, pair), jnp.float32),
            jax.ShapeDtypeStruct((cells, total), jnp.bfloat16),
            jax.ShapeDtypeStruct((cells, total), jnp.bfloat16),
        ],
        in_specs=[vmem] * 3,
        out_specs=[vmem] * 4,
        scratch_shapes=[
            pltpu.VMEM((2, cells, pair), jnp.float32),
            pltpu.VMEM((cells, pair), jnp.float32),
            pltpu.VMEM((count, 2, 2, cells, pair), jnp.bfloat16),
            dma((1,)),
            dma((PIECES,)),
            dma((count, 2 * PIECES)),
            dma((count, 2)),
        ]
        + [dma((count,))] * 4
        + [dma((count, PIECES))],
        compiler_params=pltpu.CompilerParams(collective_id=0, has_side_effects=True, vmem_limit_bytes=16 << 20),
    )(operator, echo_data.reshape(rows, pair), psf_kernel)
    return pl.pallas_call(
        filter_kernel,
        name="filter",
        out_shape=jax.ShapeDtypeStruct((LAT_DEV, depth, half), jnp.float32),
        in_specs=[vmem] * 4,
        out_specs=vmem,
        scratch_shapes=[pltpu.VMEM((pair, pair), jnp.bfloat16)] * 2,
        compiler_params=pltpu.CompilerParams(vmem_limit_bytes=16 << 20),
    )(*gathered)


def solution(mesh):
    in_specs = (
        P(("groups", "vox"), "chan", None, None, "frm"),
        P("vox", "chan", None, None, None),
        P("vox", "chan", None),
        P("vox", "chan", None),
        P("vox", "chan"),
        P("vox", None),
        P(),
    )
    out_specs = P(("groups", "vox"), "chan", "frm")
    body = shards
    if mesh.shape["chan"] == 2 and mesh.shape["frm"] == 2:
        body = functools.partial(kernel_shards, mesh.shape["vox"])
    return jax.shard_map(body, mesh=mesh, in_specs=in_specs, out_specs=out_specs, check_vma=False)
```

```python
import functools

import jax
import jax.numpy as jnp
from jax import lax
from jax.experimental import pallas as pl
from jax.experimental.pallas import tpu as pltpu
from jax.sharding import PartitionSpec as P

MESH = pl.DeviceIdType.MESH
PIECES = 4
HOP = 1
PACE = 2
LAG = 5
TWIN = (7, 1)
SIDE = (13.1, 1)
FIRST = 3
GROUP = 8

TBATCH = 8
LAT_DEV = 8


POLY_COEFFS = (1.0, -0.6, 0.15, -0.03)


def with_halo(shard, sides, width):
    for axis, dim in sides:
        devices, length = (lax.axis_size(axis), shard.shape[dim])
        up = [(i, (i + 1) % devices) for i in range(devices - 1)]
        down = [(j, i) for i, j in up]
        last = lax.slice_in_dim(shard, length - width, length, axis=dim)
        leading = lax.slice_in_dim(shard, 0, width, axis=dim)
        before = lax.ppermute(last, axis, up)
        after = lax.ppermute(leading, axis, down)
        shard = jnp.concatenate([before, shard, after], axis=dim)
    return shard


def complex_times(left_real, left_imag, right_real, right_imag):
    level = lax.Precision.HIGH
    real_part = jnp.dot(
        left_real, right_real, precision=level, preferred_element_type=jnp.float32
    ) - jnp.dot(left_imag, right_imag, precision=level, preferred_element_type=jnp.float32)
    imag_part = jnp.dot(
        left_real, right_imag, precision=level, preferred_element_type=jnp.float32
    ) + jnp.dot(left_imag, right_real, precision=level, preferred_element_type=jnp.float32)
    return (real_part, imag_part)


def tile_pass(flat_echo, weights, tile_goal, tile_start, live_total, tiles_out):
    tile_size = weights.shape[-1]
    col_count = flat_echo.shape[-1]
    slot_count = weights.shape[0]
    lane_ids = jnp.arange(TBATCH, dtype=jnp.int32)
    target_ids = jnp.arange(tiles_out, dtype=jnp.int32)
    zero_index = jnp.zeros((), jnp.int32)

    def cut_rows(offset_id):
        return lax.dynamic_slice(flat_echo, (offset_id, zero_index), (tile_size, col_count))

    def one_turn(turn_index, totals):
        where_at = turn_index * TBATCH + lane_ids
        live_lane = where_at < live_total
        chosen = jnp.minimum(where_at, slot_count - 1)
        picked = weights[chosen]
        samples = jax.vmap(cut_rows)(tile_start[chosen])
        product = jnp.einsum("krs,ksc->krc", picked, samples, preferred_element_type=jnp.float32)
        placing = ((tile_goal[chosen][:, None] == target_ids[None, :]) & live_lane[:, None]).astype(
            jnp.float32
        )
        return totals + jnp.einsum(
            "kt,krc->trc", placing, product, precision=lax.Precision.HIGHEST
        )

    start_totals = jnp.zeros((tiles_out, tile_size, col_count), jnp.float32)
    turn_count = (live_total + TBATCH - 1) // TBATCH
    return lax.fori_loop(0, turn_count, one_turn, start_totals)


def shards(echo_data, tile_weights, tile_target, tile_offset, tile_count, grid_map, psf_kernel):
    row_count = echo_data.shape[2]
    half_frames = echo_data.shape[4]
    tile_size = tile_weights.shape[-1]
    slot_count = tile_weights.shape[2]
    voxels = grid_map.shape[1]
    tiles_out = voxels // tile_size
    flat_echo = echo_data.reshape(row_count, 2 * half_frames)
    weights = tile_weights.reshape(slot_count, tile_size, tile_size)
    tile_sums = tile_pass(
        flat_echo,
        weights,
        tile_target.reshape(-1),
        tile_offset.reshape(-1),
        tile_count[0, 0],
        tiles_out,
    )
    arranged = jnp.take(tile_sums.reshape(voxels, 2, half_frames), grid_map[0], axis=0)
    arranged = arranged.reshape(LAT_DEV, voxels // LAT_DEV, 2, half_frames)
    beamformed = lax.psum_scatter(arranged, "chan", scatter_dimension=1, tiled=True).astype(
        jnp.bfloat16
    )
    lat_count = beamformed.shape[0]
    depth_count = beamformed.shape[1]
    cell_count = lat_count * depth_count
    own_frames = beamformed.reshape(cell_count, 2, half_frames)
    all_frames = lax.all_gather(own_frames, "frm", axis=2, tiled=True)
    frames = all_frames.shape[2]
    own_flat = own_frames.reshape(cell_count, 2 * half_frames)
    all_flat = all_frames.reshape(cell_count, 2 * frames)
    gram_block = lax.dot_general(
        own_flat, all_flat, (((0,), (0,)), ((), ())), preferred_element_type=jnp.float32
    )
    gram_real = gram_block[:half_frames, :frames] + gram_block[half_frames:, frames:]
    gram_imag = gram_block[:half_frames, frames:] - gram_block[half_frames:, :frames]
    frame_start = lax.axis_index("frm") * half_frames
    echo_real = all_frames[:, 0, :].astype(jnp.float32)
    echo_imag = all_frames[:, 1, :].astype(jnp.float32)
    energy = jnp.sum(echo_real * echo_real + echo_imag * echo_imag)
    gram_real, gram_imag, trace_value = lax.psum((gram_real, gram_imag, energy), ("vox", "chan"))
    factor = frames / trace_value
    norm_real = factor * gram_real
    norm_imag = factor * gram_imag
    full_real, full_imag = (
        lax.all_gather(norm_real, "frm", axis=0, tiled=True),
        lax.all_gather(norm_imag, "frm", axis=0, tiled=True),
    )
    identity = jnp.eye(frames, dtype=jnp.float32)
    poly_real = POLY_COEFFS[3] * full_real + POLY_COEFFS[2] * identity
    poly_imag = POLY_COEFFS[3] * full_imag
    poly_real, poly_imag = complex_times(poly_real, poly_imag, full_real, full_imag)
    poly_real = poly_real + POLY_COEFFS[1] * identity
    cols_real = lax.dynamic_slice_in_dim(full_real, frame_start, half_frames, 1)
    cols_imag = lax.dynamic_slice_in_dim(full_imag, frame_start, half_frames, 1)
    filter_real, filter_imag = complex_times(poly_real, poly_imag, cols_real, cols_imag)
    filter_real = filter_real + POLY_COEFFS[0] * lax.dynamic_slice_in_dim(
        identity, frame_start, half_frames, 1
    )
    out_real, out_imag = complex_times(echo_real, echo_imag, filter_real, filter_imag)
    envelope = jnp.sqrt(out_real * out_real + out_imag * out_imag + 1e-06)
    envelope = envelope.reshape(lat_count, depth_count, half_frames)
    padded = with_halo(envelope, (("vox", 0), ("chan", 1)), 2)
    psf_image = jnp.zeros_like(envelope)
    for shift_a in range(5):
        for shift_b in range(5):
            psf_image = (
                psf_image
                + psf_kernel[shift_a, shift_b]
                * padded[shift_a : shift_a + lat_count, shift_b : shift_b + depth_count]
            )
    return psf_image


def split(value):
    high = value.astype(jnp.bfloat16)
    return high, (value - high.astype(jnp.float32)).astype(jnp.bfloat16)


def beam_kernel(
    goal_hbm, start_hbm, live_hbm, weights_hbm, map_hbm, out_ref, operator, goal_ref, start_ref, live_ref, weights_ref, map_ref, few, many
):
    blocks, voxels, tile = operator.shape
    slots = weights_ref.shape[0]
    turns = slots // GROUP
    small = [
        pltpu.make_async_copy(source, target, few.at[index])
        for index, (source, target) in enumerate(
            ((live_hbm, live_ref), (start_hbm, start_ref), (goal_hbm, goal_ref), (map_hbm, map_ref))
        )
    ]

    def fetch(turn):
        span = pl.ds(turn * GROUP, GROUP)
        return pltpu.make_async_copy(weights_hbm.at[span], weights_ref.at[span], many.at[turn])

    for copy in small:
        copy.start()
    for turn in range(turns):
        fetch(turn).start()
    operator[...] = jnp.zeros_like(operator)
    lane = lax.broadcasted_iota(jnp.int32, (tile, tile), 1)
    for copy in small:
        copy.wait()
    live = live_ref[0, 0]
    used = (live + GROUP - 1) // GROUP

    def place(turn, carry):
        fetch(turn).wait()
        ready = []
        for index in range(GROUP):
            kept = turn * GROUP + index
            slot = kept
            first = start_ref[0, kept]
            block = first // tile
            shift = first - block * tile
            rows = pl.ds(pl.multiple_of(goal_ref[0, kept] * tile, tile), tile)
            turned = pltpu.roll(weights_ref[kept].astype(jnp.float32), shift, 1)
            limit = jnp.where(slot < live, shift, tile)
            least = jnp.where(slot < live, 0, tile)
            ready.append((block, rows, jnp.where(lane >= limit, turned, 0.0), turned, shift, least))
        for block, rows, high, turned, shift, least in ready:
            operator[block, rows, :] += high
            operator[block + 1, rows, :] += jnp.where((lane < shift) & (lane >= least), turned, 0.0)
        return carry

    lax.fori_loop(0, used, place, 0)
    picks = lax.broadcasted_iota(jnp.int32, (voxels, voxels), 0) == map_ref[...]
    picks = picks.astype(jnp.float32).T.astype(jnp.bfloat16)
    cells = voxels // 2
    width = cells // LAT_DEV
    for block in range(blocks - 1):
        columns = slice(block * tile, (block + 1) * tile)
        both = jnp.concatenate(split(operator[block]), axis=1)
        moved = jnp.dot(picks, both, preferred_element_type=jnp.float32).astype(jnp.bfloat16)
        for lat in range(LAT_DEV):
            for half in range(2):
                source = (lat * 2 + half) * width
                for level in range(2):
                    target = level * cells + lat * width
                    side = slice(level * tile, (level + 1) * tile)
                    out_ref[half, target : target + width, columns] = moved[source : source + width, side]

    def settle(turn, carry):
        fetch(turn).wait()
        return carry

    lax.fori_loop(used, turns, settle, 0)


def gather_kernel(
    count, operator_ref, echo_ref, psf_ref, rows_ref, gram_ref, near_ref, fine_ref, part, arrived, beams,
    swap_send, swap_recv, own_recv, mate_recv, up_send, down_send, mate_send, side_send, side_recv,
):
    vox, chan, frm = lax.axis_index("vox"), lax.axis_index("chan"), lax.axis_index("frm")
    beside, mate = {"chan": 1 - chan}, {"frm": 1 - frm}
    above, below = {"vox": vox + 1}, {"vox": vox - 1}
    can_up, can_down = vox + 1 < count, vox > 0
    pieces = PIECES
    cells, pair = beams.shape[3], beams.shape[4]
    half = pair // 2
    height = cells // pieces
    depth = cells // LAT_DEV
    barrier = pltpu.get_barrier_semaphore()

    def greet(target):
        pl.semaphore_signal(barrier, inc=1, device_id=target, device_id_type=MESH)

    greet(beside)
    greet(mate)
    for step in range(1, count):
        pl.when(vox + step < count)(functools.partial(greet, {"vox": vox + step}))
        pl.when(vox >= step)(functools.partial(greet, {"vox": vox - step}))

    def sums(side):
        value = jnp.dot(operator_ref[side], echo_ref[...], preferred_element_type=jnp.float32)
        part[side] = value[:cells] + value[cells:]

    def remote(source, target, sent, received, device):
        return pltpu.make_async_remote_copy(
            src_ref=source, dst_ref=target, send_sem=sent, recv_sem=received, device_id=device, device_id_type=MESH
        )

    def rows(unit):
        return pl.ds((unit % pieces) * height, height)

    def side_of(unit):
        return chan if unit < pieces else 1 - chan

    def swap(unit):
        return remote(part.at[1 - chan, rows(unit)], arrived.at[rows(unit)], swap_send.at[0], swap_recv.at[unit], beside)

    def item(block, unit, sent, device):
        place = beams.at[block, frm, side_of(unit), rows(unit)]
        return remote(place, place, sent, own_recv.at[block, unit], device)

    def to_mate(block, unit):
        place = beams.at[block, frm, side_of(unit), rows(unit)]
        return remote(place, place, mate_send.at[block], mate_recv.at[block, side_of(unit)], mate)

    def mated(block, owner, side):
        place = beams.at[block, owner, side]
        return remote(place, place, mate_send.at[block], mate_recv.at[block, side], mate)

    def go_up(step, unit):
        return item(vox, unit, up_send.at[step] if unit < pieces else up_send.at[0], {"vox": vox + step})

    def go_down(step, unit):
        return item(vox, unit, down_send.at[step] if unit < pieces else down_send.at[0], {"vox": vox - step})

    twin_up = can_up & ((vox == 0) | (vox + 2 == count))
    twin_down = can_down & ((vox == count - 1) | (vox == 1))

    def cross(block, unit, side=None):
        place = beams.at[block, frm, chan if side is None else side, rows(unit)]
        return remote(place, place, side_send.at[block], side_recv.at[block, unit], beside)

    def own(unit):
        swap(unit).wait_recv()
        mine = part[chan, rows(unit)] + arrived[rows(unit)]
        beams[vox, frm, chan, rows(unit)] = mine.astype(beams.dtype)
        for step in range(count - 1, 0, -1):
            pl.when(vox + step < count)(lambda: go_up(step, unit).start())
            pl.when(vox >= step)(lambda: go_down(step, unit).start())
        cross(vox, unit).start()
        to_mate(vox, unit).start()

    def own_other(unit):
        cross(vox, unit, 1 - chan).wait_recv()
        pl.when(twin_up)(lambda: go_up(1, pieces + unit).start())
        pl.when(twin_down)(lambda: go_down(1, pieces + unit).start())
        to_mate(vox, pieces + unit).start()

    def relay(step, unit):
        low, high = vox - step, vox + step

        @pl.when(vox >= step)
        def _():
            item(low, unit, up_send.at[0], above).wait_recv()
            if step > 1:
                cross(low, unit).start()
            else:
                pl.when(~twin_down)(lambda: cross(low, unit).start())
            to_mate(low, unit).start()

        @pl.when(vox + step < count)
        def _():
            item(high, unit, down_send.at[0], below).wait_recv()
            if step > 1:
                cross(high, unit).start()
            else:
                pl.when(~twin_up)(lambda: cross(high, unit).start())
            to_mate(high, unit).start()

    def other(step, unit):
        low, high = vox - step, vox + step

        @pl.when(vox >= step)
        def _():
            if step > 1:
                cross(low, unit, 1 - chan).wait_recv()
            else:
                pl.when(twin_down)(item(low, pieces + unit, up_send.at[0], above).wait_recv)
                pl.when(~twin_down)(cross(low, unit, 1 - chan).wait_recv)
            to_mate(low, pieces + unit).start()

        @pl.when(vox + step < count)
        def _():
            if step > 1:
                cross(high, unit, 1 - chan).wait_recv()
            else:
                pl.when(twin_up)(item(high, pieces + unit, down_send.at[0], below).wait_recv)
                pl.when(~twin_up)(cross(high, unit, 1 - chan).wait_recv)
            to_mate(high, pieces + unit).start()

    def from_mate(step, side):
        def settle(block):
            mated(block, 1 - frm, side).wait_recv()

        if step == 0:
            settle(vox)
        else:
            pl.when(vox >= step)(lambda: settle(vox - step))
            pl.when(vox + step < count)(lambda: settle(vox + step))

    def gram(halves, index, first=False):
        left, right = ((0, 0), (0, 1), (1, 1))[index]

        def take(owner):
            return jnp.concatenate([beams[block, owner, side] for block, side in halves], axis=0)

        value = lax.dot_general(
            take(left), take(right), (((0,), (0,)), ((), ())), preferred_element_type=jnp.float32
        )
        if first:
            gram_ref[index] = value
        else:
            gram_ref[index] += value

    def nth(step):
        return jnp.where(2 * vox < count, (vox + step) % count, (vox + count - step) % count)

    tall = LAT_DEV + 4
    slots = near_ref.shape[1] - tall * depth

    def correlation():
        shape = near_ref.shape
        place = lax.broadcasted_iota(jnp.int32, shape, 0)
        source = lax.broadcasted_iota(jnp.int32, shape, 1)
        inside = source < tall * depth
        extra = source - tall * depth
        line = jnp.where(inside, source // depth, extra // 2)
        column = jnp.where(inside, source % depth, extra % 2 + jnp.where(chan == 0, depth, -2))
        down, across = line - place // depth, column - place % depth + 2
        least, most = jnp.where(vox > 0, 0, 2), jnp.where(vox + 1 < count, tall, tall - 2)
        valid = (line >= least) & (line < most) & (across >= 0) & (across < 5)
        key = jnp.where(valid, down * 5 + across, -1)
        value = jnp.zeros(shape, jnp.float32)
        taps = psf_ref[...]
        for shift_a in range(5):
            for shift_b in range(5):
                value = jnp.where(key == shift_a * 5 + shift_b, taps[shift_a : shift_a + 1, shift_b : shift_b + 1], value)
        near_ref[...], fine_ref[...] = split(value)

    def place_rows(start, value):
        total = rows_ref.shape[0] // 2
        size = value.shape[0]
        rows_ref[start : start + size, :] = value[:, :pair]
        rows_ref[total + start : total + start + size, :] = value[:, pair:]

    def collect():
        before, after = jnp.maximum(vox - 1, 0), jnp.minimum(vox + 1, count - 1)
        edge = 2 * depth

        def both(side):
            def lines(block, where):
                parts = [beams[block, owner, side, where] for owner in (0, 1)]
                return jnp.concatenate(
                    [parts[0][:, :half], parts[1][:, :half], parts[0][:, half:], parts[1][:, half:]], axis=1
                )

            return jnp.concatenate(
                [
                    lines(before, slice(cells - edge, cells)),
                    lines(vox, slice(0, cells)),
                    lines(after, slice(0, edge)),
                ],
                axis=0,
            )

        picked = lax.broadcasted_iota(jnp.int32, (slots, tall * depth), 0)
        source = lax.broadcasted_iota(jnp.int32, (slots, tall * depth), 1)
        wanted = (picked // 2) * depth + picked % 2 + jnp.where(chan == 0, 0, depth - 2)
        picks = ((source == wanted) & (picked < 2 * tall)).astype(jnp.float32).astype(jnp.bfloat16)
        extra = jnp.dot(picks, both(1 - chan), preferred_element_type=jnp.float32).astype(jnp.bfloat16)
        place_rows(0, both(chan))
        place_rows(tall * depth, extra)

    def first_stage(index):
        if index == 0:
            from_mate(0, chan)
            from_mate(0, 1 - chan)
        gram([(vox, 0), (vox, 1)], index, True)

    def stage(members):
        for step, far in members:
            from_mate(step, 1 - chan if far else chan)
        if (1, 1) in members:
            collect()
        for index in range(3):
            gram([(nth(step), 1 - chan if far else chan) for step, far in members], index)

    def wave(step, far, unit):
        if step == 0:
            return TWIN[0] + TWIN[1] * unit if far else PACE * unit
        if far and step == 1:
            return SIDE[0] + SIDE[1] * unit
        return PACE * unit + FIRST + HOP * step + (LAG if far else 0)

    def ready(step, far):
        return wave(step, far, pieces - 1)

    events = [(wave(0, 0, pieces - 1), 2, correlation)]
    for unit in range(pieces):
        events += [(wave(0, 0, unit), 0, functools.partial(own, unit))]
        events += [(wave(0, 1, unit), 1, functools.partial(own_other, unit))]
        for step in range(1, count):
            events += [(wave(step, 0, unit), 1, functools.partial(relay, step, unit))]
            events += [(wave(step, 1, unit), 1, functools.partial(other, step, unit))]
    begin = wave(0, 1, pieces - 1) + 1
    events += [(begin, 3, functools.partial(first_stage, index)) for index in range(3)]
    order = [(step, far) for far in (0, 1) for step in range(1, count)]
    latest = begin
    for turn in range(count - 1):
        members = order[2 * turn : 2 * turn + 2]
        latest = max([latest] + [ready(*member) for member in members]) + 1
        events += [(latest, 4, functools.partial(stage, members))]

    sums(1 - chan)
    pl.semaphore_wait(barrier, count + 1)
    for unit in range(pieces):
        swap(unit).start()
    sums(chan)
    for _, _, action in sorted(events, key=lambda event: event[:2]):
        action()

    remote(part.at[1 - chan], arrived, swap_send.at[0], swap_recv.at[0], beside).wait_send()
    twin = beams.at[vox, frm, 1 - chan]
    pl.when(twin_up)(remote(twin, twin, up_send.at[0], own_recv.at[0, 0], above).wait_send)
    pl.when(twin_down)(remote(twin, twin, down_send.at[0], own_recv.at[0, 0], below).wait_send)
    place = beams.at[vox, frm, chan]
    for step in range(1, count):
        up = remote(place, place, up_send.at[step], own_recv.at[0, 0], {"vox": vox + step})
        down = remote(place, place, down_send.at[step], own_recv.at[0, 0], {"vox": vox - step})
        pl.when(vox + step < count)(up.wait_send)
        pl.when(vox >= step)(down.wait_send)
    for block in range(count):
        mated(block, frm, 0).wait_send()
        mated(block, frm, 1).wait_send()
        side = remote(place, place, side_send.at[block], side_recv.at[block, 0], beside)
        by_twin = (twin_down & (vox == block + 1)) | (twin_up & (vox + 1 == block))
        pl.when(~by_twin)(side.wait_send)


def filter_kernel(rows_ref, gram_ref, near_ref, fine_ref, out_ref, real_ref, imag_ref):
    frm = lax.axis_index("frm")
    lat, depth, half = out_ref.shape
    total = rows_ref.shape[0] // 2

    def parts(index):
        block = gram_ref[index]
        return block[:half, :half] + block[half:, half:], block[:half, half:] - block[half:, :half]

    grams = {(0, 0): parts(0), (0, 1): parts(1), (1, 1): parts(2)}
    grams[1, 0] = (grams[0, 1][0].T, -grams[0, 1][1].T)
    eye = lax.broadcasted_iota(jnp.int32, (half, half), 0) == lax.broadcasted_iota(jnp.int32, (half, half), 1)
    diagonal = []
    for (row, column), (real, imag) in grams.items():
        if row == column:
            diagonal.append(jnp.sum(jnp.where(eye, real, 0.0), axis=0, keepdims=True))
            real = jnp.where(eye, 0.0, real)
        place = (slice(row * half, (row + 1) * half), slice(column * half, (column + 1) * half))
        real_ref[place] = real.astype(jnp.bfloat16)
        imag_ref[place] = imag.astype(jnp.bfloat16)
    trace = jnp.sum(diagonal[0] + diagonal[1], axis=1, keepdims=True)
    factor = (2 * half) / trace
    weight = jnp.concatenate(diagonal, axis=1)

    def mine(value):
        return jnp.where(frm == 0, value[:, :half], value[:, half:])

    def times(value, columns):
        value = value.astype(jnp.bfloat16)
        by_real = jnp.dot(value, real_ref[:, columns], preferred_element_type=jnp.float32)
        by_imag = jnp.dot(value, imag_ref[:, columns], preferred_element_type=jnp.float32)
        return jnp.concatenate([by_real[:total] - by_imag[total:], by_imag[:total] + by_real[total:]], axis=0)

    rows = rows_ref[...]
    echo = rows.astype(jnp.float32)
    every = slice(0, 2 * half)
    once = factor * (times(rows, every) + weight * echo)
    twice = factor * (times(once, every) + weight * once)
    mixed = POLY_COEFFS[2] * once + POLY_COEFFS[3] * twice
    own = pl.ds(pl.multiple_of(frm * half, half), half)
    term = factor * (times(mixed, own) + mine(weight) * mine(mixed))
    term += POLY_COEFFS[0] * mine(echo) + POLY_COEFFS[1] * mine(once)
    real, imag = term[:total], term[total:]
    high, low = split(jnp.sqrt(real * real + imag * imag + 1e-06))
    result = jnp.dot(near_ref[...], high, preferred_element_type=jnp.float32)
    result += jnp.dot(near_ref[...], low, preferred_element_type=jnp.float32)
    result += jnp.dot(fine_ref[...], high, preferred_element_type=jnp.float32)
    out_ref[...] = result.reshape(lat, depth, half)


def kernel_shards(count, echo_data, tile_weights, tile_target, tile_offset, tile_count, grid_map, psf_kernel):
    rows, half = echo_data.shape[2], echo_data.shape[4]
    slots, tile = tile_weights.shape[2], tile_weights.shape[4]
    voxels = grid_map.shape[1]
    cells, pair = voxels // 2, 2 * half
    depth = cells // LAT_DEV
    tall = LAT_DEV + 4
    total = tall * depth + -(-2 * tall // 16) * 16
    vmem = pl.BlockSpec(memory_space=pltpu.VMEM)
    operator = pl.pallas_call(
        beam_kernel,
        name="beam",
        out_shape=jax.ShapeDtypeStruct((2, voxels, rows), jnp.bfloat16),
        in_specs=[pl.BlockSpec(memory_space=pltpu.HBM)] * 5,
        out_specs=vmem,
        scratch_shapes=[
            pltpu.VMEM((rows // tile + 1, voxels, tile), jnp.float32),
            pltpu.SMEM((1, slots), jnp.int32),
            pltpu.SMEM((1, slots), jnp.int32),
            pltpu.SMEM((1, 1), jnp.int32),
            pltpu.VMEM((slots, tile, tile), jnp.bfloat16),
            pltpu.VMEM((1, voxels), jnp.int32),
            pltpu.SemaphoreType.DMA((4,)),
            pltpu.SemaphoreType.DMA((slots // GROUP,)),
        ],
        compiler_params=pltpu.CompilerParams(vmem_limit_bytes=8 << 20),
    )(
        *[
            pltpu.with_memory_space_constraint(value, pltpu.HBM) if value.size > 1 else value
            for value in (
                tile_target.reshape(1, slots),
                tile_offset.reshape(1, slots),
                tile_count,
                tile_weights.reshape(slots, tile, tile),
                grid_map,
            )
        ]
    )
    dma = pltpu.SemaphoreType.DMA
    gathered = pl.pallas_call(
        functools.partial(gather_kernel, count),
        name="gather",
        out_shape=[
            jax.ShapeDtypeStruct((2 * total, pair), jnp.bfloat16),
            jax.ShapeDtypeStruct((3, pair, pair), jnp.float32),
            jax.ShapeDtypeStruct((cells, total), jnp.bfloat16),
            jax.ShapeDtypeStruct((cells, total), jnp.bfloat16),
        ],
        in_specs=[vmem] * 3,
        out_specs=[vmem] * 4,
        scratch_shapes=[
            pltpu.VMEM((2, cells, pair), jnp.float32),
            pltpu.VMEM((cells, pair), jnp.float32),
            pltpu.VMEM((count, 2, 2, cells, pair), jnp.bfloat16),
            dma((1,)),
            dma((PIECES,)),
            dma((count, 2 * PIECES)),
            dma((count, 2)),
        ]
        + [dma((count,))] * 4
        + [dma((count, PIECES))],
        compiler_params=pltpu.CompilerParams(collective_id=0, has_side_effects=True, vmem_limit_bytes=16 << 20),
    )(operator, echo_data.reshape(rows, pair), psf_kernel)
    return pl.pallas_call(
        filter_kernel,
        name="filter",
        out_shape=jax.ShapeDtypeStruct((LAT_DEV, depth, half), jnp.float32),
        in_specs=[vmem] * 4,
        out_specs=vmem,
        scratch_shapes=[pltpu.VMEM((pair, pair), jnp.bfloat16)] * 2,
        compiler_params=pltpu.CompilerParams(vmem_limit_bytes=16 << 20),
    )(*gathered)


def solution(mesh):
    in_specs = (
        P(("groups", "vox"), "chan", None, None, "frm"),
        P("vox", "chan", None, None, None),
        P("vox", "chan", None),
        P("vox", "chan", None),
        P("vox", "chan"),
        P("vox", None),
        P(),
    )
    out_specs = P(("groups", "vox"), "chan", "frm")
    body = shards
    if mesh.shape["chan"] == 2 and mesh.shape["frm"] == 2:
        body = functools.partial(kernel_shards, mesh.shape["vox"])
    return jax.shard_map(body, mesh=mesh, in_specs=in_specs, out_specs=out_specs, check_vma=False)
```

```python
import functools

import jax
import jax.numpy as jnp
from jax import lax
from jax.experimental import pallas as pl
from jax.experimental.pallas import tpu as pltpu
from jax.sharding import PartitionSpec as P

MESH = pl.DeviceIdType.MESH
PIECES = 4
HOP = 1
PACE = 2
LAG = 5
TWIN = (7, 1)
SIDE = (13.1, 1)
FIRST = 3
GROUP = 16

TBATCH = 8
LAT_DEV = 8


POLY_COEFFS = (1.0, -0.6, 0.15, -0.03)


def with_halo(shard, sides, width):
    for axis, dim in sides:
        devices, length = (lax.axis_size(axis), shard.shape[dim])
        up = [(i, (i + 1) % devices) for i in range(devices - 1)]
        down = [(j, i) for i, j in up]
        last = lax.slice_in_dim(shard, length - width, length, axis=dim)
        leading = lax.slice_in_dim(shard, 0, width, axis=dim)
        before = lax.ppermute(last, axis, up)
        after = lax.ppermute(leading, axis, down)
        shard = jnp.concatenate([before, shard, after], axis=dim)
    return shard


def complex_times(left_real, left_imag, right_real, right_imag):
    level = lax.Precision.HIGH
    real_part = jnp.dot(
        left_real, right_real, precision=level, preferred_element_type=jnp.float32
    ) - jnp.dot(left_imag, right_imag, precision=level, preferred_element_type=jnp.float32)
    imag_part = jnp.dot(
        left_real, right_imag, precision=level, preferred_element_type=jnp.float32
    ) + jnp.dot(left_imag, right_real, precision=level, preferred_element_type=jnp.float32)
    return (real_part, imag_part)


def tile_pass(flat_echo, weights, tile_goal, tile_start, live_total, tiles_out):
    tile_size = weights.shape[-1]
    col_count = flat_echo.shape[-1]
    slot_count = weights.shape[0]
    lane_ids = jnp.arange(TBATCH, dtype=jnp.int32)
    target_ids = jnp.arange(tiles_out, dtype=jnp.int32)
    zero_index = jnp.zeros((), jnp.int32)

    def cut_rows(offset_id):
        return lax.dynamic_slice(flat_echo, (offset_id, zero_index), (tile_size, col_count))

    def one_turn(turn_index, totals):
        where_at = turn_index * TBATCH + lane_ids
        live_lane = where_at < live_total
        chosen = jnp.minimum(where_at, slot_count - 1)
        picked = weights[chosen]
        samples = jax.vmap(cut_rows)(tile_start[chosen])
        product = jnp.einsum("krs,ksc->krc", picked, samples, preferred_element_type=jnp.float32)
        placing = ((tile_goal[chosen][:, None] == target_ids[None, :]) & live_lane[:, None]).astype(
            jnp.float32
        )
        return totals + jnp.einsum(
            "kt,krc->trc", placing, product, precision=lax.Precision.HIGHEST
        )

    start_totals = jnp.zeros((tiles_out, tile_size, col_count), jnp.float32)
    turn_count = (live_total + TBATCH - 1) // TBATCH
    return lax.fori_loop(0, turn_count, one_turn, start_totals)


def shards(echo_data, tile_weights, tile_target, tile_offset, tile_count, grid_map, psf_kernel):
    row_count = echo_data.shape[2]
    half_frames = echo_data.shape[4]
    tile_size = tile_weights.shape[-1]
    slot_count = tile_weights.shape[2]
    voxels = grid_map.shape[1]
    tiles_out = voxels // tile_size
    flat_echo = echo_data.reshape(row_count, 2 * half_frames)
    weights = tile_weights.reshape(slot_count, tile_size, tile_size)
    tile_sums = tile_pass(
        flat_echo,
        weights,
        tile_target.reshape(-1),
        tile_offset.reshape(-1),
        tile_count[0, 0],
        tiles_out,
    )
    arranged = jnp.take(tile_sums.reshape(voxels, 2, half_frames), grid_map[0], axis=0)
    arranged = arranged.reshape(LAT_DEV, voxels // LAT_DEV, 2, half_frames)
    beamformed = lax.psum_scatter(arranged, "chan", scatter_dimension=1, tiled=True).astype(
        jnp.bfloat16
    )
    lat_count = beamformed.shape[0]
    depth_count = beamformed.shape[1]
    cell_count = lat_count * depth_count
    own_frames = beamformed.reshape(cell_count, 2, half_frames)
    all_frames = lax.all_gather(own_frames, "frm", axis=2, tiled=True)
    frames = all_frames.shape[2]
    own_flat = own_frames.reshape(cell_count, 2 * half_frames)
    all_flat = all_frames.reshape(cell_count, 2 * frames)
    gram_block = lax.dot_general(
        own_flat, all_flat, (((0,), (0,)), ((), ())), preferred_element_type=jnp.float32
    )
    gram_real = gram_block[:half_frames, :frames] + gram_block[half_frames:, frames:]
    gram_imag = gram_block[:half_frames, frames:] - gram_block[half_frames:, :frames]
    frame_start = lax.axis_index("frm") * half_frames
    echo_real = all_frames[:, 0, :].astype(jnp.float32)
    echo_imag = all_frames[:, 1, :].astype(jnp.float32)
    energy = jnp.sum(echo_real * echo_real + echo_imag * echo_imag)
    gram_real, gram_imag, trace_value = lax.psum((gram_real, gram_imag, energy), ("vox", "chan"))
    factor = frames / trace_value
    norm_real = factor * gram_real
    norm_imag = factor * gram_imag
    full_real, full_imag = (
        lax.all_gather(norm_real, "frm", axis=0, tiled=True),
        lax.all_gather(norm_imag, "frm", axis=0, tiled=True),
    )
    identity = jnp.eye(frames, dtype=jnp.float32)
    poly_real = POLY_COEFFS[3] * full_real + POLY_COEFFS[2] * identity
    poly_imag = POLY_COEFFS[3] * full_imag
    poly_real, poly_imag = complex_times(poly_real, poly_imag, full_real, full_imag)
    poly_real = poly_real + POLY_COEFFS[1] * identity
    cols_real = lax.dynamic_slice_in_dim(full_real, frame_start, half_frames, 1)
    cols_imag = lax.dynamic_slice_in_dim(full_imag, frame_start, half_frames, 1)
    filter_real, filter_imag = complex_times(poly_real, poly_imag, cols_real, cols_imag)
    filter_real = filter_real + POLY_COEFFS[0] * lax.dynamic_slice_in_dim(
        identity, frame_start, half_frames, 1
    )
    out_real, out_imag = complex_times(echo_real, echo_imag, filter_real, filter_imag)
    envelope = jnp.sqrt(out_real * out_real + out_imag * out_imag + 1e-06)
    envelope = envelope.reshape(lat_count, depth_count, half_frames)
    padded = with_halo(envelope, (("vox", 0), ("chan", 1)), 2)
    psf_image = jnp.zeros_like(envelope)
    for shift_a in range(5):
        for shift_b in range(5):
            psf_image = (
                psf_image
                + psf_kernel[shift_a, shift_b]
                * padded[shift_a : shift_a + lat_count, shift_b : shift_b + depth_count]
            )
    return psf_image


def split(value):
    high = value.astype(jnp.bfloat16)
    return high, (value - high.astype(jnp.float32)).astype(jnp.bfloat16)


def beam_kernel(
    goal_hbm, start_hbm, live_hbm, weights_hbm, map_hbm, out_ref, operator, goal_ref, start_ref, live_ref, weights_ref, map_ref, few, many
):
    blocks, voxels, tile = operator.shape
    slots = weights_ref.shape[0]
    turns = slots // GROUP
    small = [
        pltpu.make_async_copy(source, target, few.at[index])
        for index, (source, target) in enumerate(
            ((live_hbm, live_ref), (start_hbm, start_ref), (goal_hbm, goal_ref), (map_hbm, map_ref))
        )
    ]

    def fetch(turn):
        span = pl.ds(turn * GROUP, GROUP)
        return pltpu.make_async_copy(weights_hbm.at[span], weights_ref.at[span], many.at[turn])

    for copy in small:
        copy.start()
    for turn in range(turns):
        fetch(turn).start()
    operator[...] = jnp.zeros_like(operator)
    lane = lax.broadcasted_iota(jnp.int32, (tile, tile), 1)
    for copy in small:
        copy.wait()
    live = live_ref[0, 0]
    used = (live + GROUP - 1) // GROUP

    def place(turn, carry):
        fetch(turn).wait()
        ready = []
        for index in range(GROUP):
            kept = turn * GROUP + index
            slot = kept
            first = start_ref[0, kept]
            block = first // tile
            shift = first - block * tile
            rows = pl.ds(pl.multiple_of(goal_ref[0, kept] * tile, tile), tile)
            turned = pltpu.roll(weights_ref[kept].astype(jnp.float32), shift, 1)
            limit = jnp.where(slot < live, shift, tile)
            least = jnp.where(slot < live, 0, tile)
            ready.append((block, rows, jnp.where(lane >= limit, turned, 0.0), turned, shift, least))
        for block, rows, high, turned, shift, least in ready:
            operator[block, rows, :] += high
            operator[block + 1, rows, :] += jnp.where((lane < shift) & (lane >= least), turned, 0.0)
        return carry

    lax.fori_loop(0, used, place, 0)
    picks = lax.broadcasted_iota(jnp.int32, (voxels, voxels), 0) == map_ref[...]
    picks = picks.astype(jnp.float32).T.astype(jnp.bfloat16)
    cells = voxels // 2
    width = cells // LAT_DEV
    for block in range(blocks - 1):
        columns = slice(block * tile, (block + 1) * tile)
        both = jnp.concatenate(split(operator[block]), axis=1)
        moved = jnp.dot(picks, both, preferred_element_type=jnp.float32).astype(jnp.bfloat16)
        for lat in range(LAT_DEV):
            for half in range(2):
                source = (lat * 2 + half) * width
                for level in range(2):
                    target = level * cells + lat * width
                    side = slice(level * tile, (level + 1) * tile)
                    out_ref[half, target : target + width, columns] = moved[source : source + width, side]

    def settle(turn, carry):
        fetch(turn).wait()
        return carry

    lax.fori_loop(used, turns, settle, 0)


def gather_kernel(
    count, operator_ref, echo_ref, psf_ref, rows_ref, gram_ref, near_ref, fine_ref, part, arrived, beams,
    swap_send, swap_recv, own_recv, mate_recv, up_send, down_send, mate_send, side_send, side_recv,
):
    vox, chan, frm = lax.axis_index("vox"), lax.axis_index("chan"), lax.axis_index("frm")
    beside, mate = {"chan": 1 - chan}, {"frm": 1 - frm}
    above, below = {"vox": vox + 1}, {"vox": vox - 1}
    can_up, can_down = vox + 1 < count, vox > 0
    pieces = PIECES
    cells, pair = beams.shape[3], beams.shape[4]
    half = pair // 2
    height = cells // pieces
    depth = cells // LAT_DEV
    barrier = pltpu.get_barrier_semaphore()

    def greet(target):
        pl.semaphore_signal(barrier, inc=1, device_id=target, device_id_type=MESH)

    greet(beside)
    greet(mate)
    for step in range(1, count):
        pl.when(vox + step < count)(functools.partial(greet, {"vox": vox + step}))
        pl.when(vox >= step)(functools.partial(greet, {"vox": vox - step}))

    def sums(side):
        value = jnp.dot(operator_ref[side], echo_ref[...], preferred_element_type=jnp.float32)
        part[side] = value[:cells] + value[cells:]

    def remote(source, target, sent, received, device):
        return pltpu.make_async_remote_copy(
            src_ref=source, dst_ref=target, send_sem=sent, recv_sem=received, device_id=device, device_id_type=MESH
        )

    def rows(unit):
        return pl.ds((unit % pieces) * height, height)

    def side_of(unit):
        return chan if unit < pieces else 1 - chan

    def swap(unit):
        return remote(part.at[1 - chan, rows(unit)], arrived.at[rows(unit)], swap_send.at[0], swap_recv.at[unit], beside)

    def item(block, unit, sent, device):
        place = beams.at[block, frm, side_of(unit), rows(unit)]
        return remote(place, place, sent, own_recv.at[block, unit], device)

    def to_mate(block, unit):
        place = beams.at[block, frm, side_of(unit), rows(unit)]
        return remote(place, place, mate_send.at[block], mate_recv.at[block, side_of(unit)], mate)

    def mated(block, owner, side):
        place = beams.at[block, owner, side]
        return remote(place, place, mate_send.at[block], mate_recv.at[block, side], mate)

    def go_up(step, unit):
        return item(vox, unit, up_send.at[step] if unit < pieces else up_send.at[0], {"vox": vox + step})

    def go_down(step, unit):
        return item(vox, unit, down_send.at[step] if unit < pieces else down_send.at[0], {"vox": vox - step})

    twin_up = can_up & ((vox == 0) | (vox + 2 == count))
    twin_down = can_down & ((vox == count - 1) | (vox == 1))

    def cross(block, unit, side=None):
        place = beams.at[block, frm, chan if side is None else side, rows(unit)]
        return remote(place, place, side_send.at[block], side_recv.at[block, unit], beside)

    def own(unit):
        swap(unit).wait_recv()
        mine = part[chan, rows(unit)] + arrived[rows(unit)]
        beams[vox, frm, chan, rows(unit)] = mine.astype(beams.dtype)
        for step in range(count - 1, 0, -1):
            pl.when(vox + step < count)(lambda: go_up(step, unit).start())
            pl.when(vox >= step)(lambda: go_down(step, unit).start())
        cross(vox, unit).start()
        to_mate(vox, unit).start()

    def own_other(unit):
        cross(vox, unit, 1 - chan).wait_recv()
        pl.when(twin_up)(lambda: go_up(1, pieces + unit).start())
        pl.when(twin_down)(lambda: go_down(1, pieces + unit).start())
        to_mate(vox, pieces + unit).start()

    def relay(step, unit):
        low, high = vox - step, vox + step

        @pl.when(vox >= step)
        def _():
            item(low, unit, up_send.at[0], above).wait_recv()
            if step > 1:
                cross(low, unit).start()
            else:
                pl.when(~twin_down)(lambda: cross(low, unit).start())
            to_mate(low, unit).start()

        @pl.when(vox + step < count)
        def _():
            item(high, unit, down_send.at[0], below).wait_recv()
            if step > 1:
                cross(high, unit).start()
            else:
                pl.when(~twin_up)(lambda: cross(high, unit).start())
            to_mate(high, unit).start()

    def other(step, unit):
        low, high = vox - step, vox + step

        @pl.when(vox >= step)
        def _():
            if step > 1:
                cross(low, unit, 1 - chan).wait_recv()
            else:
                pl.when(twin_down)(item(low, pieces + unit, up_send.at[0], above).wait_recv)
                pl.when(~twin_down)(cross(low, unit, 1 - chan).wait_recv)
            to_mate(low, pieces + unit).start()

        @pl.when(vox + step < count)
        def _():
            if step > 1:
                cross(high, unit, 1 - chan).wait_recv()
            else:
                pl.when(twin_up)(item(high, pieces + unit, down_send.at[0], below).wait_recv)
                pl.when(~twin_up)(cross(high, unit, 1 - chan).wait_recv)
            to_mate(high, pieces + unit).start()

    def from_mate(step, side):
        def settle(block):
            mated(block, 1 - frm, side).wait_recv()

        if step == 0:
            settle(vox)
        else:
            pl.when(vox >= step)(lambda: settle(vox - step))
            pl.when(vox + step < count)(lambda: settle(vox + step))

    def gram(halves, index, first=False):
        left, right = ((0, 0), (0, 1), (1, 1))[index]

        def take(owner):
            return jnp.concatenate([beams[block, owner, side] for block, side in halves], axis=0)

        value = lax.dot_general(
            take(left), take(right), (((0,), (0,)), ((), ())), preferred_element_type=jnp.float32
        )
        if first:
            gram_ref[index] = value
        else:
            gram_ref[index] += value

    def nth(step):
        return jnp.where(2 * vox < count, (vox + step) % count, (vox + count - step) % count)

    tall = LAT_DEV + 4
    slots = near_ref.shape[1] - tall * depth

    def correlation():
        shape = near_ref.shape
        place = lax.broadcasted_iota(jnp.int32, shape, 0)
        source = lax.broadcasted_iota(jnp.int32, shape, 1)
        inside = source < tall * depth
        extra = source - tall * depth
        line = jnp.where(inside, source // depth, extra // 2)
        column = jnp.where(inside, source % depth, extra % 2 + jnp.where(chan == 0, depth, -2))
        down, across = line - place // depth, column - place % depth + 2
        least, most = jnp.where(vox > 0, 0, 2), jnp.where(vox + 1 < count, tall, tall - 2)
        valid = (line >= least) & (line < most) & (across >= 0) & (across < 5)
        key = jnp.where(valid, down * 5 + across, -1)
        value = jnp.zeros(shape, jnp.float32)
        taps = psf_ref[...]
        for shift_a in range(5):
            for shift_b in range(5):
                value = jnp.where(key == shift_a * 5 + shift_b, taps[shift_a : shift_a + 1, shift_b : shift_b + 1], value)
        near_ref[...], fine_ref[...] = split(value)

    def place_rows(start, value):
        total = rows_ref.shape[0] // 2
        size = value.shape[0]
        rows_ref[start : start + size, :] = value[:, :pair]
        rows_ref[total + start : total + start + size, :] = value[:, pair:]

    def collect():
        before, after = jnp.maximum(vox - 1, 0), jnp.minimum(vox + 1, count - 1)
        edge = 2 * depth

        def both(side):
            def lines(block, where):
                parts = [beams[block, owner, side, where] for owner in (0, 1)]
                return jnp.concatenate(
                    [parts[0][:, :half], parts[1][:, :half], parts[0][:, half:], parts[1][:, half:]], axis=1
                )

            return jnp.concatenate(
                [
                    lines(before, slice(cells - edge, cells)),
                    lines(vox, slice(0, cells)),
                    lines(after, slice(0, edge)),
                ],
                axis=0,
            )

        picked = lax.broadcasted_iota(jnp.int32, (slots, tall * depth), 0)
        source = lax.broadcasted_iota(jnp.int32, (slots, tall * depth), 1)
        wanted = (picked // 2) * depth + picked % 2 + jnp.where(chan == 0, 0, depth - 2)
        picks = ((source == wanted) & (picked < 2 * tall)).astype(jnp.float32).astype(jnp.bfloat16)
        extra = jnp.dot(picks, both(1 - chan), preferred_element_type=jnp.float32).astype(jnp.bfloat16)
        place_rows(0, both(chan))
        place_rows(tall * depth, extra)

    def first_stage(index):
        if index == 0:
            from_mate(0, chan)
            from_mate(0, 1 - chan)
        gram([(vox, 0), (vox, 1)], index, True)

    def stage(members):
        for step, far in members:
            from_mate(step, 1 - chan if far else chan)
        if (1, 1) in members:
            collect()
        for index in range(3):
            gram([(nth(step), 1 - chan if far else chan) for step, far in members], index)

    def wave(step, far, unit):
        if step == 0:
            return TWIN[0] + TWIN[1] * unit if far else PACE * unit
        if far and step == 1:
            return SIDE[0] + SIDE[1] * unit
        return PACE * unit + FIRST + HOP * step + (LAG if far else 0)

    def ready(step, far):
        return wave(step, far, pieces - 1)

    events = [(wave(0, 0, pieces - 1), 2, correlation)]
    for unit in range(pieces):
        events += [(wave(0, 0, unit), 0, functools.partial(own, unit))]
        events += [(wave(0, 1, unit), 1, functools.partial(own_other, unit))]
        for step in range(1, count):
            events += [(wave(step, 0, unit), 1, functools.partial(relay, step, unit))]
            events += [(wave(step, 1, unit), 1, functools.partial(other, step, unit))]
    begin = wave(0, 1, pieces - 1) + 1
    events += [(begin, 3, functools.partial(first_stage, index)) for index in range(3)]
    order = [(step, far) for far in (0, 1) for step in range(1, count)]
    latest = begin
    for turn in range(count - 1):
        members = order[2 * turn : 2 * turn + 2]
        latest = max([latest] + [ready(*member) for member in members]) + 1
        events += [(latest, 4, functools.partial(stage, members))]

    sums(1 - chan)
    pl.semaphore_wait(barrier, count + 1)
    for unit in range(pieces):
        swap(unit).start()
    sums(chan)
    for _, _, action in sorted(events, key=lambda event: event[:2]):
        action()

    remote(part.at[1 - chan], arrived, swap_send.at[0], swap_recv.at[0], beside).wait_send()
    twin = beams.at[vox, frm, 1 - chan]
    pl.when(twin_up)(remote(twin, twin, up_send.at[0], own_recv.at[0, 0], above).wait_send)
    pl.when(twin_down)(remote(twin, twin, down_send.at[0], own_recv.at[0, 0], below).wait_send)
    place = beams.at[vox, frm, chan]
    for step in range(1, count):
        up = remote(place, place, up_send.at[step], own_recv.at[0, 0], {"vox": vox + step})
        down = remote(place, place, down_send.at[step], own_recv.at[0, 0], {"vox": vox - step})
        pl.when(vox + step < count)(up.wait_send)
        pl.when(vox >= step)(down.wait_send)
    for block in range(count):
        mated(block, frm, 0).wait_send()
        mated(block, frm, 1).wait_send()
        side = remote(place, place, side_send.at[block], side_recv.at[block, 0], beside)
        by_twin = (twin_down & (vox == block + 1)) | (twin_up & (vox + 1 == block))
        pl.when(~by_twin)(side.wait_send)


def filter_kernel(rows_ref, gram_ref, near_ref, fine_ref, out_ref, real_ref, imag_ref):
    frm = lax.axis_index("frm")
    lat, depth, half = out_ref.shape
    total = rows_ref.shape[0] // 2

    def parts(index):
        block = gram_ref[index]
        return block[:half, :half] + block[half:, half:], block[:half, half:] - block[half:, :half]

    grams = {(0, 0): parts(0), (0, 1): parts(1), (1, 1): parts(2)}
    grams[1, 0] = (grams[0, 1][0].T, -grams[0, 1][1].T)
    eye = lax.broadcasted_iota(jnp.int32, (half, half), 0) == lax.broadcasted_iota(jnp.int32, (half, half), 1)
    diagonal = []
    for (row, column), (real, imag) in grams.items():
        if row == column:
            diagonal.append(jnp.sum(jnp.where(eye, real, 0.0), axis=0, keepdims=True))
            real = jnp.where(eye, 0.0, real)
        place = (slice(row * half, (row + 1) * half), slice(column * half, (column + 1) * half))
        real_ref[place] = real.astype(jnp.bfloat16)
        imag_ref[place] = imag.astype(jnp.bfloat16)
    trace = jnp.sum(diagonal[0] + diagonal[1], axis=1, keepdims=True)
    factor = (2 * half) / trace
    weight = jnp.concatenate(diagonal, axis=1)

    def mine(value):
        return jnp.where(frm == 0, value[:, :half], value[:, half:])

    def times(value, columns):
        value = value.astype(jnp.bfloat16)
        by_real = jnp.dot(value, real_ref[:, columns], preferred_element_type=jnp.float32)
        by_imag = jnp.dot(value, imag_ref[:, columns], preferred_element_type=jnp.float32)
        return jnp.concatenate([by_real[:total] - by_imag[total:], by_imag[:total] + by_real[total:]], axis=0)

    rows = rows_ref[...]
    echo = rows.astype(jnp.float32)
    every = slice(0, 2 * half)
    once = factor * (times(rows, every) + weight * echo)
    twice = factor * (times(once, every) + weight * once)
    mixed = POLY_COEFFS[2] * once + POLY_COEFFS[3] * twice
    own = pl.ds(pl.multiple_of(frm * half, half), half)
    term = factor * (times(mixed, own) + mine(weight) * mine(mixed))
    term += POLY_COEFFS[0] * mine(echo) + POLY_COEFFS[1] * mine(once)
    real, imag = term[:total], term[total:]
    high, low = split(jnp.sqrt(real * real + imag * imag + 1e-06))
    result = jnp.dot(near_ref[...], high, preferred_element_type=jnp.float32)
    result += jnp.dot(near_ref[...], low, preferred_element_type=jnp.float32)
    result += jnp.dot(fine_ref[...], high, preferred_element_type=jnp.float32)
    out_ref[...] = result.reshape(lat, depth, half)


def kernel_shards(count, echo_data, tile_weights, tile_target, tile_offset, tile_count, grid_map, psf_kernel):
    rows, half = echo_data.shape[2], echo_data.shape[4]
    slots, tile = tile_weights.shape[2], tile_weights.shape[4]
    voxels = grid_map.shape[1]
    cells, pair = voxels // 2, 2 * half
    depth = cells // LAT_DEV
    tall = LAT_DEV + 4
    total = tall * depth + -(-2 * tall // 16) * 16
    vmem = pl.BlockSpec(memory_space=pltpu.VMEM)
    operator = pl.pallas_call(
        beam_kernel,
        name="beam",
        out_shape=jax.ShapeDtypeStruct((2, voxels, rows), jnp.bfloat16),
        in_specs=[pl.BlockSpec(memory_space=pltpu.HBM)] * 5,
        out_specs=vmem,
        scratch_shapes=[
            pltpu.VMEM((rows // tile + 1, voxels, tile), jnp.float32),
            pltpu.SMEM((1, slots), jnp.int32),
            pltpu.SMEM((1, slots), jnp.int32),
            pltpu.SMEM((1, 1), jnp.int32),
            pltpu.VMEM((slots, tile, tile), jnp.bfloat16),
            pltpu.VMEM((1, voxels), jnp.int32),
            pltpu.SemaphoreType.DMA((4,)),
            pltpu.SemaphoreType.DMA((slots // GROUP,)),
        ],
        compiler_params=pltpu.CompilerParams(vmem_limit_bytes=8 << 20),
    )(
        *[
            pltpu.with_memory_space_constraint(value, pltpu.HBM) if value.size > 1 else value
            for value in (
                tile_target.reshape(1, slots),
                tile_offset.reshape(1, slots),
                tile_count,
                tile_weights.reshape(slots, tile, tile),
                grid_map,
            )
        ]
    )
    dma = pltpu.SemaphoreType.DMA
    gathered = pl.pallas_call(
        functools.partial(gather_kernel, count),
        name="gather",
        out_shape=[
            jax.ShapeDtypeStruct((2 * total, pair), jnp.bfloat16),
            jax.ShapeDtypeStruct((3, pair, pair), jnp.float32),
            jax.ShapeDtypeStruct((cells, total), jnp.bfloat16),
            jax.ShapeDtypeStruct((cells, total), jnp.bfloat16),
        ],
        in_specs=[vmem] * 3,
        out_specs=[vmem] * 4,
        scratch_shapes=[
            pltpu.VMEM((2, cells, pair), jnp.float32),
            pltpu.VMEM((cells, pair), jnp.float32),
            pltpu.VMEM((count, 2, 2, cells, pair), jnp.bfloat16),
            dma((1,)),
            dma((PIECES,)),
            dma((count, 2 * PIECES)),
            dma((count, 2)),
        ]
        + [dma((count,))] * 4
        + [dma((count, PIECES))],
        compiler_params=pltpu.CompilerParams(collective_id=0, has_side_effects=True, vmem_limit_bytes=16 << 20),
    )(operator, echo_data.reshape(rows, pair), psf_kernel)
    return pl.pallas_call(
        filter_kernel,
        name="filter",
        out_shape=jax.ShapeDtypeStruct((LAT_DEV, depth, half), jnp.float32),
        in_specs=[vmem] * 4,
        out_specs=vmem,
        scratch_shapes=[pltpu.VMEM((pair, pair), jnp.bfloat16)] * 2,
        compiler_params=pltpu.CompilerParams(vmem_limit_bytes=16 << 20),
    )(*gathered)


def solution(mesh):
    in_specs = (
        P(("groups", "vox"), "chan", None, None, "frm"),
        P("vox", "chan", None, None, None),
        P("vox", "chan", None),
        P("vox", "chan", None),
        P("vox", "chan"),
        P("vox", None),
        P(),
    )
    out_specs = P(("groups", "vox"), "chan", "frm")
    body = shards
    if mesh.shape["chan"] == 2 and mesh.shape["frm"] == 2:
        body = functools.partial(kernel_shards, mesh.shape["vox"])
    return jax.shard_map(body, mesh=mesh, in_specs=in_specs, out_specs=out_specs, check_vma=False)
```

```python
import functools

import jax
import jax.numpy as jnp
from jax import lax
from jax.experimental import pallas as pl
from jax.experimental.pallas import tpu as pltpu
from jax.sharding import PartitionSpec as P

MESH = pl.DeviceIdType.MESH
PIECES = 4
HOP = 1
PACE = 2
LAG = 5
TWIN = (7, 1)
SIDE = (13.1, 1)
FIRST = 3
GROUP = 32

TBATCH = 8
LAT_DEV = 8


POLY_COEFFS = (1.0, -0.6, 0.15, -0.03)


def with_halo(shard, sides, width):
    for axis, dim in sides:
        devices, length = (lax.axis_size(axis), shard.shape[dim])
        up = [(i, (i + 1) % devices) for i in range(devices - 1)]
        down = [(j, i) for i, j in up]
        last = lax.slice_in_dim(shard, length - width, length, axis=dim)
        leading = lax.slice_in_dim(shard, 0, width, axis=dim)
        before = lax.ppermute(last, axis, up)
        after = lax.ppermute(leading, axis, down)
        shard = jnp.concatenate([before, shard, after], axis=dim)
    return shard


def complex_times(left_real, left_imag, right_real, right_imag):
    level = lax.Precision.HIGH
    real_part = jnp.dot(
        left_real, right_real, precision=level, preferred_element_type=jnp.float32
    ) - jnp.dot(left_imag, right_imag, precision=level, preferred_element_type=jnp.float32)
    imag_part = jnp.dot(
        left_real, right_imag, precision=level, preferred_element_type=jnp.float32
    ) + jnp.dot(left_imag, right_real, precision=level, preferred_element_type=jnp.float32)
    return (real_part, imag_part)


def tile_pass(flat_echo, weights, tile_goal, tile_start, live_total, tiles_out):
    tile_size = weights.shape[-1]
    col_count = flat_echo.shape[-1]
    slot_count = weights.shape[0]
    lane_ids = jnp.arange(TBATCH, dtype=jnp.int32)
    target_ids = jnp.arange(tiles_out, dtype=jnp.int32)
    zero_index = jnp.zeros((), jnp.int32)

    def cut_rows(offset_id):
        return lax.dynamic_slice(flat_echo, (offset_id, zero_index), (tile_size, col_count))

    def one_turn(turn_index, totals):
        where_at = turn_index * TBATCH + lane_ids
        live_lane = where_at < live_total
        chosen = jnp.minimum(where_at, slot_count - 1)
        picked = weights[chosen]
        samples = jax.vmap(cut_rows)(tile_start[chosen])
        product = jnp.einsum("krs,ksc->krc", picked, samples, preferred_element_type=jnp.float32)
        placing = ((tile_goal[chosen][:, None] == target_ids[None, :]) & live_lane[:, None]).astype(
            jnp.float32
        )
        return totals + jnp.einsum(
            "kt,krc->trc", placing, product, precision=lax.Precision.HIGHEST
        )

    start_totals = jnp.zeros((tiles_out, tile_size, col_count), jnp.float32)
    turn_count = (live_total + TBATCH - 1) // TBATCH
    return lax.fori_loop(0, turn_count, one_turn, start_totals)


def shards(echo_data, tile_weights, tile_target, tile_offset, tile_count, grid_map, psf_kernel):
    row_count = echo_data.shape[2]
    half_frames = echo_data.shape[4]
    tile_size = tile_weights.shape[-1]
    slot_count = tile_weights.shape[2]
    voxels = grid_map.shape[1]
    tiles_out = voxels // tile_size
    flat_echo = echo_data.reshape(row_count, 2 * half_frames)
    weights = tile_weights.reshape(slot_count, tile_size, tile_size)
    tile_sums = tile_pass(
        flat_echo,
        weights,
        tile_target.reshape(-1),
        tile_offset.reshape(-1),
        tile_count[0, 0],
        tiles_out,
    )
    arranged = jnp.take(tile_sums.reshape(voxels, 2, half_frames), grid_map[0], axis=0)
    arranged = arranged.reshape(LAT_DEV, voxels // LAT_DEV, 2, half_frames)
    beamformed = lax.psum_scatter(arranged, "chan", scatter_dimension=1, tiled=True).astype(
        jnp.bfloat16
    )
    lat_count = beamformed.shape[0]
    depth_count = beamformed.shape[1]
    cell_count = lat_count * depth_count
    own_frames = beamformed.reshape(cell_count, 2, half_frames)
    all_frames = lax.all_gather(own_frames, "frm", axis=2, tiled=True)
    frames = all_frames.shape[2]
    own_flat = own_frames.reshape(cell_count, 2 * half_frames)
    all_flat = all_frames.reshape(cell_count, 2 * frames)
    gram_block = lax.dot_general(
        own_flat, all_flat, (((0,), (0,)), ((), ())), preferred_element_type=jnp.float32
    )
    gram_real = gram_block[:half_frames, :frames] + gram_block[half_frames:, frames:]
    gram_imag = gram_block[:half_frames, frames:] - gram_block[half_frames:, :frames]
    frame_start = lax.axis_index("frm") * half_frames
    echo_real = all_frames[:, 0, :].astype(jnp.float32)
    echo_imag = all_frames[:, 1, :].astype(jnp.float32)
    energy = jnp.sum(echo_real * echo_real + echo_imag * echo_imag)
    gram_real, gram_imag, trace_value = lax.psum((gram_real, gram_imag, energy), ("vox", "chan"))
    factor = frames / trace_value
    norm_real = factor * gram_real
    norm_imag = factor * gram_imag
    full_real, full_imag = (
        lax.all_gather(norm_real, "frm", axis=0, tiled=True),
        lax.all_gather(norm_imag, "frm", axis=0, tiled=True),
    )
    identity = jnp.eye(frames, dtype=jnp.float32)
    poly_real = POLY_COEFFS[3] * full_real + POLY_COEFFS[2] * identity
    poly_imag = POLY_COEFFS[3] * full_imag
    poly_real, poly_imag = complex_times(poly_real, poly_imag, full_real, full_imag)
    poly_real = poly_real + POLY_COEFFS[1] * identity
    cols_real = lax.dynamic_slice_in_dim(full_real, frame_start, half_frames, 1)
    cols_imag = lax.dynamic_slice_in_dim(full_imag, frame_start, half_frames, 1)
    filter_real, filter_imag = complex_times(poly_real, poly_imag, cols_real, cols_imag)
    filter_real = filter_real + POLY_COEFFS[0] * lax.dynamic_slice_in_dim(
        identity, frame_start, half_frames, 1
    )
    out_real, out_imag = complex_times(echo_real, echo_imag, filter_real, filter_imag)
    envelope = jnp.sqrt(out_real * out_real + out_imag * out_imag + 1e-06)
    envelope = envelope.reshape(lat_count, depth_count, half_frames)
    padded = with_halo(envelope, (("vox", 0), ("chan", 1)), 2)
    psf_image = jnp.zeros_like(envelope)
    for shift_a in range(5):
        for shift_b in range(5):
            psf_image = (
                psf_image
                + psf_kernel[shift_a, shift_b]
                * padded[shift_a : shift_a + lat_count, shift_b : shift_b + depth_count]
            )
    return psf_image


def split(value):
    high = value.astype(jnp.bfloat16)
    return high, (value - high.astype(jnp.float32)).astype(jnp.bfloat16)


def beam_kernel(
    goal_hbm, start_hbm, live_hbm, weights_hbm, map_hbm, out_ref, operator, goal_ref, start_ref, live_ref, weights_ref, map_ref, few, many
):
    blocks, voxels, tile = operator.shape
    slots = weights_ref.shape[0]
    turns = slots // GROUP
    small = [
        pltpu.make_async_copy(source, target, few.at[index])
        for index, (source, target) in enumerate(
            ((live_hbm, live_ref), (start_hbm, start_ref), (goal_hbm, goal_ref), (map_hbm, map_ref))
        )
    ]

    def fetch(turn):
        span = pl.ds(turn * GROUP, GROUP)
        return pltpu.make_async_copy(weights_hbm.at[span], weights_ref.at[span], many.at[turn])

    for copy in small:
        copy.start()
    for turn in range(turns):
        fetch(turn).start()
    operator[...] = jnp.zeros_like(operator)
    lane = lax.broadcasted_iota(jnp.int32, (tile, tile), 1)
    for copy in small:
        copy.wait()
    live = live_ref[0, 0]
    used = (live + GROUP - 1) // GROUP

    def place(turn, carry):
        fetch(turn).wait()
        ready = []
        for index in range(GROUP):
            kept = turn * GROUP + index
            slot = kept
            first = start_ref[0, kept]
            block = first // tile
            shift = first - block * tile
            rows = pl.ds(pl.multiple_of(goal_ref[0, kept] * tile, tile), tile)
            turned = pltpu.roll(weights_ref[kept].astype(jnp.float32), shift, 1)
            limit = jnp.where(slot < live, shift, tile)
            least = jnp.where(slot < live, 0, tile)
            ready.append((block, rows, jnp.where(lane >= limit, turned, 0.0), turned, shift, least))
        for block, rows, high, turned, shift, least in ready:
            operator[block, rows, :] += high
            operator[block + 1, rows, :] += jnp.where((lane < shift) & (lane >= least), turned, 0.0)
        return carry

    lax.fori_loop(0, used, place, 0)
    picks = lax.broadcasted_iota(jnp.int32, (voxels, voxels), 0) == map_ref[...]
    picks = picks.astype(jnp.float32).T.astype(jnp.bfloat16)
    cells = voxels // 2
    width = cells // LAT_DEV
    for block in range(blocks - 1):
        columns = slice(block * tile, (block + 1) * tile)
        both = jnp.concatenate(split(operator[block]), axis=1)
        moved = jnp.dot(picks, both, preferred_element_type=jnp.float32).astype(jnp.bfloat16)
        for lat in range(LAT_DEV):
            for half in range(2):
                source = (lat * 2 + half) * width
                for level in range(2):
                    target = level * cells + lat * width
                    side = slice(level * tile, (level + 1) * tile)
                    out_ref[half, target : target + width, columns] = moved[source : source + width, side]

    def settle(turn, carry):
        fetch(turn).wait()
        return carry

    lax.fori_loop(used, turns, settle, 0)


def gather_kernel(
    count, operator_ref, echo_ref, psf_ref, rows_ref, gram_ref, near_ref, fine_ref, part, arrived, beams,
    swap_send, swap_recv, own_recv, mate_recv, up_send, down_send, mate_send, side_send, side_recv,
):
    vox, chan, frm = lax.axis_index("vox"), lax.axis_index("chan"), lax.axis_index("frm")
    beside, mate = {"chan": 1 - chan}, {"frm": 1 - frm}
    above, below = {"vox": vox + 1}, {"vox": vox - 1}
    can_up, can_down = vox + 1 < count, vox > 0
    pieces = PIECES
    cells, pair = beams.shape[3], beams.shape[4]
    half = pair // 2
    height = cells // pieces
    depth = cells // LAT_DEV
    barrier = pltpu.get_barrier_semaphore()

    def greet(target):
        pl.semaphore_signal(barrier, inc=1, device_id=target, device_id_type=MESH)

    greet(beside)
    greet(mate)
    for step in range(1, count):
        pl.when(vox + step < count)(functools.partial(greet, {"vox": vox + step}))
        pl.when(vox >= step)(functools.partial(greet, {"vox": vox - step}))

    def sums(side):
        value = jnp.dot(operator_ref[side], echo_ref[...], preferred_element_type=jnp.float32)
        part[side] = value[:cells] + value[cells:]

    def remote(source, target, sent, received, device):
        return pltpu.make_async_remote_copy(
            src_ref=source, dst_ref=target, send_sem=sent, recv_sem=received, device_id=device, device_id_type=MESH
        )

    def rows(unit):
        return pl.ds((unit % pieces) * height, height)

    def side_of(unit):
        return chan if unit < pieces else 1 - chan

    def swap(unit):
        return remote(part.at[1 - chan, rows(unit)], arrived.at[rows(unit)], swap_send.at[0], swap_recv.at[unit], beside)

    def item(block, unit, sent, device):
        place = beams.at[block, frm, side_of(unit), rows(unit)]
        return remote(place, place, sent, own_recv.at[block, unit], device)

    def to_mate(block, unit):
        place = beams.at[block, frm, side_of(unit), rows(unit)]
        return remote(place, place, mate_send.at[block], mate_recv.at[block, side_of(unit)], mate)

    def mated(block, owner, side):
        place = beams.at[block, owner, side]
        return remote(place, place, mate_send.at[block], mate_recv.at[block, side], mate)

    def go_up(step, unit):
        return item(vox, unit, up_send.at[step] if unit < pieces else up_send.at[0], {"vox": vox + step})

    def go_down(step, unit):
        return item(vox, unit, down_send.at[step] if unit < pieces else down_send.at[0], {"vox": vox - step})

    twin_up = can_up & ((vox == 0) | (vox + 2 == count))
    twin_down = can_down & ((vox == count - 1) | (vox == 1))

    def cross(block, unit, side=None):
        place = beams.at[block, frm, chan if side is None else side, rows(unit)]
        return remote(place, place, side_send.at[block], side_recv.at[block, unit], beside)

    def own(unit):
        swap(unit).wait_recv()
        mine = part[chan, rows(unit)] + arrived[rows(unit)]
        beams[vox, frm, chan, rows(unit)] = mine.astype(beams.dtype)
        for step in range(count - 1, 0, -1):
            pl.when(vox + step < count)(lambda: go_up(step, unit).start())
            pl.when(vox >= step)(lambda: go_down(step, unit).start())
        cross(vox, unit).start()
        to_mate(vox, unit).start()

    def own_other(unit):
        cross(vox, unit, 1 - chan).wait_recv()
        pl.when(twin_up)(lambda: go_up(1, pieces + unit).start())
        pl.when(twin_down)(lambda: go_down(1, pieces + unit).start())
        to_mate(vox, pieces + unit).start()

    def relay(step, unit):
        low, high = vox - step, vox + step

        @pl.when(vox >= step)
        def _():
            item(low, unit, up_send.at[0], above).wait_recv()
            if step > 1:
                cross(low, unit).start()
            else:
                pl.when(~twin_down)(lambda: cross(low, unit).start())
            to_mate(low, unit).start()

        @pl.when(vox + step < count)
        def _():
            item(high, unit, down_send.at[0], below).wait_recv()
            if step > 1:
                cross(high, unit).start()
            else:
                pl.when(~twin_up)(lambda: cross(high, unit).start())
            to_mate(high, unit).start()

    def other(step, unit):
        low, high = vox - step, vox + step

        @pl.when(vox >= step)
        def _():
            if step > 1:
                cross(low, unit, 1 - chan).wait_recv()
            else:
                pl.when(twin_down)(item(low, pieces + unit, up_send.at[0], above).wait_recv)
                pl.when(~twin_down)(cross(low, unit, 1 - chan).wait_recv)
            to_mate(low, pieces + unit).start()

        @pl.when(vox + step < count)
        def _():
            if step > 1:
                cross(high, unit, 1 - chan).wait_recv()
            else:
                pl.when(twin_up)(item(high, pieces + unit, down_send.at[0], below).wait_recv)
                pl.when(~twin_up)(cross(high, unit, 1 - chan).wait_recv)
            to_mate(high, pieces + unit).start()

    def from_mate(step, side):
        def settle(block):
            mated(block, 1 - frm, side).wait_recv()

        if step == 0:
            settle(vox)
        else:
            pl.when(vox >= step)(lambda: settle(vox - step))
            pl.when(vox + step < count)(lambda: settle(vox + step))

    def gram(halves, index, first=False):
        left, right = ((0, 0), (0, 1), (1, 1))[index]

        def take(owner):
            return jnp.concatenate([beams[block, owner, side] for block, side in halves], axis=0)

        value = lax.dot_general(
            take(left), take(right), (((0,), (0,)), ((), ())), preferred_element_type=jnp.float32
        )
        if first:
            gram_ref[index] = value
        else:
            gram_ref[index] += value

    def nth(step):
        return jnp.where(2 * vox < count, (vox + step) % count, (vox + count - step) % count)

    tall = LAT_DEV + 4
    slots = near_ref.shape[1] - tall * depth

    def correlation():
        shape = near_ref.shape
        place = lax.broadcasted_iota(jnp.int32, shape, 0)
        source = lax.broadcasted_iota(jnp.int32, shape, 1)
        inside = source < tall * depth
        extra = source - tall * depth
        line = jnp.where(inside, source // depth, extra // 2)
        column = jnp.where(inside, source % depth, extra % 2 + jnp.where(chan == 0, depth, -2))
        down, across = line - place // depth, column - place % depth + 2
        least, most = jnp.where(vox > 0, 0, 2), jnp.where(vox + 1 < count, tall, tall - 2)
        valid = (line >= least) & (line < most) & (across >= 0) & (across < 5)
        key = jnp.where(valid, down * 5 + across, -1)
        value = jnp.zeros(shape, jnp.float32)
        taps = psf_ref[...]
        for shift_a in range(5):
            for shift_b in range(5):
                value = jnp.where(key == shift_a * 5 + shift_b, taps[shift_a : shift_a + 1, shift_b : shift_b + 1], value)
        near_ref[...], fine_ref[...] = split(value)

    def place_rows(start, value):
        total = rows_ref.shape[0] // 2
        size = value.shape[0]
        rows_ref[start : start + size, :] = value[:, :pair]
        rows_ref[total + start : total + start + size, :] = value[:, pair:]

    def collect():
        before, after = jnp.maximum(vox - 1, 0), jnp.minimum(vox + 1, count - 1)
        edge = 2 * depth

        def both(side):
            def lines(block, where):
                parts = [beams[block, owner, side, where] for owner in (0, 1)]
                return jnp.concatenate(
                    [parts[0][:, :half], parts[1][:, :half], parts[0][:, half:], parts[1][:, half:]], axis=1
                )

            return jnp.concatenate(
                [
                    lines(before, slice(cells - edge, cells)),
                    lines(vox, slice(0, cells)),
                    lines(after, slice(0, edge)),
                ],
                axis=0,
            )

        picked = lax.broadcasted_iota(jnp.int32, (slots, tall * depth), 0)
        source = lax.broadcasted_iota(jnp.int32, (slots, tall * depth), 1)
        wanted = (picked // 2) * depth + picked % 2 + jnp.where(chan == 0, 0, depth - 2)
        picks = ((source == wanted) & (picked < 2 * tall)).astype(jnp.float32).astype(jnp.bfloat16)
        extra = jnp.dot(picks, both(1 - chan), preferred_element_type=jnp.float32).astype(jnp.bfloat16)
        place_rows(0, both(chan))
        place_rows(tall * depth, extra)

    def first_stage(index):
        if index == 0:
            from_mate(0, chan)
            from_mate(0, 1 - chan)
        gram([(vox, 0), (vox, 1)], index, True)

    def stage(members):
        for step, far in members:
            from_mate(step, 1 - chan if far else chan)
        if (1, 1) in members:
            collect()
        for index in range(3):
            gram([(nth(step), 1 - chan if far else chan) for step, far in members], index)

    def wave(step, far, unit):
        if step == 0:
            return TWIN[0] + TWIN[1] * unit if far else PACE * unit
        if far and step == 1:
            return SIDE[0] + SIDE[1] * unit
        return PACE * unit + FIRST + HOP * step + (LAG if far else 0)

    def ready(step, far):
        return wave(step, far, pieces - 1)

    events = [(wave(0, 0, pieces - 1), 2, correlation)]
    for unit in range(pieces):
        events += [(wave(0, 0, unit), 0, functools.partial(own, unit))]
        events += [(wave(0, 1, unit), 1, functools.partial(own_other, unit))]
        for step in range(1, count):
            events += [(wave(step, 0, unit), 1, functools.partial(relay, step, unit))]
            events += [(wave(step, 1, unit), 1, functools.partial(other, step, unit))]
    begin = wave(0, 1, pieces - 1) + 1
    events += [(begin, 3, functools.partial(first_stage, index)) for index in range(3)]
    order = [(step, far) for far in (0, 1) for step in range(1, count)]
    latest = begin
    for turn in range(count - 1):
        members = order[2 * turn : 2 * turn + 2]
        latest = max([latest] + [ready(*member) for member in members]) + 1
        events += [(latest, 4, functools.partial(stage, members))]

    sums(1 - chan)
    pl.semaphore_wait(barrier, count + 1)
    for unit in range(pieces):
        swap(unit).start()
    sums(chan)
    for _, _, action in sorted(events, key=lambda event: event[:2]):
        action()

    remote(part.at[1 - chan], arrived, swap_send.at[0], swap_recv.at[0], beside).wait_send()
    twin = beams.at[vox, frm, 1 - chan]
    pl.when(twin_up)(remote(twin, twin, up_send.at[0], own_recv.at[0, 0], above).wait_send)
    pl.when(twin_down)(remote(twin, twin, down_send.at[0], own_recv.at[0, 0], below).wait_send)
    place = beams.at[vox, frm, chan]
    for step in range(1, count):
        up = remote(place, place, up_send.at[step], own_recv.at[0, 0], {"vox": vox + step})
        down = remote(place, place, down_send.at[step], own_recv.at[0, 0], {"vox": vox - step})
        pl.when(vox + step < count)(up.wait_send)
        pl.when(vox >= step)(down.wait_send)
    for block in range(count):
        mated(block, frm, 0).wait_send()
        mated(block, frm, 1).wait_send()
        side = remote(place, place, side_send.at[block], side_recv.at[block, 0], beside)
        by_twin = (twin_down & (vox == block + 1)) | (twin_up & (vox + 1 == block))
        pl.when(~by_twin)(side.wait_send)


def filter_kernel(rows_ref, gram_ref, near_ref, fine_ref, out_ref, real_ref, imag_ref):
    frm = lax.axis_index("frm")
    lat, depth, half = out_ref.shape
    total = rows_ref.shape[0] // 2

    def parts(index):
        block = gram_ref[index]
        return block[:half, :half] + block[half:, half:], block[:half, half:] - block[half:, :half]

    grams = {(0, 0): parts(0), (0, 1): parts(1), (1, 1): parts(2)}
    grams[1, 0] = (grams[0, 1][0].T, -grams[0, 1][1].T)
    eye = lax.broadcasted_iota(jnp.int32, (half, half), 0) == lax.broadcasted_iota(jnp.int32, (half, half), 1)
    diagonal = []
    for (row, column), (real, imag) in grams.items():
        if row == column:
            diagonal.append(jnp.sum(jnp.where(eye, real, 0.0), axis=0, keepdims=True))
            real = jnp.where(eye, 0.0, real)
        place = (slice(row * half, (row + 1) * half), slice(column * half, (column + 1) * half))
        real_ref[place] = real.astype(jnp.bfloat16)
        imag_ref[place] = imag.astype(jnp.bfloat16)
    trace = jnp.sum(diagonal[0] + diagonal[1], axis=1, keepdims=True)
    factor = (2 * half) / trace
    weight = jnp.concatenate(diagonal, axis=1)

    def mine(value):
        return jnp.where(frm == 0, value[:, :half], value[:, half:])

    def times(value, columns):
        value = value.astype(jnp.bfloat16)
        by_real = jnp.dot(value, real_ref[:, columns], preferred_element_type=jnp.float32)
        by_imag = jnp.dot(value, imag_ref[:, columns], preferred_element_type=jnp.float32)
        return jnp.concatenate([by_real[:total] - by_imag[total:], by_imag[:total] + by_real[total:]], axis=0)

    rows = rows_ref[...]
    echo = rows.astype(jnp.float32)
    every = slice(0, 2 * half)
    once = factor * (times(rows, every) + weight * echo)
    twice = factor * (times(once, every) + weight * once)
    mixed = POLY_COEFFS[2] * once + POLY_COEFFS[3] * twice
    own = pl.ds(pl.multiple_of(frm * half, half), half)
    term = factor * (times(mixed, own) + mine(weight) * mine(mixed))
    term += POLY_COEFFS[0] * mine(echo) + POLY_COEFFS[1] * mine(once)
    real, imag = term[:total], term[total:]
    high, low = split(jnp.sqrt(real * real + imag * imag + 1e-06))
    result = jnp.dot(near_ref[...], high, preferred_element_type=jnp.float32)
    result += jnp.dot(near_ref[...], low, preferred_element_type=jnp.float32)
    result += jnp.dot(fine_ref[...], high, preferred_element_type=jnp.float32)
    out_ref[...] = result.reshape(lat, depth, half)


def kernel_shards(count, echo_data, tile_weights, tile_target, tile_offset, tile_count, grid_map, psf_kernel):
    rows, half = echo_data.shape[2], echo_data.shape[4]
    slots, tile = tile_weights.shape[2], tile_weights.shape[4]
    voxels = grid_map.shape[1]
    cells, pair = voxels // 2, 2 * half
    depth = cells // LAT_DEV
    tall = LAT_DEV + 4
    total = tall * depth + -(-2 * tall // 16) * 16
    vmem = pl.BlockSpec(memory_space=pltpu.VMEM)
    operator = pl.pallas_call(
        beam_kernel,
        name="beam",
        out_shape=jax.ShapeDtypeStruct((2, voxels, rows), jnp.bfloat16),
        in_specs=[pl.BlockSpec(memory_space=pltpu.HBM)] * 5,
        out_specs=vmem,
        scratch_shapes=[
            pltpu.VMEM((rows // tile + 1, voxels, tile), jnp.float32),
            pltpu.SMEM((1, slots), jnp.int32),
            pltpu.SMEM((1, slots), jnp.int32),
            pltpu.SMEM((1, 1), jnp.int32),
            pltpu.VMEM((slots, tile, tile), jnp.bfloat16),
            pltpu.VMEM((1, voxels), jnp.int32),
            pltpu.SemaphoreType.DMA((4,)),
            pltpu.SemaphoreType.DMA((slots // GROUP,)),
        ],
        compiler_params=pltpu.CompilerParams(vmem_limit_bytes=8 << 20),
    )(
        *[
            pltpu.with_memory_space_constraint(value, pltpu.HBM) if value.size > 1 else value
            for value in (
                tile_target.reshape(1, slots),
                tile_offset.reshape(1, slots),
                tile_count,
                tile_weights.reshape(slots, tile, tile),
                grid_map,
            )
        ]
    )
    dma = pltpu.SemaphoreType.DMA
    gathered = pl.pallas_call(
        functools.partial(gather_kernel, count),
        name="gather",
        out_shape=[
            jax.ShapeDtypeStruct((2 * total, pair), jnp.bfloat16),
            jax.ShapeDtypeStruct((3, pair, pair), jnp.float32),
            jax.ShapeDtypeStruct((cells, total), jnp.bfloat16),
            jax.ShapeDtypeStruct((cells, total), jnp.bfloat16),
        ],
        in_specs=[vmem] * 3,
        out_specs=[vmem] * 4,
        scratch_shapes=[
            pltpu.VMEM((2, cells, pair), jnp.float32),
            pltpu.VMEM((cells, pair), jnp.float32),
            pltpu.VMEM((count, 2, 2, cells, pair), jnp.bfloat16),
            dma((1,)),
            dma((PIECES,)),
            dma((count, 2 * PIECES)),
            dma((count, 2)),
        ]
        + [dma((count,))] * 4
        + [dma((count, PIECES))],
        compiler_params=pltpu.CompilerParams(collective_id=0, has_side_effects=True, vmem_limit_bytes=16 << 20),
    )(operator, echo_data.reshape(rows, pair), psf_kernel)
    return pl.pallas_call(
        filter_kernel,
        name="filter",
        out_shape=jax.ShapeDtypeStruct((LAT_DEV, depth, half), jnp.float32),
        in_specs=[vmem] * 4,
        out_specs=vmem,
        scratch_shapes=[pltpu.VMEM((pair, pair), jnp.bfloat16)] * 2,
        compiler_params=pltpu.CompilerParams(vmem_limit_bytes=16 << 20),
    )(*gathered)


def solution(mesh):
    in_specs = (
        P(("groups", "vox"), "chan", None, None, "frm"),
        P("vox", "chan", None, None, None),
        P("vox", "chan", None),
        P("vox", "chan", None),
        P("vox", "chan"),
        P("vox", None),
        P(),
    )
    out_specs = P(("groups", "vox"), "chan", "frm")
    body = shards
    if mesh.shape["chan"] == 2 and mesh.shape["frm"] == 2:
        body = functools.partial(kernel_shards, mesh.shape["vox"])
    return jax.shard_map(body, mesh=mesh, in_specs=in_specs, out_specs=out_specs, check_vma=False)
```

```python
import functools

import jax
import jax.numpy as jnp
from jax import lax
from jax.experimental import pallas as pl
from jax.experimental.pallas import tpu as pltpu
from jax.sharding import PartitionSpec as P

MESH = pl.DeviceIdType.MESH
PIECES = 4
HOP = 1
PACE = 2
LAG = 4.5
TWIN = (7, 1)
SIDE = (13.1, 1)
FIRST = 3
GROUP = 32

TBATCH = 8
LAT_DEV = 8


POLY_COEFFS = (1.0, -0.6, 0.15, -0.03)


def with_halo(shard, sides, width):
    for axis, dim in sides:
        devices, length = (lax.axis_size(axis), shard.shape[dim])
        up = [(i, (i + 1) % devices) for i in range(devices - 1)]
        down = [(j, i) for i, j in up]
        last = lax.slice_in_dim(shard, length - width, length, axis=dim)
        leading = lax.slice_in_dim(shard, 0, width, axis=dim)
        before = lax.ppermute(last, axis, up)
        after = lax.ppermute(leading, axis, down)
        shard = jnp.concatenate([before, shard, after], axis=dim)
    return shard


def complex_times(left_real, left_imag, right_real, right_imag):
    level = lax.Precision.HIGH
    real_part = jnp.dot(
        left_real, right_real, precision=level, preferred_element_type=jnp.float32
    ) - jnp.dot(left_imag, right_imag, precision=level, preferred_element_type=jnp.float32)
    imag_part = jnp.dot(
        left_real, right_imag, precision=level, preferred_element_type=jnp.float32
    ) + jnp.dot(left_imag, right_real, precision=level, preferred_element_type=jnp.float32)
    return (real_part, imag_part)


def tile_pass(flat_echo, weights, tile_goal, tile_start, live_total, tiles_out):
    tile_size = weights.shape[-1]
    col_count = flat_echo.shape[-1]
    slot_count = weights.shape[0]
    lane_ids = jnp.arange(TBATCH, dtype=jnp.int32)
    target_ids = jnp.arange(tiles_out, dtype=jnp.int32)
    zero_index = jnp.zeros((), jnp.int32)

    def cut_rows(offset_id):
        return lax.dynamic_slice(flat_echo, (offset_id, zero_index), (tile_size, col_count))

    def one_turn(turn_index, totals):
        where_at = turn_index * TBATCH + lane_ids
        live_lane = where_at < live_total
        chosen = jnp.minimum(where_at, slot_count - 1)
        picked = weights[chosen]
        samples = jax.vmap(cut_rows)(tile_start[chosen])
        product = jnp.einsum("krs,ksc->krc", picked, samples, preferred_element_type=jnp.float32)
        placing = ((tile_goal[chosen][:, None] == target_ids[None, :]) & live_lane[:, None]).astype(
            jnp.float32
        )
        return totals + jnp.einsum(
            "kt,krc->trc", placing, product, precision=lax.Precision.HIGHEST
        )

    start_totals = jnp.zeros((tiles_out, tile_size, col_count), jnp.float32)
    turn_count = (live_total + TBATCH - 1) // TBATCH
    return lax.fori_loop(0, turn_count, one_turn, start_totals)


def shards(echo_data, tile_weights, tile_target, tile_offset, tile_count, grid_map, psf_kernel):
    row_count = echo_data.shape[2]
    half_frames = echo_data.shape[4]
    tile_size = tile_weights.shape[-1]
    slot_count = tile_weights.shape[2]
    voxels = grid_map.shape[1]
    tiles_out = voxels // tile_size
    flat_echo = echo_data.reshape(row_count, 2 * half_frames)
    weights = tile_weights.reshape(slot_count, tile_size, tile_size)
    tile_sums = tile_pass(
        flat_echo,
        weights,
        tile_target.reshape(-1),
        tile_offset.reshape(-1),
        tile_count[0, 0],
        tiles_out,
    )
    arranged = jnp.take(tile_sums.reshape(voxels, 2, half_frames), grid_map[0], axis=0)
    arranged = arranged.reshape(LAT_DEV, voxels // LAT_DEV, 2, half_frames)
    beamformed = lax.psum_scatter(arranged, "chan", scatter_dimension=1, tiled=True).astype(
        jnp.bfloat16
    )
    lat_count = beamformed.shape[0]
    depth_count = beamformed.shape[1]
    cell_count = lat_count * depth_count
    own_frames = beamformed.reshape(cell_count, 2, half_frames)
    all_frames = lax.all_gather(own_frames, "frm", axis=2, tiled=True)
    frames = all_frames.shape[2]
    own_flat = own_frames.reshape(cell_count, 2 * half_frames)
    all_flat = all_frames.reshape(cell_count, 2 * frames)
    gram_block = lax.dot_general(
        own_flat, all_flat, (((0,), (0,)), ((), ())), preferred_element_type=jnp.float32
    )
    gram_real = gram_block[:half_frames, :frames] + gram_block[half_frames:, frames:]
    gram_imag = gram_block[:half_frames, frames:] - gram_block[half_frames:, :frames]
    frame_start = lax.axis_index("frm") * half_frames
    echo_real = all_frames[:, 0, :].astype(jnp.float32)
    echo_imag = all_frames[:, 1, :].astype(jnp.float32)
    energy = jnp.sum(echo_real * echo_real + echo_imag * echo_imag)
    gram_real, gram_imag, trace_value = lax.psum((gram_real, gram_imag, energy), ("vox", "chan"))
    factor = frames / trace_value
    norm_real = factor * gram_real
    norm_imag = factor * gram_imag
    full_real, full_imag = (
        lax.all_gather(norm_real, "frm", axis=0, tiled=True),
        lax.all_gather(norm_imag, "frm", axis=0, tiled=True),
    )
    identity = jnp.eye(frames, dtype=jnp.float32)
    poly_real = POLY_COEFFS[3] * full_real + POLY_COEFFS[2] * identity
    poly_imag = POLY_COEFFS[3] * full_imag
    poly_real, poly_imag = complex_times(poly_real, poly_imag, full_real, full_imag)
    poly_real = poly_real + POLY_COEFFS[1] * identity
    cols_real = lax.dynamic_slice_in_dim(full_real, frame_start, half_frames, 1)
    cols_imag = lax.dynamic_slice_in_dim(full_imag, frame_start, half_frames, 1)
    filter_real, filter_imag = complex_times(poly_real, poly_imag, cols_real, cols_imag)
    filter_real = filter_real + POLY_COEFFS[0] * lax.dynamic_slice_in_dim(
        identity, frame_start, half_frames, 1
    )
    out_real, out_imag = complex_times(echo_real, echo_imag, filter_real, filter_imag)
    envelope = jnp.sqrt(out_real * out_real + out_imag * out_imag + 1e-06)
    envelope = envelope.reshape(lat_count, depth_count, half_frames)
    padded = with_halo(envelope, (("vox", 0), ("chan", 1)), 2)
    psf_image = jnp.zeros_like(envelope)
    for shift_a in range(5):
        for shift_b in range(5):
            psf_image = (
                psf_image
                + psf_kernel[shift_a, shift_b]
                * padded[shift_a : shift_a + lat_count, shift_b : shift_b + depth_count]
            )
    return psf_image


def split(value):
    high = value.astype(jnp.bfloat16)
    return high, (value - high.astype(jnp.float32)).astype(jnp.bfloat16)


def beam_kernel(
    goal_hbm, start_hbm, live_hbm, weights_hbm, map_hbm, out_ref, operator, goal_ref, start_ref, live_ref, weights_ref, map_ref, few, many
):
    blocks, voxels, tile = operator.shape
    slots = weights_ref.shape[0]
    turns = slots // GROUP
    small = [
        pltpu.make_async_copy(source, target, few.at[index])
        for index, (source, target) in enumerate(
            ((live_hbm, live_ref), (start_hbm, start_ref), (goal_hbm, goal_ref), (map_hbm, map_ref))
        )
    ]

    def fetch(turn):
        span = pl.ds(turn * GROUP, GROUP)
        return pltpu.make_async_copy(weights_hbm.at[span], weights_ref.at[span], many.at[turn])

    for copy in small:
        copy.start()
    for turn in range(turns):
        fetch(turn).start()
    operator[...] = jnp.zeros_like(operator)
    lane = lax.broadcasted_iota(jnp.int32, (tile, tile), 1)
    for copy in small:
        copy.wait()
    live = live_ref[0, 0]
    used = (live + GROUP - 1) // GROUP

    def place(turn, carry):
        fetch(turn).wait()
        ready = []
        for index in range(GROUP):
            kept = turn * GROUP + index
            slot = kept
            first = start_ref[0, kept]
            block = first // tile
            shift = first - block * tile
            rows = pl.ds(pl.multiple_of(goal_ref[0, kept] * tile, tile), tile)
            turned = pltpu.roll(weights_ref[kept].astype(jnp.float32), shift, 1)
            limit = jnp.where(slot < live, shift, tile)
            least = jnp.where(slot < live, 0, tile)
            ready.append((block, rows, jnp.where(lane >= limit, turned, 0.0), turned, shift, least))
        for block, rows, high, turned, shift, least in ready:
            operator[block, rows, :] += high
            operator[block + 1, rows, :] += jnp.where((lane < shift) & (lane >= least), turned, 0.0)
        return carry

    lax.fori_loop(0, used, place, 0)
    picks = lax.broadcasted_iota(jnp.int32, (voxels, voxels), 0) == map_ref[...]
    picks = picks.astype(jnp.float32).T.astype(jnp.bfloat16)
    cells = voxels // 2
    width = cells // LAT_DEV
    for block in range(blocks - 1):
        columns = slice(block * tile, (block + 1) * tile)
        both = jnp.concatenate(split(operator[block]), axis=1)
        moved = jnp.dot(picks, both, preferred_element_type=jnp.float32).astype(jnp.bfloat16)
        for lat in range(LAT_DEV):
            for half in range(2):
                source = (lat * 2 + half) * width
                for level in range(2):
                    target = level * cells + lat * width
                    side = slice(level * tile, (level + 1) * tile)
                    out_ref[half, target : target + width, columns] = moved[source : source + width, side]

    def settle(turn, carry):
        fetch(turn).wait()
        return carry

    lax.fori_loop(used, turns, settle, 0)


def gather_kernel(
    count, operator_ref, echo_ref, psf_ref, rows_ref, gram_ref, near_ref, fine_ref, part, arrived, beams,
    swap_send, swap_recv, own_recv, mate_recv, up_send, down_send, mate_send, side_send, side_recv,
):
    vox, chan, frm = lax.axis_index("vox"), lax.axis_index("chan"), lax.axis_index("frm")
    beside, mate = {"chan": 1 - chan}, {"frm": 1 - frm}
    above, below = {"vox": vox + 1}, {"vox": vox - 1}
    can_up, can_down = vox + 1 < count, vox > 0
    pieces = PIECES
    cells, pair = beams.shape[3], beams.shape[4]
    half = pair // 2
    height = cells // pieces
    depth = cells // LAT_DEV
    barrier = pltpu.get_barrier_semaphore()

    def greet(target):
        pl.semaphore_signal(barrier, inc=1, device_id=target, device_id_type=MESH)

    greet(beside)
    greet(mate)
    for step in range(1, count):
        pl.when(vox + step < count)(functools.partial(greet, {"vox": vox + step}))
        pl.when(vox >= step)(functools.partial(greet, {"vox": vox - step}))

    def sums(side):
        value = jnp.dot(operator_ref[side], echo_ref[...], preferred_element_type=jnp.float32)
        part[side] = value[:cells] + value[cells:]

    def remote(source, target, sent, received, device):
        return pltpu.make_async_remote_copy(
            src_ref=source, dst_ref=target, send_sem=sent, recv_sem=received, device_id=device, device_id_type=MESH
        )

    def rows(unit):
        return pl.ds((unit % pieces) * height, height)

    def side_of(unit):
        return chan if unit < pieces else 1 - chan

    def swap(unit):
        return remote(part.at[1 - chan, rows(unit)], arrived.at[rows(unit)], swap_send.at[0], swap_recv.at[unit], beside)

    def item(block, unit, sent, device):
        place = beams.at[block, frm, side_of(unit), rows(unit)]
        return remote(place, place, sent, own_recv.at[block, unit], device)

    def to_mate(block, unit):
        place = beams.at[block, frm, side_of(unit), rows(unit)]
        return remote(place, place, mate_send.at[block], mate_recv.at[block, side_of(unit)], mate)

    def mated(block, owner, side):
        place = beams.at[block, owner, side]
        return remote(place, place, mate_send.at[block], mate_recv.at[block, side], mate)

    def go_up(step, unit):
        return item(vox, unit, up_send.at[step] if unit < pieces else up_send.at[0], {"vox": vox + step})

    def go_down(step, unit):
        return item(vox, unit, down_send.at[step] if unit < pieces else down_send.at[0], {"vox": vox - step})

    twin_up = can_up & ((vox == 0) | (vox + 2 == count))
    twin_down = can_down & ((vox == count - 1) | (vox == 1))

    def cross(block, unit, side=None):
        place = beams.at[block, frm, chan if side is None else side, rows(unit)]
        return remote(place, place, side_send.at[block], side_recv.at[block, unit], beside)

    def own(unit):
        swap(unit).wait_recv()
        mine = part[chan, rows(unit)] + arrived[rows(unit)]
        beams[vox, frm, chan, rows(unit)] = mine.astype(beams.dtype)
        for step in range(count - 1, 0, -1):
            pl.when(vox + step < count)(lambda: go_up(step, unit).start())
            pl.when(vox >= step)(lambda: go_down(step, unit).start())
        cross(vox, unit).start()
        to_mate(vox, unit).start()

    def own_other(unit):
        cross(vox, unit, 1 - chan).wait_recv()
        pl.when(twin_up)(lambda: go_up(1, pieces + unit).start())
        pl.when(twin_down)(lambda: go_down(1, pieces + unit).start())
        to_mate(vox, pieces + unit).start()

    def relay(step, unit):
        low, high = vox - step, vox + step

        @pl.when(vox >= step)
        def _():
            item(low, unit, up_send.at[0], above).wait_recv()
            if step > 1:
                cross(low, unit).start()
            else:
                pl.when(~twin_down)(lambda: cross(low, unit).start())
            to_mate(low, unit).start()

        @pl.when(vox + step < count)
        def _():
            item(high, unit, down_send.at[0], below).wait_recv()
            if step > 1:
                cross(high, unit).start()
            else:
                pl.when(~twin_up)(lambda: cross(high, unit).start())
            to_mate(high, unit).start()

    def other(step, unit):
        low, high = vox - step, vox + step

        @pl.when(vox >= step)
        def _():
            if step > 1:
                cross(low, unit, 1 - chan).wait_recv()
            else:
                pl.when(twin_down)(item(low, pieces + unit, up_send.at[0], above).wait_recv)
                pl.when(~twin_down)(cross(low, unit, 1 - chan).wait_recv)
            to_mate(low, pieces + unit).start()

        @pl.when(vox + step < count)
        def _():
            if step > 1:
                cross(high, unit, 1 - chan).wait_recv()
            else:
                pl.when(twin_up)(item(high, pieces + unit, down_send.at[0], below).wait_recv)
                pl.when(~twin_up)(cross(high, unit, 1 - chan).wait_recv)
            to_mate(high, pieces + unit).start()

    def from_mate(step, side):
        def settle(block):
            mated(block, 1 - frm, side).wait_recv()

        if step == 0:
            settle(vox)
        else:
            pl.when(vox >= step)(lambda: settle(vox - step))
            pl.when(vox + step < count)(lambda: settle(vox + step))

    def gram(halves, index, first=False):
        left, right = ((0, 0), (0, 1), (1, 1))[index]

        def take(owner):
            return jnp.concatenate([beams[block, owner, side] for block, side in halves], axis=0)

        value = lax.dot_general(
            take(left), take(right), (((0,), (0,)), ((), ())), preferred_element_type=jnp.float32
        )
        if first:
            gram_ref[index] = value
        else:
            gram_ref[index] += value

    def nth(step):
        return jnp.where(2 * vox < count, (vox + step) % count, (vox + count - step) % count)

    tall = LAT_DEV + 4
    slots = near_ref.shape[1] - tall * depth

    def correlation():
        shape = near_ref.shape
        place = lax.broadcasted_iota(jnp.int32, shape, 0)
        source = lax.broadcasted_iota(jnp.int32, shape, 1)
        inside = source < tall * depth
        extra = source - tall * depth
        line = jnp.where(inside, source // depth, extra // 2)
        column = jnp.where(inside, source % depth, extra % 2 + jnp.where(chan == 0, depth, -2))
        down, across = line - place // depth, column - place % depth + 2
        least, most = jnp.where(vox > 0, 0, 2), jnp.where(vox + 1 < count, tall, tall - 2)
        valid = (line >= least) & (line < most) & (across >= 0) & (across < 5)
        key = jnp.where(valid, down * 5 + across, -1)
        value = jnp.zeros(shape, jnp.float32)
        taps = psf_ref[...]
        for shift_a in range(5):
            for shift_b in range(5):
                value = jnp.where(key == shift_a * 5 + shift_b, taps[shift_a : shift_a + 1, shift_b : shift_b + 1], value)
        near_ref[...], fine_ref[...] = split(value)

    def place_rows(start, value):
        total = rows_ref.shape[0] // 2
        size = value.shape[0]
        rows_ref[start : start + size, :] = value[:, :pair]
        rows_ref[total + start : total + start + size, :] = value[:, pair:]

    def collect():
        before, after = jnp.maximum(vox - 1, 0), jnp.minimum(vox + 1, count - 1)
        edge = 2 * depth

        def both(side):
            def lines(block, where):
                parts = [beams[block, owner, side, where] for owner in (0, 1)]
                return jnp.concatenate(
                    [parts[0][:, :half], parts[1][:, :half], parts[0][:, half:], parts[1][:, half:]], axis=1
                )

            return jnp.concatenate(
                [
                    lines(before, slice(cells - edge, cells)),
                    lines(vox, slice(0, cells)),
                    lines(after, slice(0, edge)),
                ],
                axis=0,
            )

        picked = lax.broadcasted_iota(jnp.int32, (slots, tall * depth), 0)
        source = lax.broadcasted_iota(jnp.int32, (slots, tall * depth), 1)
        wanted = (picked // 2) * depth + picked % 2 + jnp.where(chan == 0, 0, depth - 2)
        picks = ((source == wanted) & (picked < 2 * tall)).astype(jnp.float32).astype(jnp.bfloat16)
        extra = jnp.dot(picks, both(1 - chan), preferred_element_type=jnp.float32).astype(jnp.bfloat16)
        place_rows(0, both(chan))
        place_rows(tall * depth, extra)

    def first_stage(index):
        if index == 0:
            from_mate(0, chan)
            from_mate(0, 1 - chan)
        gram([(vox, 0), (vox, 1)], index, True)

    def stage(members):
        for step, far in members:
            from_mate(step, 1 - chan if far else chan)
        if (1, 1) in members:
            collect()
        for index in range(3):
            gram([(nth(step), 1 - chan if far else chan) for step, far in members], index)

    def wave(step, far, unit):
        if step == 0:
            return TWIN[0] + TWIN[1] * unit if far else PACE * unit
        if far and step == 1:
            return SIDE[0] + SIDE[1] * unit
        return PACE * unit + FIRST + HOP * step + (LAG if far else 0)

    def ready(step, far):
        return wave(step, far, pieces - 1)

    events = [(-1, 2, correlation)]
    for unit in range(pieces):
        events += [(wave(0, 0, unit), 0, functools.partial(own, unit))]
        events += [(wave(0, 1, unit), 1, functools.partial(own_other, unit))]
        for step in range(1, count):
            events += [(wave(step, 0, unit), 1, functools.partial(relay, step, unit))]
            events += [(wave(step, 1, unit), 1, functools.partial(other, step, unit))]
    begin = wave(0, 1, pieces - 1) + 1
    events += [(begin, 3, functools.partial(first_stage, index)) for index in range(3)]
    order = [(step, far) for far in (0, 1) for step in range(1, count)]
    latest = begin
    for turn in range(count - 1):
        members = order[2 * turn : 2 * turn + 2]
        latest = max([latest] + [ready(*member) for member in members]) + 1
        events += [(latest, 4, functools.partial(stage, members))]

    sums(1 - chan)
    pl.semaphore_wait(barrier, count + 1)
    for unit in range(pieces):
        swap(unit).start()
    sums(chan)
    for _, _, action in sorted(events, key=lambda event: event[:2]):
        action()

    remote(part.at[1 - chan], arrived, swap_send.at[0], swap_recv.at[0], beside).wait_send()
    twin = beams.at[vox, frm, 1 - chan]
    pl.when(twin_up)(remote(twin, twin, up_send.at[0], own_recv.at[0, 0], above).wait_send)
    pl.when(twin_down)(remote(twin, twin, down_send.at[0], own_recv.at[0, 0], below).wait_send)
    place = beams.at[vox, frm, chan]
    for step in range(1, count):
        up = remote(place, place, up_send.at[step], own_recv.at[0, 0], {"vox": vox + step})
        down = remote(place, place, down_send.at[step], own_recv.at[0, 0], {"vox": vox - step})
        pl.when(vox + step < count)(up.wait_send)
        pl.when(vox >= step)(down.wait_send)
    for block in range(count):
        mated(block, frm, 0).wait_send()
        mated(block, frm, 1).wait_send()
        side = remote(place, place, side_send.at[block], side_recv.at[block, 0], beside)
        by_twin = (twin_down & (vox == block + 1)) | (twin_up & (vox + 1 == block))
        pl.when(~by_twin)(side.wait_send)


def filter_kernel(rows_ref, gram_ref, near_ref, fine_ref, out_ref, real_ref, imag_ref):
    frm = lax.axis_index("frm")
    lat, depth, half = out_ref.shape
    total = rows_ref.shape[0] // 2

    def parts(index):
        block = gram_ref[index]
        return block[:half, :half] + block[half:, half:], block[:half, half:] - block[half:, :half]

    grams = {(0, 0): parts(0), (0, 1): parts(1), (1, 1): parts(2)}
    grams[1, 0] = (grams[0, 1][0].T, -grams[0, 1][1].T)
    eye = lax.broadcasted_iota(jnp.int32, (half, half), 0) == lax.broadcasted_iota(jnp.int32, (half, half), 1)
    diagonal = []
    for (row, column), (real, imag) in grams.items():
        if row == column:
            diagonal.append(jnp.sum(jnp.where(eye, real, 0.0), axis=0, keepdims=True))
            real = jnp.where(eye, 0.0, real)
        place = (slice(row * half, (row + 1) * half), slice(column * half, (column + 1) * half))
        real_ref[place] = real.astype(jnp.bfloat16)
        imag_ref[place] = imag.astype(jnp.bfloat16)
    trace = jnp.sum(diagonal[0] + diagonal[1], axis=1, keepdims=True)
    factor = (2 * half) / trace
    weight = jnp.concatenate(diagonal, axis=1)

    def mine(value):
        return jnp.where(frm == 0, value[:, :half], value[:, half:])

    def times(value, columns):
        value = value.astype(jnp.bfloat16)
        by_real = jnp.dot(value, real_ref[:, columns], preferred_element_type=jnp.float32)
        by_imag = jnp.dot(value, imag_ref[:, columns], preferred_element_type=jnp.float32)
        return jnp.concatenate([by_real[:total] - by_imag[total:], by_imag[:total] + by_real[total:]], axis=0)

    rows = rows_ref[...]
    echo = rows.astype(jnp.float32)
    every = slice(0, 2 * half)
    once = factor * (times(rows, every) + weight * echo)
    twice = factor * (times(once, every) + weight * once)
    mixed = POLY_COEFFS[2] * once + POLY_COEFFS[3] * twice
    own = pl.ds(pl.multiple_of(frm * half, half), half)
    term = factor * (times(mixed, own) + mine(weight) * mine(mixed))
    term += POLY_COEFFS[0] * mine(echo) + POLY_COEFFS[1] * mine(once)
    real, imag = term[:total], term[total:]
    high, low = split(jnp.sqrt(real * real + imag * imag + 1e-06))
    result = jnp.dot(near_ref[...], high, preferred_element_type=jnp.float32)
    result += jnp.dot(near_ref[...], low, preferred_element_type=jnp.float32)
    result += jnp.dot(fine_ref[...], high, preferred_element_type=jnp.float32)
    out_ref[...] = result.reshape(lat, depth, half)


def kernel_shards(count, echo_data, tile_weights, tile_target, tile_offset, tile_count, grid_map, psf_kernel):
    rows, half = echo_data.shape[2], echo_data.shape[4]
    slots, tile = tile_weights.shape[2], tile_weights.shape[4]
    voxels = grid_map.shape[1]
    cells, pair = voxels // 2, 2 * half
    depth = cells // LAT_DEV
    tall = LAT_DEV + 4
    total = tall * depth + -(-2 * tall // 16) * 16
    vmem = pl.BlockSpec(memory_space=pltpu.VMEM)
    operator = pl.pallas_call(
        beam_kernel,
        name="beam",
        out_shape=jax.ShapeDtypeStruct((2, voxels, rows), jnp.bfloat16),
        in_specs=[pl.BlockSpec(memory_space=pltpu.HBM)] * 5,
        out_specs=vmem,
        scratch_shapes=[
            pltpu.VMEM((rows // tile + 1, voxels, tile), jnp.float32),
            pltpu.SMEM((1, slots), jnp.int32),
            pltpu.SMEM((1, slots), jnp.int32),
            pltpu.SMEM((1, 1), jnp.int32),
            pltpu.VMEM((slots, tile, tile), jnp.bfloat16),
            pltpu.VMEM((1, voxels), jnp.int32),
            pltpu.SemaphoreType.DMA((4,)),
            pltpu.SemaphoreType.DMA((slots // GROUP,)),
        ],
        compiler_params=pltpu.CompilerParams(vmem_limit_bytes=8 << 20),
    )(
        *[
            pltpu.with_memory_space_constraint(value, pltpu.HBM) if value.size > 1 else value
            for value in (
                tile_target.reshape(1, slots),
                tile_offset.reshape(1, slots),
                tile_count,
                tile_weights.reshape(slots, tile, tile),
                grid_map,
            )
        ]
    )
    dma = pltpu.SemaphoreType.DMA
    gathered = pl.pallas_call(
        functools.partial(gather_kernel, count),
        name="gather",
        out_shape=[
            jax.ShapeDtypeStruct((2 * total, pair), jnp.bfloat16),
            jax.ShapeDtypeStruct((3, pair, pair), jnp.float32),
            jax.ShapeDtypeStruct((cells, total), jnp.bfloat16),
            jax.ShapeDtypeStruct((cells, total), jnp.bfloat16),
        ],
        in_specs=[vmem] * 3,
        out_specs=[vmem] * 4,
        scratch_shapes=[
            pltpu.VMEM((2, cells, pair), jnp.float32),
            pltpu.VMEM((cells, pair), jnp.float32),
            pltpu.VMEM((count, 2, 2, cells, pair), jnp.bfloat16),
            dma((1,)),
            dma((PIECES,)),
            dma((count, 2 * PIECES)),
            dma((count, 2)),
        ]
        + [dma((count,))] * 4
        + [dma((count, PIECES))],
        compiler_params=pltpu.CompilerParams(collective_id=0, has_side_effects=True, vmem_limit_bytes=16 << 20),
    )(operator, echo_data.reshape(rows, pair), psf_kernel)
    return pl.pallas_call(
        filter_kernel,
        name="filter",
        out_shape=jax.ShapeDtypeStruct((LAT_DEV, depth, half), jnp.float32),
        in_specs=[vmem] * 4,
        out_specs=vmem,
        scratch_shapes=[pltpu.VMEM((pair, pair), jnp.bfloat16)] * 2,
        compiler_params=pltpu.CompilerParams(vmem_limit_bytes=16 << 20),
    )(*gathered)


def solution(mesh):
    in_specs = (
        P(("groups", "vox"), "chan", None, None, "frm"),
        P("vox", "chan", None, None, None),
        P("vox", "chan", None),
        P("vox", "chan", None),
        P("vox", "chan"),
        P("vox", None),
        P(),
    )
    out_specs = P(("groups", "vox"), "chan", "frm")
    body = shards
    if mesh.shape["chan"] == 2 and mesh.shape["frm"] == 2:
        body = functools.partial(kernel_shards, mesh.shape["vox"])
    return jax.shard_map(body, mesh=mesh, in_specs=in_specs, out_specs=out_specs, check_vma=False)
```
